32 devices in a mesh: fsdp: 8 (over z, core), dp: 4 (over y, x).
Axes of the slice: x: 2, y: 2, z: 4, core: 2. Of those that a mesh axis runs over, the one named last changes fastest.
Arguments:
- tokens: bfloat16 [32768, 1152], P(('fsdp', 'dp')), may hold values from -6 to 6
- conditions: bfloat16 [128, 1152], P(('fsdp', 'dp')), may hold values from -6 to 6
- resolution: int32 [32], P(('fsdp', 'dp')), may hold values 0 or 1
- modulate_weight: bfloat16 [1152, 6912], P('fsdp', 'dp'), may hold values from -0.1875 to 0.1875
- modulate_bias: bfloat16 [6912], P(('fsdp', 'dp')), may hold values from -3 to 3
- attend_weight: bfloat16 [1152, 3456], P('fsdp', 'dp'), may hold values from -0.1875 to 0.1875
- forget_weight: bfloat16 [1152, 16], P('fsdp', 'dp'), may hold values from -0.1875 to 0.1875
- forget_bias: float32 [16], replicated, may hold values from 0.5 to 4.5
- conv_taps: float32 [9, 1152], replicated, may hold values from -2 to 2
- output_weight: bfloat16 [1152, 1152], P('fsdp', 'dp'), may hold values from -0.1875 to 0.1875
- expand_weight: bfloat16 [1152, 4608], P('fsdp', 'dp'), may hold values from -0.1875 to 0.1875
- expand_bias: bfloat16 [4608], P(('fsdp', 'dp')), may hold values from -3 to 3
- reduce_weight: bfloat16 [4608, 1152], P('fsdp', 'dp'), may hold values from -0.09375 to 0.09375
- cotangent: bfloat16 [32768, 1152], P(('fsdp', 'dp')), may hold values from -6 to 6
Outputs:
- block_out: bfloat16 [32768, 1152], P(('fsdp', 'dp'))
- tokens_grad: bfloat16 [32768, 1152], P(('fsdp', 'dp'))
- conditions_grad: bfloat16 [128, 1152], P(('fsdp', 'dp'))
- modulate_grad: float32 [1152, 6912], P('fsdp', 'dp')
- modbias_grad: float32 [6912], P(('fsdp', 'dp'))
- attend_grad: float32 [1152, 3456], P('fsdp', 'dp')
- forget_grad: float32 [1152, 16], P('fsdp', 'dp')
- forgetbias_grad: float32 [16], replicated
- taps_grad: float32 [9, 1152], replicated
- output_grad: float32 [1152, 1152], P('fsdp', 'dp')
- expand_grad: float32 [1152, 4608], P('fsdp', 'dp')
- expandbias_grad: float32 [4608], P(('fsdp', 'dp'))
- reduce_grad: float32 [4608, 1152], P('fsdp', 'dp')
The draws below stay inside these ranges and needn't reach their ends.
Inputs may be any that keep to these rules, and one draw needn't show every extreme that they name: `resolution`: 1 marks a block holding one item of 32 x 32 patches, 0 a block of four items, each a square grid of half that side.
All inputs are finite; a program needn't handle non-finite values.
Results may differ from the reference program's by a relative error of at most 0.019.
The reference program's roundings to bfloat16 on the way count: a program that leaves them out, or rounds other values in their place, can miss the bound.
Values may be sent and summed in bfloat16 or wider, within the bound.
No kernel may reach another device: no remote copies, remote signals or barrier semaphores. Data moves between devices by JAX's collectives and lax.ppermute only.
A program may use at most 448 MiB of HBM per device.

```python
import jax
import jax.numpy as jnp
from jax import lax

D = 1152
HEADS = 16
FF = 4608
GRID = 32
BLOCK_ROWS = 64
BLOCKS = 32
SLOTS = 128
ROWS = 32768


def touch_ends(drawn, key, smallest, top_value):
    dims = drawn.shape
    place = [jax.random.randint(jax.random.fold_in(key, axis), (), 0, dims[axis]) for axis in range(len(dims))]
    drawn = drawn.at[tuple(place)].set(smallest)
    longest = dims.index(max(dims))
    place[longest] = (place[longest] + 1) % dims[longest]
    return drawn.at[tuple(place)].set(top_value)


def levels(stream_key, dims, cuts, smallest, top_value):
    def one(axis_at, blocks):
        draws = jax.random.uniform(jax.random.fold_in(jax.random.fold_in(stream_key, 6), axis_at), (blocks,), jnp.float32, smallest / len(cuts), top_value / len(cuts))
        return jnp.repeat(jnp.exp(draws), dims[axis_at] // blocks).reshape((-1,) + (1,) * (len(dims) - axis_at - 1))

    loudness = one(*cuts[0])
    for cut in cuts[1:]:
        loudness = loudness * one(*cut)
    return loudness


def bell_draw(own_key, dims, scale, limit, shards=(), held_as=jnp.bfloat16):
    drawn = jax.random.normal(own_key, dims, jnp.float32) * scale
    if len(shards) > 0:
        drawn = levels(own_key, dims, shards, -0.22, 0.18) * drawn
    return jnp.clip(drawn, min=-limit, max=limit).astype(held_as)


def setup_inputs(seed: int = 0) -> dict:
    splits = jax.random.split(jax.random.key(seed), 15)
    tokens = bell_draw(splits[0], (ROWS, D), 1.0, 6.0, ((0, 32),))
    conditions = bell_draw(splits[1], (SLOTS, D), 1.0, 6.0, ((0, 32),))
    resolution = touch_ends((jax.random.randint(splits[2], (BLOCKS,), 0, 3) < 2).astype(jnp.int32), jax.random.fold_in(splits[2], 1), 0, 1)
    modulate_weight = bell_draw(splits[3], (D, 6 * D), D ** -0.5, 0.1875, ((0, 8), (1, 4)))
    modulate_bias = bell_draw(splits[4], (6 * D,), 0.5, 3.0, ((0, 32),))
    attend_weight = bell_draw(splits[5], (D, 3 * D), D ** -0.5, 0.1875, ((0, 8), (1, 4)))
    forget_weight = bell_draw(splits[6], (D, HEADS), D ** -0.5, 0.1875, ((0, 8), (1, 4)))
    forget_bias = jnp.clip(jax.random.uniform(splits[7], (HEADS,), jnp.float32, 0.5, 4.5), 0.5, 4.5)
    conv_taps = bell_draw(splits[8], (9, D), 0.35, 2.0, (), jnp.float32)
    output_weight = bell_draw(splits[9], (D, D), D ** -0.5, 0.1875, ((0, 8), (1, 4)))
    expand_weight = bell_draw(splits[10], (D, FF), D ** -0.5, 0.1875, ((0, 8), (1, 4)))
    expand_bias = bell_draw(splits[11], (FF,), 0.5, 3.0, ((0, 32),))
    reduce_weight = bell_draw(splits[12], (FF, D), FF ** -0.5, 0.09375, ((0, 8), (1, 4)))
    cotangent = bell_draw(splits[13], (ROWS, D), 1.0, 6.0, ((0, 32),))
    return {"tokens": tokens, "conditions": conditions, "resolution": resolution, "modulate_weight": modulate_weight, "modulate_bias": modulate_bias, "attend_weight": attend_weight, "forget_weight": forget_weight, "forget_bias": forget_bias, "conv_taps": conv_taps, "output_weight": output_weight, "expand_weight": expand_weight, "expand_bias": expand_bias, "reduce_weight": reduce_weight, "cotangent": cotangent}


highest = lax.Precision.HIGHEST
normalizer = 16.0
ln_eps = 1e-06
rms_floor = 1.0

@jax.custom_vjp
def low(v):
    return lax.optimization_barrier(v.astype(jnp.bfloat16)).astype(jnp.float32)

@jax.custom_vjp
def low_back(v):
    return v

def low_keep(v):
    return (low(v), None)

def low_pass(kept, grad):
    return (grad,)

def back_keep(v):
    return (v, None)

def back_low(kept, grad):
    return (low(grad),)
low.defvjp(low_keep, low_pass)
low_back.defvjp(back_keep, back_low)

def matmul(former, latter):
    return jnp.dot(former, latter, precision=highest, preferred_element_type=jnp.float32)

def layer_norm(values):
    centred = values - lax.optimization_barrier(jnp.mean(values, axis=-1, keepdims=True))
    return centred * lax.rsqrt(lax.optimization_barrier(jnp.mean(centred * centred, axis=-1, keepdims=True)) + ln_eps)

def slot_pieces(modulation, resolution):
    features = modulation.shape[1] // 6
    grouped = modulation.reshape(resolution.shape[0], 4, 6 * features)
    chosen = jnp.where((resolution == 1)[:, None, None], jnp.broadcast_to(grouped[:, :1], grouped.shape), grouped)
    return [chosen[:, :, None, index_piece * features:(index_piece + 1) * features] for index_piece in range(6)]

def front_piece(token_values, modulation, resolution):
    pieces = slot_pieces(modulation, resolution)
    features = token_values.shape[1]
    grid_tokens = token_values.reshape(resolution.shape[0], 4, -1, features)
    return (layer_norm(grid_tokens) * (1.0 + pieces[1]) + pieces[0]).reshape(-1, features)

def middle_piece(token_values, attended, modulation, resolution):
    pieces = slot_pieces(modulation, resolution)
    features = token_values.shape[1]
    grid_tokens = token_values.reshape(resolution.shape[0], 4, -1, features)
    after_attn = grid_tokens + pieces[2] * attended.reshape(grid_tokens.shape)
    normed_mid = layer_norm(after_attn) * (1.0 + pieces[4]) + pieces[3]
    return (after_attn.reshape(-1, features), normed_mid.reshape(-1, features))

def final_piece(after_attn, reduced, modulation, resolution):
    pieces = slot_pieces(modulation, resolution)
    features = after_attn.shape[1]
    shaped = after_attn.reshape(resolution.shape[0], 4, -1, features)
    return (shaped + pieces[5] * reduced.reshape(shaped.shape)).reshape(-1, features)

def linear_attention(query_rows, key_rows, value_rows, decay_log, starts):
    span_rows = query_rows.shape[1]
    heads_count = query_rows.shape[2]
    head_size = query_rows.shape[3]
    cumul_log = jnp.cumsum(decay_log, axis=1)
    scaling = head_size ** (-0.5)
    scores = jnp.einsum('ntha,nsha->nhts', query_rows, key_rows, precision=highest) * scaling
    causal = jnp.arange(span_rows)[:, None] >= jnp.arange(span_rows)[None, :]
    by_head = jnp.swapaxes(cumul_log, 1, 2)
    spread = by_head[:, :, :, None] - by_head[:, :, None, :]
    weights = jnp.where(causal, jnp.exp(jnp.where(causal, spread, 0.0)), 0.0)
    inside = jnp.einsum('nhts,nshb->nthb', scores * weights, value_rows, precision=highest)
    final_log = cumul_log[:, -1]
    tail_decay = jnp.exp(final_log[:, None, :] - cumul_log)
    contrib = jnp.einsum('ncha,nchb->nhab', key_rows * tail_decay[..., None], value_rows, precision=highest)

    def advance(carried, inputs):
        contrib_one, last_log, start_flag = inputs
        before = carried * (1.0 - start_flag)
        updated = before * jnp.exp(last_log)[:, None, None] + contrib_one
        return (updated, before)
    initial = jnp.zeros((heads_count, head_size, head_size), jnp.float32)
    ignored, befores = lax.scan(advance, initial, (contrib, final_log, starts))
    across = jnp.einsum('ntha,nhab->nthb', query_rows * jnp.exp(cumul_log)[..., None], befores, precision=highest) * scaling
    return inside + across

def depthwise(normed, resolution, taps):
    length = normed.shape[1]
    position = jnp.arange(length, dtype=jnp.int32)[None, :]
    single = (resolution == 1)[:, None]
    row_width = jnp.where(single, GRID, GRID // 2)
    local_pos = jnp.where(single, position, position % (length // 4))
    grid_row = local_pos // row_width
    grid_col = local_pos % row_width
    total = jnp.zeros(normed.shape, jnp.float32)
    for row_step in (-1, 0, 1):
        moved = jnp.where(single[:, :, None], jnp.roll(normed, -row_step * GRID, axis=1), jnp.roll(normed, -row_step * (GRID // 2), axis=1))
        for col_step in (-1, 0, 1):
            shifted = jnp.roll(moved, -col_step, axis=1)
            valid = (grid_row + row_step >= 0) & (grid_row + row_step < row_width) & (grid_col + col_step >= 0) & (grid_col + col_step < row_width)
            total = total + jnp.where(valid[:, :, None], shifted, 0.0) * taps[(row_step + 1) * 3 + col_step + 1]
    return total

def attention_piece(projected_values, gate_logit, forget_bias, conv_taps, resolution):
    row_count = projected_values.shape[0]
    features = projected_values.shape[1] // 3
    heads_count = forget_bias.shape[0]
    head_size = features // heads_count
    blocks = resolution.shape[0]
    per_block = row_count // blocks
    span_count = row_count // BLOCK_ROWS
    block_spans = per_block // BLOCK_ROWS

    def split_heads(block_part):
        return block_part.reshape(span_count, BLOCK_ROWS, heads_count, head_size)
    query_rows = split_heads(projected_values[:, :features])
    key_rows = split_heads(projected_values[:, features:2 * features])
    value_rows = split_heads(projected_values[:, 2 * features:])
    decay_log = (jax.nn.log_sigmoid(gate_logit + forget_bias) / normalizer).reshape(span_count, BLOCK_ROWS, heads_count)
    span_index = jnp.arange(span_count, dtype=jnp.int32)
    within = span_index % block_spans
    single = jnp.repeat(resolution == 1, block_spans)
    starts = jnp.where(single, within == 0, within % (block_spans // 4) == 0).astype(jnp.float32)
    mixed_heads = linear_attention(query_rows, key_rows, value_rows, decay_log, starts).reshape(row_count, heads_count, head_size)
    normed = mixed_heads * lax.rsqrt(jnp.maximum(lax.optimization_barrier(jnp.mean(mixed_heads * mixed_heads, axis=-1, keepdims=True)), rms_floor))
    return depthwise(normed.reshape(blocks, per_block, features), resolution, conv_taps).reshape(row_count, features)

def block_forward(params, inputs):
    modulate_full, modbias_full, attend_full, forget_full, forgetbias_full, taps_full, output_full, expand_full, expandbias_full, reduce_full = params
    token_block, cond_block, wide_flag = inputs
    resolution_one = wide_flag.reshape(1)
    cond_low = low(jax.nn.silu(cond_block))
    modulation = low_back(matmul(cond_low, modulate_full) + modbias_full)
    normed_in = low(front_piece(token_block, modulation, resolution_one))
    projected = low(low_back(matmul(normed_in, attend_full)))
    gate_logit = low_back(matmul(normed_in, forget_full))
    conv_out = attention_piece(projected, gate_logit, forgetbias_full, taps_full, resolution_one)
    attended = low_back(matmul(low(conv_out), output_full))
    after_attn, normed_raw = middle_piece(token_block, attended, modulation, resolution_one)
    normed_mid = low(normed_raw)
    hidden = low(jax.nn.gelu(low_back(matmul(normed_mid, expand_full) + expandbias_full), approximate=True))
    reduced = low_back(matmul(hidden, reduce_full))
    return final_piece(after_attn, reduced, modulation, resolution_one)

def reference(tokens, conditions, resolution, modulate_weight, modulate_bias, attend_weight, forget_weight, forget_bias, conv_taps, output_weight, expand_weight, expand_bias, reduce_weight, cotangent):
    blocks = resolution.shape[0]
    features = tokens.shape[1]

    def forward(token_values, cond_values, modulate_full, modbias_full, attend_full, forget_full, forgetbias_full, taps_full, output_full, expand_full, expandbias_full, reduce_full):
        params = (modulate_full, modbias_full, attend_full, forget_full, forgetbias_full, taps_full, output_full, expand_full, expandbias_full, reduce_full)

        def one_block(inputs):
            return block_forward(params, inputs)
        mapped = lax.map(jax.checkpoint(one_block), (token_values.reshape(blocks, -1, features), cond_values.reshape(blocks, 4, features), resolution))
        return mapped.reshape(-1, features)
    floats = (tokens.astype(jnp.float32), conditions.astype(jnp.float32), modulate_weight.astype(jnp.float32), modulate_bias.astype(jnp.float32), attend_weight.astype(jnp.float32), forget_weight.astype(jnp.float32), forget_bias.astype(jnp.float32), conv_taps.astype(jnp.float32), output_weight.astype(jnp.float32), expand_weight.astype(jnp.float32), expand_bias.astype(jnp.float32), reduce_weight.astype(jnp.float32))
    result, pullback = jax.vjp(forward, *floats)
    grads = pullback(cotangent.astype(jnp.float32))
    return (result.astype(jnp.bfloat16), grads[0].astype(jnp.bfloat16), grads[1].astype(jnp.bfloat16), grads[2], grads[3], grads[4], grads[5], grads[6], grads[7], grads[8], grads[9], grads[10], grads[11])
```

```python
import functools
import math

import jax
import jax.numpy as jnp
from jax import lax
from jax.experimental import pallas as pl
from jax.experimental.pallas import tpu as pltpu
from jax.sharding import PartitionSpec as P

GRID = 32
CHUNK = 256
LANES = 128
VMEM_BYTES = 60 * 1024 * 1024
QUARTERS = 4
COST = 0.02
Z_AT, CORE_AT, U_AT, V_AT, FLAG_AT = range(5)
normalizer = 16.0
ln_eps = 1e-06
gelu_scale = math.sqrt(2.0 / math.pi)
rms_floor = 1.0
masked_log = -1e30
highest = lax.Precision.HIGHEST


def dot_nn(former, latter, precision=None):
    return lax.dot_general(
        former, latter, (((1,), (0,)), ((), ())), precision=precision, preferred_element_type=jnp.float32
    )


def dot_nt(former, latter):
    return lax.dot_general(former, latter, (((1,), (1,)), ((), ())), preferred_element_type=jnp.float32)


def dot_tn(former, latter):
    return lax.dot_general(former, latter, (((0,), (0,)), ((), ())), preferred_element_type=jnp.float32)


def head_window(head, head_size):
    first = head * head_size
    start = first // LANES * LANES
    stop = -(-(first + head_size) // LANES) * LANES
    return start, stop - start, first - start


def lane_mask(width, offset, head_size):
    lanes = lax.broadcasted_iota(jnp.int32, (1, width), 1)
    return (lanes >= offset) & (lanes < offset + head_size)


def cell_masks(rows, side):
    position = lax.broadcasted_iota(jnp.int32, (rows, 1), 0)
    grid_col = position & (side - 1)
    grid_row = (position & (side * side - 1)) >> int(math.log2(side))
    return grid_row, grid_col


def conv_forward_tile(values, taps, side):
    rows = values.shape[0]
    grid_row, grid_col = cell_masks(rows, side)
    before = jnp.where(grid_col > 0, pltpu.roll(values, 1, 0), 0.0)
    after = jnp.where(grid_col < side - 1, pltpu.roll(values, rows - 1, 0), 0.0)
    sums = [
        before * taps[3 * step : 3 * step + 1]
        + values * taps[3 * step + 1 : 3 * step + 2]
        + after * taps[3 * step + 2 : 3 * step + 3]
        for step in range(3)
    ]
    upper = jnp.where(grid_row > 0, pltpu.roll(sums[0], side, 0), 0.0)
    lower = jnp.where(grid_row < side - 1, pltpu.roll(sums[2], rows - side, 0), 0.0)
    return sums[1] + upper + lower


def conv_backward_tile(values, grads, taps, side):
    rows = values.shape[0]
    grid_row, grid_col = cell_masks(rows, side)
    before = jnp.where(grid_col > 0, pltpu.roll(values, 1, 0), 0.0)
    after = jnp.where(grid_col < side - 1, pltpu.roll(values, rows - 1, 0), 0.0)
    grad_sums = [
        jnp.where(grid_row < side - 1, pltpu.roll(grads, rows - side, 0), 0.0),
        grads,
        jnp.where(grid_row > 0, pltpu.roll(grads, side, 0), 0.0),
    ]
    tap_rows = []
    for step in range(3):
        for shifted in (before, values, after):
            tap_rows.append(jnp.sum(grad_sums[step] * shifted, axis=0, keepdims=True))
    parts = [
        sum(grad_sums[step] * taps[3 * step + col : 3 * step + col + 1] for step in range(3))
        for col in range(3)
    ]
    result = (
        parts[1]
        + pltpu.roll(jnp.where(grid_col > 0, parts[0], 0.0), rows - 1, 0)
        + pltpu.roll(jnp.where(grid_col < side - 1, parts[2], 0.0), 1, 0)
    )
    return result, tap_rows


def decay_sums(gate, bias, chunk):
    logit = gate + bias
    decay = (jnp.minimum(logit, 0.0) - jnp.log1p(jnp.exp(-jnp.abs(logit)))) / normalizer
    row_at = lax.broadcasted_iota(jnp.int32, (chunk, chunk), 0)
    col_at = lax.broadcasted_iota(jnp.int32, (chunk, chunk), 1)
    lower = jnp.where(row_at >= col_at, 1.0, 0.0)
    return dot_nn(lower, decay, highest)


def attention_forward_kernel(
    heads, head_size, flag_ref, proj_ref, gate_ref, bias_ref, taps_ref, conv_ref, normed_ref, ratio_ref, states_ref, state
):
    chunk_at = pl.program_id(0)
    chunk = proj_ref.shape[0]
    features = heads * head_size
    single = flag_ref[0] == 1

    @pl.when(jnp.logical_or(chunk_at == 0, jnp.logical_not(single)))
    def _():
        state[...] = jnp.zeros_like(state)

    cumul = decay_sums(gate_ref[...], bias_ref[...], chunk)
    cumul_t = jnp.transpose(cumul)
    scaled = cumul + math.log(head_size ** (-0.5))
    from_start = jnp.exp(scaled)
    last = cumul[chunk - 1 : chunk, :]
    to_end = jnp.exp(last - cumul)
    whole = jnp.exp(last)
    row_at = lax.broadcasted_iota(jnp.int32, (chunk, chunk), 0)
    col_at = lax.broadcasted_iota(jnp.int32, (chunk, chunk), 1)
    causal = row_at >= col_at
    lane_at = lax.broadcasted_iota(jnp.int32, (1, LANES), 1)
    rows = pl.ds(pl.multiple_of(chunk_at * chunk, chunk), chunk)
    ratios = jnp.zeros((chunk, LANES), jnp.float32)
    for head in range(heads):
        start, width, offset = head_window(head, head_size)
        inside = lane_mask(width, offset, head_size)
        query = jnp.where(inside, proj_ref[:, start : start + width], 0)
        key = proj_ref[:, features + start : features + start + width]
        value = proj_ref[:, 2 * features + start : 2 * features + start + width]
        spread = scaled[:, head : head + 1] - cumul_t[head : head + 1, :]
        weights = jnp.exp(jnp.where(causal, spread, masked_log))
        scores = (dot_nt(query, key) * weights).astype(jnp.bfloat16)
        held = state[head, :width, :width]
        held_low = held.astype(jnp.bfloat16)
        states_ref[0, head, :width, :width] = held_low
        mixed = dot_nn(scores, value) + from_start[:, head : head + 1] * dot_nn(query, held_low)
        mixed = jnp.where(inside, mixed, 0.0)
        mean_square = jnp.sum(mixed * mixed, axis=1, keepdims=True) / head_size
        ratio = lax.rsqrt(jnp.maximum(mean_square, rms_floor))
        slope = jnp.where(mean_square > rms_floor, 1.0, jnp.where(mean_square == rms_floor, 0.5, 0.0))
        ratios = jnp.where(lane_at == head, ratio, ratios)
        ratios = jnp.where(lane_at == heads + head, slope, ratios)
        window = normed_ref[rows, start : start + width]
        normed_ref[rows, start : start + width] = jnp.where(inside, mixed * ratio, window)
        key_end = (jnp.where(inside, key, 0) * to_end[:, head : head + 1]).astype(jnp.bfloat16)
        state[head, :width, :width] = held * whole[:, head : head + 1] + dot_tn(key_end, value)
    ratio_ref[...] = ratios

    def convolve(side):
        def tile(at, carry):
            lanes = pl.ds(pl.multiple_of(at * LANES, LANES), LANES)
            conv_ref[:, lanes] = conv_forward_tile(normed_ref[:, lanes], taps_ref[:, lanes], side).astype(conv_ref.dtype)
            return carry

        lax.fori_loop(0, features // LANES, tile, 0)

    finished = chunk_at == pl.num_programs(0) - 1

    @pl.when(jnp.logical_and(finished, single))
    def _():
        convolve(GRID)

    @pl.when(jnp.logical_and(finished, jnp.logical_not(single)))
    def _():
        convolve(GRID // 2)


def attention_forward(flag, proj, gate, bias, taps, heads):
    rows = proj.shape[0]
    features = taps.shape[1]
    head_size = features // heads
    chunks = rows // CHUNK
    whole_rows = lambda at: (0, 0)
    return pl.pallas_call(
        functools.partial(attention_forward_kernel, heads, head_size),
        grid=(chunks,),
        in_specs=[
            pl.BlockSpec(memory_space=pltpu.SMEM),
            pl.BlockSpec((CHUNK, 3 * features), lambda at: (at, 0)),
            pl.BlockSpec((CHUNK, LANES), lambda at: (at, 0)),
            pl.BlockSpec((1, LANES), whole_rows),
            pl.BlockSpec((9, features), whole_rows),
        ],
        out_specs=[
            pl.BlockSpec((rows, features), whole_rows),
            pl.BlockSpec((rows, features), whole_rows),
            pl.BlockSpec((CHUNK, LANES), lambda at: (at, 0)),
            pl.BlockSpec((1, heads, 2 * LANES, 2 * LANES), lambda at: (at, 0, 0, 0)),
        ],
        out_shape=[
            jax.ShapeDtypeStruct((rows, features), jnp.bfloat16),
            jax.ShapeDtypeStruct((rows, features), jnp.float32),
            jax.ShapeDtypeStruct((rows, LANES), jnp.float32),
            jax.ShapeDtypeStruct((chunks, heads, 2 * LANES, 2 * LANES), jnp.bfloat16),
        ],
        scratch_shapes=[pltpu.VMEM((heads, 2 * LANES, 2 * LANES), jnp.float32)],
        compiler_params=pltpu.CompilerParams(vmem_limit_bytes=VMEM_BYTES),
        cost_estimate=pl.CostEstimate(flops=int(17 * 10**9 * COST), bytes_accessed=int(20 * 10**6 * COST), transcendentals=0),
        name="attention_forward",
    )(flag, proj, gate, bias, taps)


def attention_backward_kernel(
    heads,
    head_size,
    flag_ref,
    proj_ref,
    gate_ref,
    bias_ref,
    taps_ref,
    normed_ref,
    ratio_ref,
    states_ref,
    grads_ref,
    dproj_ref,
    dgate_ref,
    dbias_ref,
    dtaps_ref,
    dnormed,
    dstate,
):
    step = pl.program_id(0)
    chunks = pl.num_programs(0)
    chunk_at = chunks - 1 - step
    chunk = proj_ref.shape[0]
    features = heads * head_size
    single = flag_ref[0] == 1

    def convolve(side):
        def tile(at, carry):
            lanes = pl.ds(pl.multiple_of(at * LANES, LANES), LANES)
            result, tap_rows = conv_backward_tile(
                normed_ref[:, lanes], grads_ref[:, lanes], taps_ref[:, lanes], side
            )
            dnormed[:, lanes] = result
            for row, tap_row in enumerate(tap_rows):
                dtaps_ref[row : row + 1, lanes] = tap_row
            return carry

        lax.fori_loop(0, features // LANES, tile, 0)

    @pl.when(jnp.logical_and(step == 0, single))
    def _():
        convolve(GRID)

    @pl.when(jnp.logical_and(step == 0, jnp.logical_not(single)))
    def _():
        convolve(GRID // 2)

    @pl.when(step == 0)
    def _():
        dbias_ref[...] = jnp.zeros_like(dbias_ref)

    @pl.when(jnp.logical_or(step == 0, jnp.logical_not(single)))
    def _():
        dstate[...] = jnp.zeros_like(dstate)

    gate = gate_ref[...]
    bias = bias_ref[...]
    cumul = decay_sums(gate, bias, chunk)
    cumul_t = jnp.transpose(cumul)
    scaled = cumul + math.log(head_size ** (-0.5))
    from_start = jnp.exp(scaled)
    last = cumul[chunk - 1 : chunk, :]
    to_end = jnp.exp(last - cumul)
    whole = jnp.exp(last)
    row_at = lax.broadcasted_iota(jnp.int32, (chunk, chunk), 0)
    col_at = lax.broadcasted_iota(jnp.int32, (chunk, chunk), 1)
    causal = row_at >= col_at
    lane_at = lax.broadcasted_iota(jnp.int32, (1, LANES), 1)
    rows = pl.ds(pl.multiple_of(chunk_at * chunk, chunk), chunk)
    balance = jnp.zeros((chunk, LANES), jnp.float32)
    outgoing = jnp.zeros((chunk, LANES), jnp.float32)
    through = jnp.zeros((1, LANES), jnp.float32)
    for head in range(heads):
        start, width, offset = head_window(head, head_size)
        inside = lane_mask(width, offset, head_size)
        query = jnp.where(inside, proj_ref[:, start : start + width], 0)
        key = proj_ref[:, features + start : features + start + width]
        key_in = jnp.where(inside, key, 0)
        value = proj_ref[:, 2 * features + start : 2 * features + start + width]
        value_in = jnp.where(inside, value, 0)
        start_col = from_start[:, head : head + 1]
        end_col = to_end[:, head : head + 1]
        ratio = ratio_ref[:, head : head + 1]
        slope = ratio_ref[:, heads + head : heads + head + 1]
        normed = jnp.where(inside, normed_ref[rows, start : start + width], 0.0)
        dnorm = jnp.where(inside, dnormed[rows, start : start + width], 0.0)
        along = jnp.sum(dnorm * normed, axis=1, keepdims=True) * (slope / head_size)
        dmixed = (dnorm - normed * along) * ratio
        dmixed_start = (dmixed * start_col).astype(jnp.bfloat16)
        dmixed = dmixed.astype(jnp.bfloat16)
        spread = scaled[:, head : head + 1] - cumul_t[head : head + 1, :]
        weights = jnp.exp(jnp.where(causal, spread, masked_log))
        scores = (dot_nt(query, key) * weights).astype(jnp.bfloat16)
        dscores = (dot_nt(dmixed, value) * weights).astype(jnp.bfloat16)
        held = states_ref[0, head, :width, :width]
        dnext = dstate[head, :width, :width]
        dnext_low = dnext.astype(jnp.bfloat16)
        dquery = dot_nn(dscores, key) + dot_nt(dmixed_start, held)
        dkey_inside = dot_tn(dscores, query)
        dkey_after = end_col * dot_nt(value_in, dnext_low)
        dkey = dkey_inside + dkey_after
        dvalue = dot_tn(scores, dmixed) + end_col * dot_nn(key_in, dnext_low)
        dstate[head, :width, :width] = dnext * whole[:, head : head + 1] + dot_tn(query, dmixed_start)
        term = jnp.sum(jnp.sum(dnext * held, axis=1, keepdims=True), axis=0, keepdims=True)
        through = jnp.where(lane_at == head, term, through)
        balance_one = jnp.sum(query * dquery - key_in * dkey_inside, axis=1, keepdims=True)
        balance = jnp.where(lane_at == head, balance_one, balance)
        outgoing_one = jnp.sum(key_in * dkey_after, axis=1, keepdims=True)
        outgoing = jnp.where(lane_at == head, outgoing_one, outgoing)
        for place, grad in ((0, dquery), (1, dkey), (2, dvalue)):
            columns = slice(place * features + start, place * features + start + width)
            dproj_ref[:, columns] = jnp.where(inside, grad.astype(dproj_ref.dtype), dproj_ref[:, columns])
    upper = jnp.where(row_at <= col_at, 1.0, 0.0)
    strict = jnp.where(row_at > col_at, 1.0, 0.0)
    ddecay = dot_nn(upper, balance, highest) + dot_nn(strict, outgoing, highest) + through * whole
    dgate = ddecay / (1.0 + jnp.exp(gate + bias)) / normalizer
    dgate_ref[...] = dgate
    dbias_ref[...] += jnp.sum(dgate, axis=0, keepdims=True)


def attention_backward(flag, proj, gate, bias, taps, normed, ratios, states, grads, heads):
    rows = proj.shape[0]
    features = taps.shape[1]
    head_size = features // heads
    chunks = rows // CHUNK
    whole_rows = lambda at: (0, 0)
    back = lambda at: (chunks - 1 - at, 0)
    return pl.pallas_call(
        functools.partial(attention_backward_kernel, heads, head_size),
        grid=(chunks,),
        in_specs=[
            pl.BlockSpec(memory_space=pltpu.SMEM),
            pl.BlockSpec((CHUNK, 3 * features), back),
            pl.BlockSpec((CHUNK, LANES), back),
            pl.BlockSpec((1, LANES), whole_rows),
            pl.BlockSpec((9, features), whole_rows),
            pl.BlockSpec((rows, features), whole_rows),
            pl.BlockSpec((CHUNK, LANES), back),
            pl.BlockSpec((1, heads, 2 * LANES, 2 * LANES), lambda at: (chunks - 1 - at, 0, 0, 0)),
            pl.BlockSpec((rows, features), whole_rows),
        ],
        out_specs=[
            pl.BlockSpec((CHUNK, 3 * features), back),
            pl.BlockSpec((CHUNK, LANES), back),
            pl.BlockSpec((1, LANES), whole_rows),
            pl.BlockSpec((9, features), whole_rows),
        ],
        out_shape=[
            jax.ShapeDtypeStruct((rows, 3 * features), jnp.bfloat16),
            jax.ShapeDtypeStruct((rows, LANES), jnp.float32),
            jax.ShapeDtypeStruct((1, LANES), jnp.float32),
            jax.ShapeDtypeStruct((9, features), jnp.float32),
        ],
        scratch_shapes=[
            pltpu.VMEM((rows, features), jnp.float32),
            pltpu.VMEM((heads, 2 * LANES, 2 * LANES), jnp.float32),
        ],
        compiler_params=pltpu.CompilerParams(vmem_limit_bytes=VMEM_BYTES),
        cost_estimate=pl.CostEstimate(flops=int(38 * 10**9 * COST), bytes_accessed=int(40 * 10**6 * COST), transcendentals=0),
        name="attention_backward",
    )(flag, proj, gate, bias, taps, normed, ratios, states, grads)


def parts_of(fsdp_size, dp_size):
    return fsdp_size // 2, math.isqrt(dp_size)


def mesh_parts():
    return parts_of(lax.axis_size("fsdp"), lax.axis_size("dp"))


def send(values, move):
    chips, side = mesh_parts()
    pairs = []
    for z in range(chips):
        for core in range(2):
            for u in range(side):
                for v in range(side):
                    to_z, to_core, to_u, to_v = move(z, core, u, v)
                    pairs.append(
                        (
                            ((z * 2 + core) * side + u) * side + v,
                            ((to_z * 2 + to_core) * side + to_u) * side + to_v,
                        )
                    )
    return lax.ppermute(values, ("fsdp", "dp"), pairs)


def along_z(shift):
    chips = mesh_parts()[0]
    return lambda z, core, u, v: ((z + shift) % chips, core, u, v)


def across_core(z, core, u, v):
    return z, 1 - core, u, v


def along_first(shift):
    side = mesh_parts()[1]

    def move(z, core, u, v):
        return (z, core, (u + shift) % side, v) if core == 0 else (z, core, u, (v + shift) % side)

    return move


def along_second(shift):
    side = mesh_parts()[1]

    def move(z, core, u, v):
        return (z, core, u, (v + shift) % side) if core == 0 else (z, core, (u + shift) % side, v)

    return move


def along_dp(shift):
    side = mesh_parts()[1]

    def move(z, core, u, v):
        to = (u * side + v + shift) % (side * side)
        return z, core, to // side, to % side

    return move


def far_pieces(shard):
    chips = mesh_parts()[0]
    return [shard] + [send(shard, along_z(shift)) for shift in range(1, chips)]


def first_pieces(stack):
    side = mesh_parts()[1]
    return [stack] + [send(stack, along_first(shift)) for shift in range(1, side)]


def second_pieces(level):
    side = mesh_parts()[1]
    own = []
    for piece in level:
        own += [piece] + [send(piece, along_second(shift)) for shift in range(1, side)]
    return own


def core_pieces(own):
    return own + [send(piece, across_core) for piece in own]


def gather_shard(shard):
    return core_pieces(second_pieces(first_pieces(jnp.stack(far_pieces(shard)))))


def add_low(*values):
    total = values[0].astype(jnp.float32)
    for value in values[1:]:
        total = total + value.astype(jnp.float32)
    return total


def add_parts(parts, received):
    return [add_low(part, received[first]).astype(jnp.bfloat16) for first, part in enumerate(parts)]


def cross_sum(joint):
    return send(joint, across_core)


def first_sum(parts):
    side = mesh_parts()[1]
    received = [send(parts[shift], along_first(shift)) for shift in range(1, side)]
    return [
        add_low(parts[0][second], *[value[second] for value in received]).astype(jnp.bfloat16)
        for second in range(side)
    ]


def second_sum(level):
    chips, side = mesh_parts()
    received = [send(level[shift], along_second(shift)) for shift in range(1, side)]
    return [
        add_low(level[0][far], *[value[far] for value in received]).astype(jnp.bfloat16)
        for far in range(chips)
    ]


def far_sum(level):
    chips = mesh_parts()[0]
    received = [send(level[shift], along_z(shift)) for shift in range(1, chips)]
    return add_low(level[0], *received)


def tied(*values):
    return lax.optimization_barrier(values)


def fold_of(shape, columns):
    return columns if shape[0] % (16 * columns) == 0 else 1


def folded(values, fold):
    height = values.shape[0] // fold
    return jnp.concatenate([values[at * height : (at + 1) * height] for at in range(fold)], axis=1)


def unfolded(values, fold):
    width = values.shape[1] // fold
    return jnp.concatenate([values[:, at * width : (at + 1) * width] for at in range(fold)], axis=0)


def sum_everywhere(values):
    chips, side = mesh_parts()
    count = chips * 2 * side * side
    bit = 1
    while bit < count:

        def move(z, core, u, v, bit=bit):
            to = (((z * 2 + core) * side + u) * side + v) ^ bit
            return to // (2 * side * side), to // (side * side) % 2, to // side % side, to % side

        values = values + send(values, move)
        bit *= 2
    return values


def source_place(where, sibling, first, second, far, chips, side):
    core = 1 - where[CORE_AT] if sibling else where[CORE_AT]
    from_u = lax.rem(where[U_AT] - jnp.where(core == 0, first, second) + side, side)
    from_v = lax.rem(where[V_AT] - jnp.where(core == 0, second, first) + side, side)
    from_z = lax.rem(where[Z_AT] - far + chips, chips)
    return 2 * from_z + core, from_u * side + from_v


def weight_copies(where, pieces, target, sems, chips, side):
    copies = []
    rows = pieces[0].shape[1]
    for at, piece in enumerate(pieces):
        sibling, first, second = at // (side * side), at // side % side, at % side
        for far in range(chips):
            block, column = source_place(where, sibling, first, second, far, chips, side)
            copies.append(
                pltpu.make_async_copy(
                    piece.at[far],
                    target.at[column, pl.ds(pl.multiple_of(block * rows, 8), rows)],
                    sems.at[at * chips + far],
                )
            )
    return copies


def whole_copies(gathered, target, sems):
    rows = gathered.shape[1]
    columns = target.shape[0]
    return [
        pltpu.make_async_copy(
            gathered.at[at], target.at[at % columns, pl.ds(at // columns * rows, rows)], sems.at[at]
        )
        for at in range(gathered.shape[0])
    ]


def normalize(values):
    centred = values - jnp.mean(values, axis=1, keepdims=True)
    scale = lax.rsqrt(jnp.mean(centred * centred, axis=1, keepdims=True) + ln_eps)
    return centred * scale, scale


def normalize_back(grads, unit, scale):
    return scale * (
        grads - jnp.mean(grads, axis=1, keepdims=True) - unit * jnp.mean(grads * unit, axis=1, keepdims=True)
    )


def front_kernel(chips, side, where, tokens_ref, mod_ref, *rest):
    pieces, rest = rest[: 2 * side * side], rest[2 * side * side :]
    proj_ref, gate_ref, normed_t_ref, weight, sems = rest
    columns = side * side
    wide = proj_ref.shape[1] // columns
    narrow = weight.shape[2] - wide
    copies = weight_copies(where, pieces, weight, sems, chips, side)

    @pl.when(pl.program_id(0) == 0)
    def _():
        for copy in copies:
            copy.start()

    unit, ignored = normalize(tokens_ref[...].astype(jnp.float32))
    normed = (unit * (1.0 + mod_ref[0, 1:2, :]) + mod_ref[0, 0:1, :]).astype(jnp.bfloat16)
    normed_t_ref[...] = jnp.transpose(normed)

    @pl.when(pl.program_id(0) == 0)
    def _():
        for copy in copies:
            copy.wait()

    gate_ref[...] = jnp.zeros_like(gate_ref)
    for column in range(columns):
        product = dot_nn(normed, weight[column])
        proj_ref[:, column * wide : (column + 1) * wide] = product[:, :wide].astype(jnp.bfloat16)
        gate_ref[:, column * narrow : (column + 1) * narrow] = product[:, wide:]


def rows_spec(block, width):
    return pl.BlockSpec((block, width), lambda at, where: (at, 0))


def across_spec(height, block):
    return pl.BlockSpec((height, block), lambda at, where: (0, at))


def mod_spec(features, steps=4):
    share = steps // QUARTERS
    return pl.BlockSpec(
        (1, 8, features), lambda at, where: (jnp.where(where[FLAG_AT] == 1, 0, at // share), 0, 0)
    )


def any_specs(count):
    return [pl.BlockSpec(memory_space=pl.ANY)] * count


def shaped(shape, dtype):
    return jax.ShapeDtypeStruct(shape, dtype)


def call(kernel, where, args, grid, in_specs, out_specs, out_shape, scratch, name, flops, moved):
    return pl.pallas_call(
        kernel,
        grid_spec=pltpu.PrefetchScalarGridSpec(
            num_scalar_prefetch=1, grid=grid, in_specs=in_specs, out_specs=out_specs, scratch_shapes=scratch
        ),
        out_shape=out_shape,
        compiler_params=pltpu.CompilerParams(vmem_limit_bytes=VMEM_BYTES),
        cost_estimate=pl.CostEstimate(flops=int(flops * COST), bytes_accessed=int(moved * COST), transcendentals=0),
        name=name,
    )(where, *args)


def front_forward(where, tokens, mod, pieces, wide):
    chips, side = mesh_parts()
    rows, features = tokens.shape
    block = rows // QUARTERS
    columns = side * side
    depth, width = pieces[0].shape[1:]
    return call(
        functools.partial(front_kernel, chips, side),
        where,
        (tokens, mod, *pieces),
        (QUARTERS,),
        [rows_spec(block, features), mod_spec(features)] + any_specs(len(pieces)),
        [rows_spec(block, columns * wide), rows_spec(block, LANES), across_spec(features, block)],
        [
            shaped((rows, columns * wide), jnp.bfloat16),
            shaped((rows, LANES), jnp.float32),
            shaped((features, rows), jnp.bfloat16),
        ],
        [
            pltpu.VMEM((columns, features, width), jnp.bfloat16),
            pltpu.SemaphoreType.DMA((len(pieces) * chips,)),
        ],
        "front_forward",
        2 * rows * features * columns * width,
        20 * 10**6,
    )


def gelu_parts(values):
    inner = gelu_scale * (values + 0.044715 * values * values * values)
    bent = jnp.tanh(inner)
    half = 0.5 * (1.0 + bent)
    slope = half + 0.5 * values * (1.0 - bent * bent) * (gelu_scale * (1.0 + 3 * 0.044715 * values * values))
    return values * half, slope


def middle_kernel(chips, side, where, conv_ref, tokens_ref, cot_ref, mod_ref, bias_ref, gathered, *rest):
    (
        attended_ref,
        hidden_ref,
        slope_ref,
        hidden_t_ref,
        normed_t_ref,
        conv_t_ref,
        gradred_ref,
        weight,
        sems,
    ) = rest
    columns = side * side
    wide = hidden_ref.shape[1] // columns
    narrow = weight.shape[2] - wide
    copies = whole_copies(gathered, weight, sems)

    @pl.when(pl.program_id(0) == 0)
    def _():
        for copy in copies:
            copy.start()

    conv = conv_ref[...]
    conv_t_ref[...] = jnp.transpose(conv)
    gradred_ref[...] = (cot_ref[...].astype(jnp.float32) * mod_ref[0, 5:6, :]).astype(jnp.bfloat16)

    @pl.when(pl.program_id(0) == 0)
    def _():
        for copy in copies:
            copy.wait()

    for column in range(columns):
        attended_ref[:, column * narrow : (column + 1) * narrow] = dot_nn(conv, weight[column, :, wide:])
    after = tokens_ref[...].astype(jnp.float32) + mod_ref[0, 2:3, :] * attended_ref[...]
    unit, ignored = normalize(after)
    normed = (unit * (1.0 + mod_ref[0, 4:5, :]) + mod_ref[0, 3:4, :]).astype(jnp.bfloat16)
    normed_t_ref[...] = jnp.transpose(normed)
    for column in range(columns):
        span = slice(column * wide, (column + 1) * wide)
        preact = dot_nn(normed, weight[column, :, :wide]) + bias_ref[:, span]
        hidden, slope = gelu_parts(preact)
        low = hidden.astype(jnp.bfloat16)
        hidden_ref[:, span] = low
        slope_ref[:, span] = slope.astype(jnp.bfloat16)
        hidden_t_ref[span, :] = jnp.transpose(low)


def middle_forward(where, conv, tokens, cotangent, mod, bias, gathered, wide):
    chips, side = mesh_parts()
    rows, features = tokens.shape
    block = rows // QUARTERS
    columns = side * side
    width = gathered.shape[2]
    hidden = columns * wide
    return call(
        functools.partial(middle_kernel, chips, side),
        where,
        (conv, tokens, cotangent, mod, bias, gathered),
        (QUARTERS,),
        [
            rows_spec(block, features),
            rows_spec(block, features),
            rows_spec(block, features),
            mod_spec(features),
            pl.BlockSpec((1, hidden), lambda at, where: (0, 0)),
        ]
        + any_specs(1),
        [
            rows_spec(block, features),
            rows_spec(block, hidden),
            rows_spec(block, hidden),
            across_spec(hidden, block),
            across_spec(features, block),
            across_spec(features, block),
            rows_spec(block, features),
        ],
        [
            shaped((rows, features), jnp.float32),
            shaped((rows, hidden), jnp.bfloat16),
            shaped((rows, hidden), jnp.bfloat16),
            shaped((hidden, rows), jnp.bfloat16),
            shaped((features, rows), jnp.bfloat16),
            shaped((features, rows), jnp.bfloat16),
            shaped((rows, features), jnp.bfloat16),
        ],
        [
            pltpu.VMEM((columns, features, width), jnp.bfloat16),
            pltpu.SemaphoreType.DMA((gathered.shape[0],)),
        ],
        "middle_forward",
        2 * rows * features * columns * width,
        60 * 10**6,
    )


def middle_back_kernel(
    chips, side, where, hidden_ref, slope_ref, attended_ref, tokens_ref, cot_ref, mod_ref, *rest
):
    count = 2 * side * side
    gathered, reduce_pieces, rest = rest[0], rest[1 : 1 + count], rest[1 + count :]
    (
        out_ref,
        gradpre_ref,
        gradafter_ref,
        gradatt_ref,
        gradconv_ref,
        sums_ref,
        biassum_ref,
        weight,
        reduce_weight,
        stage,
        sems,
        reduce_sems,
    ) = rest
    columns = side * side
    hidden = hidden_ref.shape[1]
    wide = hidden // columns
    narrow = weight.shape[2] - wide
    height = reduce_pieces[0].shape[1]
    fold = reduce_pieces[0].shape[2] // narrow
    copies = whole_copies(gathered, weight, sems)

    @pl.when(pl.program_id(0) == 0)
    def _():
        biassum_ref[...] = jnp.zeros_like(biassum_ref)

        def staged(turn):
            sibling, far = turn // chips, turn % chips
            slot = turn % 2
            found = []
            for first in range(side):
                for second in range(side):
                    at = first * side + second
                    block, column = source_place(where, sibling, first, second, far, chips, side)
                    found.append(
                        pltpu.make_async_copy(
                            reduce_pieces[sibling * columns + at].at[far],
                            stage.at[slot, column],
                            reduce_sems.at[slot, at],
                        )
                    )
            return block, found

        turns = [staged(turn) for turn in range(2 * chips)]
        for copy in turns[0][1]:
            copy.start()
        for turn, (block, found) in enumerate(turns):
            if turn + 1 < len(turns):
                for copy in turns[turn + 1][1]:
                    copy.start()
            if turn == 0:
                for copy in copies:
                    copy.start()
            for copy in found:
                copy.wait()
            for at in range(fold):
                target = pl.ds(pl.multiple_of((block * fold + at) * height, 8), height)
                for column in range(columns):
                    reduce_weight[target, column * narrow : (column + 1) * narrow] = stage[
                        turn % 2, column, :, at * narrow : (at + 1) * narrow
                    ]

    cot = cot_ref[...].astype(jnp.float32)
    attended = attended_ref[...]
    after = tokens_ref[...].astype(jnp.float32) + mod_ref[0, 2:3, :] * attended
    reduced = dot_nn(hidden_ref[...], reduce_weight[...])
    sums_ref[...] = jnp.zeros_like(sums_ref)
    sums_ref[0, 3:4, :] = jnp.sum(cot * reduced, axis=0, keepdims=True)
    out_ref[...] = (after + mod_ref[0, 5:6, :] * reduced).astype(out_ref.dtype)
    gradred = (cot * mod_ref[0, 5:6, :]).astype(jnp.bfloat16)

    @pl.when(pl.program_id(0) == 0)
    def _():
        for copy in copies:
            copy.wait()

    gradmid = jnp.zeros(after.shape, jnp.float32)
    for column in range(columns):
        span = slice(column * wide, (column + 1) * wide)
        gradact = dot_nt(gradred, reduce_weight[span, :])
        gradpre = (gradact * slope_ref[:, span].astype(jnp.float32)).astype(jnp.bfloat16)
        gradpre_ref[:, span] = gradpre
        biassum_ref[:, span] += jnp.sum(gradpre.astype(jnp.float32), axis=0, keepdims=True)
        gradmid = gradmid + dot_nt(gradpre, weight[column, :, :wide])
    unit, scale = normalize(after)
    sums_ref[0, 1:2, :] = jnp.sum(gradmid, axis=0, keepdims=True)
    sums_ref[0, 2:3, :] = jnp.sum(gradmid * unit, axis=0, keepdims=True)
    gradafter = cot + normalize_back(gradmid * (1.0 + mod_ref[0, 4:5, :]), unit, scale)
    gradafter_ref[...] = gradafter
    sums_ref[0, 0:1, :] = jnp.sum(gradafter * attended, axis=0, keepdims=True)
    gradatt_ref[...] = (gradafter * mod_ref[0, 2:3, :]).astype(jnp.bfloat16)
    gradconv = jnp.zeros(after.shape, jnp.float32)
    for column in range(columns):
        gradconv = gradconv + dot_nt(
            gradatt_ref[:, column * narrow : (column + 1) * narrow], weight[column, :, wide:]
        )
    gradconv_ref[...] = gradconv


def middle_backward(where, hidden, slope, attended, tokens, cotangent, mod, gathered, reduce_pieces):
    chips, side = mesh_parts()
    rows, features = tokens.shape
    steps = QUARTERS if side * side <= 4 else 2 * QUARTERS
    block = rows // steps
    columns = side * side
    inner = hidden.shape[1]
    width = gathered.shape[2]
    depth, narrow = reduce_pieces[0].shape[1:]
    return call(
        functools.partial(middle_back_kernel, chips, side),
        where,
        (hidden, slope, attended, tokens, cotangent, mod, gathered, *reduce_pieces),
        (steps,),
        [
            rows_spec(block, inner),
            rows_spec(block, inner),
            rows_spec(block, features),
            rows_spec(block, features),
            rows_spec(block, features),
            mod_spec(features, steps),
        ]
        + any_specs(1 + len(reduce_pieces)),
        [
            rows_spec(block, features),
            rows_spec(block, inner),
            rows_spec(block, features),
            rows_spec(block, features),
            rows_spec(block, features),
            pl.BlockSpec((1, 8, features), lambda at, where: (at, 0, 0)),
            pl.BlockSpec((1, inner), lambda at, where: (0, 0)),
        ],
        [
            shaped((rows, features), jnp.bfloat16),
            shaped((rows, inner), jnp.bfloat16),
            shaped((rows, features), jnp.float32),
            shaped((rows, features), jnp.bfloat16),
            shaped((rows, features), jnp.float32),
            shaped((steps, 8, features), jnp.float32),
            shaped((1, inner), jnp.float32),
        ],
        [
            pltpu.VMEM((columns, features, width), jnp.bfloat16),
            pltpu.VMEM((inner, features), jnp.bfloat16),
            pltpu.VMEM((2, columns, depth, narrow), jnp.bfloat16),
            pltpu.SemaphoreType.DMA((gathered.shape[0],)),
            pltpu.SemaphoreType.DMA((2, columns)),
        ],
        "middle_backward",
        6 * rows * features * inner,
        80 * 10**6,
    )


def front_back_kernel(
    chips, side, where, gradproj_ref, gradgate_ref, gradafter_ref, tokens_ref, mod_ref, *rest
):
    pieces, rest = rest[: 2 * side * side], rest[2 * side * side :]
    out_ref, sums_ref, weight, both, sems = rest
    columns = side * side
    wide = gradproj_ref.shape[1] // columns
    narrow = weight.shape[2] - wide
    copies = weight_copies(where, pieces, weight, sems, chips, side)

    @pl.when(pl.program_id(0) == 0)
    def _():
        for copy in copies:
            copy.start()

    unit, scale = normalize(tokens_ref[...].astype(jnp.float32))

    @pl.when(pl.program_id(0) == 0)
    def _():
        for copy in copies:
            copy.wait()

    gradin = jnp.zeros(unit.shape, jnp.float32)
    for column in range(columns):
        both[:, :wide] = gradproj_ref[:, column * wide : (column + 1) * wide]
        both[:, wide:] = gradgate_ref[:, column * narrow : (column + 1) * narrow].astype(jnp.bfloat16)
        gradin = gradin + dot_nt(both[...], weight[column])
    sums_ref[...] = jnp.zeros_like(sums_ref)
    sums_ref[0, 0:1, :] = jnp.sum(gradin, axis=0, keepdims=True)
    sums_ref[0, 1:2, :] = jnp.sum(gradin * unit, axis=0, keepdims=True)
    out_ref[...] = (
        gradafter_ref[...] + normalize_back(gradin * (1.0 + mod_ref[0, 1:2, :]), unit, scale)
    ).astype(out_ref.dtype)


def front_backward(where, gradproj, gradgate, gradafter, tokens, mod, pieces):
    chips, side = mesh_parts()
    rows, features = tokens.shape
    block = rows // QUARTERS
    columns = side * side
    width = pieces[0].shape[2]
    return call(
        functools.partial(front_back_kernel, chips, side),
        where,
        (gradproj, gradgate, gradafter, tokens, mod, *pieces),
        (QUARTERS,),
        [
            rows_spec(block, gradproj.shape[1]),
            rows_spec(block, LANES),
            rows_spec(block, features),
            rows_spec(block, features),
            mod_spec(features),
        ]
        + any_specs(len(pieces)),
        [rows_spec(block, features), pl.BlockSpec((1, 8, features), lambda at, where: (at, 0, 0))],
        [shaped((rows, features), jnp.bfloat16), shaped((QUARTERS, 8, features), jnp.float32)],
        [
            pltpu.VMEM((columns, features, width), jnp.bfloat16),
            pltpu.VMEM((block, width), jnp.bfloat16),
            pltpu.SemaphoreType.DMA((len(pieces) * chips,)),
        ],
        "front_backward",
        2 * rows * features * columns * width,
        25 * 10**6,
    )


def target_core(where, sibling):
    return 1 - where[CORE_AT] if sibling else where[CORE_AT]


def target_block(where, sibling, far, chips):
    return 2 * lax.rem(where[Z_AT] + far, chips) + target_core(where, sibling)


def target_column(where, sibling, first, second, side):
    core = target_core(where, sibling)
    to_u = lax.rem(where[U_AT] + jnp.where(core == 0, first, second), side)
    to_v = lax.rem(where[V_AT] + jnp.where(core == 0, second, first), side)
    return to_u * side + to_v


def relative_column(where, sibling, column, side):
    core = target_core(where, sibling)
    by_u = lax.rem(column // side - where[U_AT] + side, side)
    by_v = lax.rem(column % side - where[V_AT] + side, side)
    return jnp.where(core == 0, by_u, by_v), jnp.where(core == 0, by_v, by_u)


def grads_by_column_kernel(side, depth, fars, sibling, added, where, *rest):
    lefts, rest = rest[:fars], rest[fars:]
    right_ref, rest = rest[0], rest[1:]
    received, outs = (rest[0], rest[1:]) if added else (None, rest)
    product = dot_nn(jnp.concatenate([left[...] for left in lefts], axis=0), right_ref[...])

    def store(out):
        for far in range(fars):
            value = product[far * depth : (far + 1) * depth]
            if added:
                value = value + received[0, 0, far].astype(jnp.float32)
            out[far] = value.astype(jnp.bfloat16)

    if sibling:
        store(outs[0].at[0, 0])
        return
    for first in range(side):

        @pl.when(pl.program_id(0) // side == first)
        def _(first=first):
            store(outs[first].at[0])


def grads_by_row_kernel(side, depth, fars, fold, sibling, added, extra, where, *rest):
    lefts, rest = rest[:fars], rest[fars:]
    right_ref, rest = rest[0], rest[1:]
    if extra:
        extra_ref, rest = rest[0], rest[1:]
    received, rest = (rest[0], rest[1:]) if added else (None, rest)
    outs, product, small = rest[:-2], rest[-2], rest[-1]
    if sibling:
        outs = [outs[0].at[first] for first in range(side)]
    columns = side * side
    wide = right_ref.shape[1] // columns
    width = outs[0].shape[-1]
    left = jnp.concatenate([piece[...] for piece in lefts], axis=0)
    product[...] = dot_nn(left, right_ref[...])
    if extra:
        small[...] = dot_nn(left, extra_ref[...].astype(jnp.bfloat16))
    for column in range(columns):
        by_first, by_second = relative_column(where, sibling, column, side)
        for first in range(side):

            @pl.when(by_first == first)
            def _(first=first, column=column, by_second=by_second):
                for far in range(fars):
                    height = depth // fold
                    for at in range(fold):
                        span = slice(far * depth + at * height, far * depth + (at + 1) * height)
                        lanes = slice(at * wide, (at + 1) * wide)
                        value = product[span, column * wide : (column + 1) * wide]
                        if added:
                            value = value + received[first, by_second, far, :, lanes].astype(jnp.float32)
                        outs[first][by_second, far, :, lanes] = value.astype(jnp.bfloat16)
                    if extra:
                        span = slice(far * depth, (far + 1) * depth)
                        narrow = width - wide
                        value = small[span, column * narrow : (column + 1) * narrow]
                        if added:
                            value = value + received[first, by_second, far, :, wide:].astype(jnp.float32)
                        outs[first][by_second, far, :, wide:] = value.astype(jnp.bfloat16)


def weight_grads(where, left_t, right, sibling, received=None, extra=None, narrow=0, fold=1):
    chips, side = mesh_parts()
    columns = side * side
    height, rows = left_t.shape
    depth = height // (2 * chips)
    wide = right.shape[1] // columns
    width = wide * fold + narrow
    added = received is not None
    piece = (depth // fold, width)
    flops = 2 * rows * (height // 2) * columns * width
    moved = 2 * (rows * height // 2 + rows * columns * width + height // 2 * columns * width * (2 if added else 1))

    def left_spec(far, moving):
        return pl.BlockSpec(
            (depth, rows),
            lambda at, where: (target_block(where, sibling, at if moving else far, chips), 0),
        )

    if wide % LANES == 0 and extra is None and fold == 1 and depth < 2 * LANES:
        steps = columns
        specs = [left_spec(far, False) for far in range(chips)]
        specs.append(
            pl.BlockSpec(
                (rows, wide),
                lambda at, where: (0, target_column(where, sibling, at // side, lax.rem(at, side), side)),
            )
        )
        args = [left_t] * chips + [right]
        joint = pl.BlockSpec((1, 1, chips, *piece), lambda at, where: (at // side, lax.rem(at, side), 0, 0, 0))

        def out_spec(first):
            return pl.BlockSpec(
                (1, chips, *piece), lambda at, where: (jnp.clip(at - first * side, 0, side - 1), 0, 0, 0)
            )

        kernel = functools.partial(grads_by_column_kernel, side, depth, chips, sibling, added)
        scratch = []
    else:
        moving = depth >= 2 * LANES
        fars = 1 if moving else chips
        steps = chips if moving else 1
        specs = [left_spec(far, moving) for far in range(fars)]
        specs.append(pl.BlockSpec(right.shape, lambda at, where: (0, 0)))
        args = [left_t] * fars + [right]
        if extra is not None:
            specs.append(pl.BlockSpec(extra.shape, lambda at, where: (0, 0)))
            args.append(extra)
        joint = pl.BlockSpec((side, side, fars, *piece), lambda at, where: (0, 0, at, 0, 0))

        def out_spec(first):
            return pl.BlockSpec((side, fars, *piece), lambda at, where: (0, at, 0, 0))

        kernel = functools.partial(
            grads_by_row_kernel, side, depth, fars, fold, sibling, added, extra is not None
        )
        scratch = [
            pltpu.VMEM((fars * depth, right.shape[1]), jnp.float32),
            pltpu.VMEM((fars * depth, LANES), jnp.float32),
        ]
    if added:
        specs.append(joint)
        args.append(received)
    if sibling:
        outs, arrays = [joint], [shaped((side, side, chips, *piece), jnp.bfloat16)]
    else:
        outs = [out_spec(first) for first in range(side)]
        arrays = [shaped((side, chips, *piece), jnp.bfloat16)] * side
    found = call(kernel, where, args, (steps,), specs, outs, arrays, scratch, "weight_grads", flops, moved)
    return found[0] if sibling else found


def pick(values, at):
    return lax.dynamic_index_in_dim(values, at, 0, keepdims=False)


def on_device(
    tokens,
    conditions,
    resolution,
    modulate_weight,
    modulate_bias,
    attend_weight,
    forget_weight,
    forget_bias,
    conv_taps,
    output_weight,
    expand_weight,
    expand_bias,
    reduce_weight,
    cotangent,
):
    chips, side = mesh_parts()
    columns = side * side
    blocks = 2 * chips
    fsdp_at = lax.axis_index("fsdp")
    dp_at = lax.axis_index("dp")
    z_at, core_at, u_at, v_at = fsdp_at // 2, fsdp_at % 2, dp_at // side, dp_at % side
    where = jnp.stack([z_at, core_at, u_at, v_at, resolution[0]]).astype(jnp.int32)
    slots, features = conditions.shape
    heads = forget_bias.shape[0]
    own_rows, own_columns = modulate_weight.shape
    single = resolution[0] == 1

    attend_pieces = gather_shard(jnp.concatenate([attend_weight, forget_weight], axis=1))

    cond_values = conditions.astype(jnp.float32)
    silu_out, silu_back = jax.vjp(jax.nn.silu, cond_values)
    cond_low = silu_out.astype(jnp.bfloat16)
    small = jnp.concatenate([cond_low.reshape(-1), modulate_bias, expand_bias])
    small_size = small.shape[0]
    small = jnp.stack(gather_shard(small.reshape(1, small_size))).reshape(blocks * columns, small_size)
    order = []
    for block in range(blocks):
        for column in range(columns):
            sibling = jnp.abs(block % 2 - core_at)
            far = (z_at - block // 2) % chips
            by_u, by_v = (u_at - column // side) % side, (v_at - column % side) % side
            first = jnp.where(block % 2 == 0, by_u, by_v)
            second = jnp.where(block % 2 == 0, by_v, by_u)
            order.append(((sibling * side + first) * side + second) * chips + far)
    order = jnp.stack(order)
    chosen = (order[:, None] == jnp.arange(blocks * columns)[None, :]).astype(jnp.bfloat16)
    small = jnp.dot(chosen, small, preferred_element_type=jnp.float32)
    cond_all = small[:, : slots * features].astype(jnp.bfloat16).reshape(-1, features)
    modbias_whole = small[:, slots * features : small_size - expand_bias.shape[0]].reshape(-1)
    expandbias_whole = small[:, small_size - expand_bias.shape[0] :].reshape(1, -1)
    cond_columns = lax.dynamic_slice_in_dim(cond_all, fsdp_at * own_rows, own_rows, axis=1)
    partial = jnp.dot(cond_columns, modulate_weight, preferred_element_type=jnp.float32)
    partial = partial.reshape(chips, 2, columns * slots, own_columns)
    to_sibling = lax.dynamic_index_in_dim(partial, 1 - core_at, 1, keepdims=False)
    partial = lax.dynamic_index_in_dim(partial, core_at, 1, keepdims=False) + send(to_sibling, across_core)
    modulation = pick(partial, z_at)
    for shift in range(1, chips):
        modulation = modulation + send(pick(partial, (z_at + shift) % chips), along_z(shift))
    modulation = modulation.reshape(columns, slots, own_columns)
    pieces = [pick(modulation, dp_at)]
    for shift in range(1, columns):
        pieces.append(send(pick(modulation, (dp_at + shift) % columns), along_dp(shift)))
    pieces = jnp.stack(pieces)
    modulation = jnp.concatenate([pick(pieces, (dp_at - column) % columns) for column in range(columns)], axis=1)
    modulation = (modulation + modbias_whole[None, :]).reshape(slots, 6, features)
    modulation = jnp.pad(modulation, ((0, 0), (0, 2), (0, 0)))

    fold = fold_of(reduce_weight.shape, columns)
    middle_pieces = lax.all_gather(
        jnp.concatenate([expand_weight, output_weight], axis=1), ("fsdp", "dp"), axis=0, tiled=False
    )
    attend_first, reduce_shard = tied(attend_pieces[0], folded(reduce_weight, fold))
    attend_pieces[0] = attend_first
    reduce_far = far_pieces(reduce_shard)

    projected, gate_logit, normed_in_t = front_forward(
        where, tokens, modulation, attend_pieces, attend_weight.shape[1]
    )
    projected, reduce_far = tied(projected, reduce_far)
    reduce_level = first_pieces(jnp.stack(reduce_far))
    bias_wide = jnp.pad(forget_bias[None, :], ((0, 0), (0, LANES - heads)))
    conv_low, normed_heads, ratios, states = attention_forward(
        resolution, projected, gate_logit, bias_wide, conv_taps, heads
    )
    conv_low, reduce_level = tied(conv_low, reduce_level)
    reduce_pieces = second_pieces(reduce_level)
    attended, hidden, slope, hidden_t, normed_mid_t, conv_t, grad_reduced = middle_forward(
        where, conv_low, tokens, cotangent, modulation, expandbias_whole, middle_pieces, expand_weight.shape[1]
    )
    hidden_t, reduce_pieces = tied(hidden_t, reduce_pieces)
    reduce_pieces = core_pieces(reduce_pieces)
    reduce_other = cross_sum(weight_grads(where, hidden_t, grad_reduced, True, fold=fold))
    reduce_parts = weight_grads(where, hidden_t, grad_reduced, False, fold=fold)
    hidden, reduce_parts, reduce_other = tied(hidden, reduce_parts, reduce_other)
    reduce_level = first_sum(add_parts(reduce_parts, reduce_other))
    block_out, grad_preact, grad_after, grad_attended, grad_conv, middle_sums, bias_sums = middle_backward(
        where, hidden, slope, attended, tokens, cotangent, modulation, middle_pieces, reduce_pieces
    )
    grad_preact, reduce_level = tied(grad_preact, reduce_level)
    reduce_level = second_sum(reduce_level)
    expand_other = weight_grads(where, normed_mid_t, grad_preact, True)
    expand_other, conv_t = tied(expand_other, conv_t)
    expand_other = cross_sum(expand_other)
    output_other = cross_sum(weight_grads(where, conv_t, grad_attended, True))
    expand_parts = weight_grads(where, normed_mid_t, grad_preact, False, expand_other)
    output_parts = weight_grads(where, conv_t, grad_attended, False, output_other)
    grad_conv, expand_parts, output_parts, reduce_level = tied(grad_conv, expand_parts, output_parts, reduce_level)
    reduce_grad = far_sum(reduce_level)
    expand_level = first_sum(expand_parts)
    output_level = first_sum(output_parts)
    grad_projected, grad_gate, forgetbias_local, taps_local = attention_backward(
        resolution, projected, gate_logit, bias_wide, conv_taps, normed_heads, ratios, states, grad_conv, heads
    )
    grad_projected, expand_level, output_level, reduce_grad = tied(
        grad_projected, expand_level, output_level, reduce_grad
    )
    reduce_grad = unfolded(reduce_grad, fold)
    expand_level = second_sum(expand_level)
    output_level = second_sum(output_level)
    tokens_grad, front_sums = front_backward(
        where, grad_projected, grad_gate, grad_after, tokens, modulation, attend_pieces
    )
    grad_projected, front_sums, expand_level, output_level = tied(
        grad_projected, front_sums, expand_level, output_level
    )
    narrow = heads // columns
    attend_other = cross_sum(weight_grads(where, normed_in_t, grad_projected, True, None, grad_gate, narrow))
    attend_parts = weight_grads(where, normed_in_t, grad_projected, False, None, grad_gate, narrow)
    attend_level = first_sum(add_parts(attend_parts, attend_other))
    expand_grad = far_sum(expand_level)
    output_grad = far_sum(output_level)
    attend_both = far_sum(second_sum(attend_level))
    attend_grad, forget_grad = attend_both[:, : attend_weight.shape[1]], attend_both[:, attend_weight.shape[1] :]

    middle_sums = jnp.sum(middle_sums.reshape(QUARTERS, -1, 8, features), axis=1)
    grad_modulation = jnp.concatenate([front_sums[:, :2], middle_sums[:, :4]], axis=1)
    first_slot = (jnp.arange(slots) == 0)[:, None, None]
    grad_modulation = jnp.where(
        single, jnp.where(first_slot, jnp.sum(grad_modulation, axis=0, keepdims=True), 0.0), grad_modulation
    )
    grad_modulation = grad_modulation.reshape(slots, columns, own_columns).astype(jnp.bfloat16)
    grad_modulation = jnp.swapaxes(grad_modulation, 0, 1)
    rows_here = [pick(grad_modulation, dp_at)]
    for shift in range(1, columns):
        rows_here.append(send(pick(grad_modulation, (dp_at + shift) % columns), along_dp(shift)))
    rows_here = jnp.concatenate(rows_here, axis=0)
    rows_here = jnp.concatenate(
        [rows_here] + [send(rows_here, along_z(shift)) for shift in range(1, chips)], axis=0
    )
    rows_here = jnp.concatenate([rows_here, send(rows_here, across_core)], axis=0)
    order = []
    for sibling in range(2):
        for far in range(chips):
            for shift in range(columns):
                block = 2 * ((z_at - far) % chips) + jnp.abs(core_at - sibling)
                order.append(block * columns + (dp_at - shift) % columns)
    order = (jnp.stack(order)[:, None] * slots + jnp.arange(slots)[None, :]).reshape(-1)
    chosen = (order[:, None] == jnp.arange(order.shape[0])[None, :]).astype(jnp.bfloat16)
    cond_here = jnp.dot(chosen, cond_columns, preferred_element_type=jnp.float32).astype(jnp.bfloat16)
    modulate_grad = lax.dot_general(
        cond_here, rows_here, (((0,), (0,)), ((), ())), preferred_element_type=jnp.float32
    )
    modbias_here = jnp.sum(rows_here.astype(jnp.float32), axis=0, keepdims=True)
    modbias_all = jnp.stack(
        [modbias_here] + [send(modbias_here, along_dp(shift)) for shift in range(1, columns)]
    )
    modbias_all = jnp.concatenate([pick(modbias_all, (dp_at - column) % columns) for column in range(columns)], axis=1)
    own_bias = modulate_bias.shape[0]
    linear_at = fsdp_at * columns + dp_at
    modbias_grad = lax.dynamic_slice_in_dim(modbias_all, linear_at * own_bias, own_bias, axis=1).reshape(-1)
    grad_cond = lax.dot_general(
        rows_here, modulate_weight, (((1,), (1,)), ((), ())), preferred_element_type=jnp.float32
    )
    grad_cond = jnp.moveaxis(grad_cond.reshape(blocks, columns, slots, own_rows), 1, 0)
    cond_sum = grad_cond[0]
    for shift in range(1, columns):
        cond_sum = cond_sum + send(grad_cond[shift], along_dp(-shift))
    cond_sum = cond_sum.reshape(2, chips, slots, own_rows)
    cond_parts = []
    for sibling in range(2):
        for far in range(chips):
            def move(z, core, u, v, sibling=sibling, far=far):
                return (z - far) % chips, core ^ sibling, u, v
            part = cond_sum[sibling, far]
            cond_parts.append(part if sibling + far == 0 else send(part, move))
    cond_parts = jnp.stack(cond_parts)
    cond_columns_all = []
    for block in range(blocks):
        sibling = jnp.abs(block % 2 - core_at)
        cond_columns_all.append(pick(cond_parts, sibling * chips + (block // 2 - z_at) % chips))
    grad_cond_low = jnp.concatenate(cond_columns_all, axis=1)
    conditions_grad = silu_back(grad_cond_low)[0].astype(jnp.bfloat16)

    sums = jnp.concatenate(
        [
            taps_local,
            jnp.pad(forgetbias_local, ((0, 0), (0, features - LANES))),
            bias_sums.reshape(-1, features),
        ],
        axis=0,
    )
    sums, front_sums = tied(sums, front_sums)
    sums = sum_everywhere(sums)
    taps_count = conv_taps.shape[0]
    taps_grad = sums[:taps_count]
    forgetbias_grad = sums[taps_count, :heads]
    own_bias = expand_bias.shape[0]
    expandbias_grad = lax.dynamic_slice_in_dim(
        sums[taps_count + 1 :].reshape(-1), linear_at * own_bias, own_bias, axis=0
    )
    return (
        block_out,
        tokens_grad,
        conditions_grad,
        modulate_grad,
        modbias_grad,
        attend_grad,
        forget_grad,
        forgetbias_grad,
        taps_grad,
        output_grad,
        expand_grad,
        expandbias_grad,
        reduce_grad,
    )


def solution(mesh):
    in_specs = (
        P(("fsdp", "dp"), None),
        P(("fsdp", "dp"), None),
        P(("fsdp", "dp")),
        P("fsdp", "dp"),
        P(("fsdp", "dp")),
        P("fsdp", "dp"),
        P("fsdp", "dp"),
        P(),
        P(),
        P("fsdp", "dp"),
        P("fsdp", "dp"),
        P(("fsdp", "dp")),
        P("fsdp", "dp"),
        P(("fsdp", "dp"), None),
    )
    out_specs = (
        P(("fsdp", "dp"), None),
        P(("fsdp", "dp"), None),
        P(("fsdp", "dp"), None),
        P("fsdp", "dp"),
        P(("fsdp", "dp")),
        P("fsdp", "dp"),
        P("fsdp", "dp"),
        P(),
        P(),
        P("fsdp", "dp"),
        P("fsdp", "dp"),
        P(("fsdp", "dp")),
        P("fsdp", "dp"),
    )
    return jax.shard_map(
        on_device, mesh=mesh, in_specs=in_specs, out_specs=out_specs, check_vma=False
    )
```

```python
import functools
import math

import jax
import jax.numpy as jnp
from jax import lax
from jax.experimental import pallas as pl
from jax.experimental.pallas import tpu as pltpu
from jax.sharding import PartitionSpec as P

GRID = 32
CHUNK = 256
LANES = 128
VMEM_BYTES = 60 * 1024 * 1024
QUARTERS = 4
COST = 0.02
Z_AT, CORE_AT, U_AT, V_AT, FLAG_AT = range(5)
normalizer = 16.0
ln_eps = 1e-06
gelu_scale = math.sqrt(2.0 / math.pi)
rms_floor = 1.0
masked_log = -1e30
highest = lax.Precision.HIGHEST


def dot_nn(former, latter, precision=None):
    return lax.dot_general(
        former, latter, (((1,), (0,)), ((), ())), precision=precision, preferred_element_type=jnp.float32
    )


def dot_nt(former, latter):
    return lax.dot_general(former, latter, (((1,), (1,)), ((), ())), preferred_element_type=jnp.float32)


def dot_tn(former, latter):
    return lax.dot_general(former, latter, (((0,), (0,)), ((), ())), preferred_element_type=jnp.float32)


def head_window(head, head_size):
    first = head * head_size
    start = first // LANES * LANES
    stop = -(-(first + head_size) // LANES) * LANES
    return start, stop - start, first - start


def lane_mask(width, offset, head_size):
    lanes = lax.broadcasted_iota(jnp.int32, (1, width), 1)
    return (lanes >= offset) & (lanes < offset + head_size)


def cell_masks(rows, side):
    position = lax.broadcasted_iota(jnp.int32, (rows, 1), 0)
    grid_col = position & (side - 1)
    grid_row = (position & (side * side - 1)) >> int(math.log2(side))
    return grid_row, grid_col


def conv_forward_tile(values, taps, side):
    rows = values.shape[0]
    grid_row, grid_col = cell_masks(rows, side)
    before = jnp.where(grid_col > 0, pltpu.roll(values, 1, 0), 0.0)
    after = jnp.where(grid_col < side - 1, pltpu.roll(values, rows - 1, 0), 0.0)
    sums = [
        before * taps[3 * step : 3 * step + 1]
        + values * taps[3 * step + 1 : 3 * step + 2]
        + after * taps[3 * step + 2 : 3 * step + 3]
        for step in range(3)
    ]
    upper = jnp.where(grid_row > 0, pltpu.roll(sums[0], side, 0), 0.0)
    lower = jnp.where(grid_row < side - 1, pltpu.roll(sums[2], rows - side, 0), 0.0)
    return sums[1] + upper + lower


def conv_backward_tile(values, grads, taps, side):
    rows = values.shape[0]
    grid_row, grid_col = cell_masks(rows, side)
    before = jnp.where(grid_col > 0, pltpu.roll(values, 1, 0), 0.0)
    after = jnp.where(grid_col < side - 1, pltpu.roll(values, rows - 1, 0), 0.0)
    grad_sums = [
        jnp.where(grid_row < side - 1, pltpu.roll(grads, rows - side, 0), 0.0),
        grads,
        jnp.where(grid_row > 0, pltpu.roll(grads, side, 0), 0.0),
    ]
    tap_rows = []
    for step in range(3):
        for shifted in (before, values, after):
            tap_rows.append(jnp.sum(grad_sums[step] * shifted, axis=0, keepdims=True))
    parts = [
        sum(grad_sums[step] * taps[3 * step + col : 3 * step + col + 1] for step in range(3))
        for col in range(3)
    ]
    result = (
        parts[1]
        + pltpu.roll(jnp.where(grid_col > 0, parts[0], 0.0), rows - 1, 0)
        + pltpu.roll(jnp.where(grid_col < side - 1, parts[2], 0.0), 1, 0)
    )
    return result, tap_rows


def decay_sums(gate, bias, chunk):
    logit = gate + bias
    decay = (jnp.minimum(logit, 0.0) - jnp.log1p(jnp.exp(-jnp.abs(logit)))) / normalizer
    row_at = lax.broadcasted_iota(jnp.int32, (chunk, chunk), 0)
    col_at = lax.broadcasted_iota(jnp.int32, (chunk, chunk), 1)
    lower = jnp.where(row_at >= col_at, 1.0, 0.0)
    return dot_nn(lower, decay, highest)


def attention_forward_kernel(
    heads, head_size, flag_ref, proj_ref, gate_ref, bias_ref, taps_ref, conv_ref, normed_ref, ratio_ref, states_ref, state
):
    chunk_at = pl.program_id(0)
    chunk = proj_ref.shape[0]
    features = heads * head_size
    single = flag_ref[0] == 1

    @pl.when(jnp.logical_or(chunk_at == 0, jnp.logical_not(single)))
    def _():
        state[...] = jnp.zeros_like(state)

    cumul = decay_sums(gate_ref[...], bias_ref[...], chunk)
    cumul_t = jnp.transpose(cumul)
    scaled = cumul + math.log(head_size ** (-0.5))
    last = cumul[chunk - 1 : chunk, :]
    last_scaled = scaled[chunk - 1 : chunk, :]
    whole = jnp.exp(last)
    row_at = lax.broadcasted_iota(jnp.int32, (chunk, chunk), 0)
    col_at = lax.broadcasted_iota(jnp.int32, (chunk, chunk), 1)
    causal = row_at >= col_at
    lane_at = lax.broadcasted_iota(jnp.int32, (1, LANES), 1)
    rows = pl.ds(pl.multiple_of(chunk_at * chunk, chunk), chunk)
    ratios = jnp.zeros((chunk, LANES), jnp.float32)
    for head in range(heads):
        start, width, offset = head_window(head, head_size)
        inside = lane_mask(width, offset, head_size)
        query = jnp.where(inside, proj_ref[:, start : start + width], 0)
        key = proj_ref[:, features + start : features + start + width]
        value = proj_ref[:, 2 * features + start : 2 * features + start + width]
        scaled_wide = jnp.broadcast_to(scaled[:, head : head + 1], (chunk, LANES))
        start_wide = jnp.exp(scaled_wide)
        end_wide = jnp.exp(last_scaled[:, head : head + 1] - scaled_wide)
        start_wide = jnp.concatenate([start_wide] * (width // LANES), axis=1)
        end_wide = jnp.concatenate([end_wide] * (width // LANES), axis=1)
        spread = jnp.concatenate([scaled_wide] * (chunk // LANES), axis=1) - cumul_t[head : head + 1, :]
        weights = jnp.exp(jnp.where(causal, spread, masked_log))
        scores = (dot_nt(query, key) * weights).astype(jnp.bfloat16)
        held = state[head, :width, :width]
        held_low = held.astype(jnp.bfloat16)
        states_ref[0, head, :width, :width] = held_low
        mixed = dot_nn(scores, value) + start_wide * dot_nn(query, held_low)
        mixed = jnp.where(inside, mixed, 0.0)
        mean_square = jnp.sum(mixed * mixed, axis=1, keepdims=True) / head_size
        ratio = lax.rsqrt(jnp.maximum(mean_square, rms_floor))
        coded = jnp.where(mean_square > rms_floor, -ratio, jnp.where(mean_square == rms_floor, 2.0, 1.0))
        ratios = jnp.where(lane_at == head, coded, ratios)
        window = normed_ref[rows, start : start + width]
        normed_ref[rows, start : start + width] = jnp.where(inside, mixed * ratio, window)
        key_end = (jnp.where(inside, key, 0) * end_wide).astype(jnp.bfloat16)
        state[head, :width, :width] = held * whole[:, head : head + 1] + dot_tn(key_end, value)
    ratio_ref[...] = ratios

    def convolve(side):
        def tile(at, carry):
            lanes = pl.ds(pl.multiple_of(at * LANES, LANES), LANES)
            conv_ref[:, lanes] = conv_forward_tile(normed_ref[:, lanes], taps_ref[:, lanes], side).astype(conv_ref.dtype)
            return carry

        lax.fori_loop(0, features // LANES, tile, 0)

    finished = chunk_at == pl.num_programs(0) - 1

    @pl.when(jnp.logical_and(finished, single))
    def _():
        convolve(GRID)

    @pl.when(jnp.logical_and(finished, jnp.logical_not(single)))
    def _():
        convolve(GRID // 2)


def attention_forward(flag, proj, gate, bias, taps, heads):
    rows = proj.shape[0]
    features = taps.shape[1]
    head_size = features // heads
    chunks = rows // CHUNK
    whole_rows = lambda at: (0, 0)
    return pl.pallas_call(
        functools.partial(attention_forward_kernel, heads, head_size),
        grid=(chunks,),
        in_specs=[
            pl.BlockSpec(memory_space=pltpu.SMEM),
            pl.BlockSpec((CHUNK, 3 * features), lambda at: (at, 0)),
            pl.BlockSpec((CHUNK, LANES), lambda at: (at, 0)),
            pl.BlockSpec((1, LANES), whole_rows),
            pl.BlockSpec((9, features), whole_rows),
        ],
        out_specs=[
            pl.BlockSpec((rows, features), whole_rows),
            pl.BlockSpec((rows, features), whole_rows),
            pl.BlockSpec((CHUNK, LANES), lambda at: (at, 0)),
            pl.BlockSpec((1, heads, 2 * LANES, 2 * LANES), lambda at: (at, 0, 0, 0)),
        ],
        out_shape=[
            jax.ShapeDtypeStruct((rows, features), jnp.bfloat16),
            jax.ShapeDtypeStruct((rows, features), jnp.float32),
            jax.ShapeDtypeStruct((rows, LANES), jnp.float32),
            jax.ShapeDtypeStruct((chunks, heads, 2 * LANES, 2 * LANES), jnp.bfloat16),
        ],
        scratch_shapes=[pltpu.VMEM((heads, 2 * LANES, 2 * LANES), jnp.float32)],
        compiler_params=pltpu.CompilerParams(vmem_limit_bytes=VMEM_BYTES),
        cost_estimate=pl.CostEstimate(flops=int(17 * 10**9 * COST), bytes_accessed=int(20 * 10**6 * COST), transcendentals=0),
        name="attention_forward",
    )(flag, proj, gate, bias, taps)


def attention_backward_kernel(
    heads,
    head_size,
    flag_ref,
    proj_ref,
    gate_ref,
    bias_ref,
    taps_ref,
    normed_ref,
    ratio_ref,
    states_ref,
    grads_ref,
    dproj_ref,
    dgate_ref,
    dbias_ref,
    dtaps_ref,
    dnormed,
    dstate,
):
    step = pl.program_id(0)
    chunks = pl.num_programs(0)
    chunk_at = chunks - 1 - step
    chunk = proj_ref.shape[0]
    features = heads * head_size
    single = flag_ref[0] == 1

    def convolve(side):
        def tile(at, carry):
            lanes = pl.ds(pl.multiple_of(at * LANES, LANES), LANES)
            result, tap_rows = conv_backward_tile(
                normed_ref[:, lanes], grads_ref[:, lanes], taps_ref[:, lanes], side
            )
            dnormed[:, lanes] = result
            for row, tap_row in enumerate(tap_rows):
                dtaps_ref[row : row + 1, lanes] = tap_row
            return carry

        lax.fori_loop(0, features // LANES, tile, 0)

    @pl.when(jnp.logical_and(step == 0, single))
    def _():
        convolve(GRID)

    @pl.when(jnp.logical_and(step == 0, jnp.logical_not(single)))
    def _():
        convolve(GRID // 2)

    @pl.when(step == 0)
    def _():
        dbias_ref[...] = jnp.zeros_like(dbias_ref)

    @pl.when(jnp.logical_or(step == 0, jnp.logical_not(single)))
    def _():
        dstate[...] = jnp.zeros_like(dstate)

    gate = gate_ref[...]
    bias = bias_ref[...]
    cumul = decay_sums(gate, bias, chunk)
    cumul_t = jnp.transpose(cumul)
    scaled = cumul + math.log(head_size ** (-0.5))
    last = cumul[chunk - 1 : chunk, :]
    last_scaled = scaled[chunk - 1 : chunk, :]
    whole = jnp.exp(last)
    row_at = lax.broadcasted_iota(jnp.int32, (chunk, chunk), 0)
    col_at = lax.broadcasted_iota(jnp.int32, (chunk, chunk), 1)
    causal = row_at >= col_at
    lane_at = lax.broadcasted_iota(jnp.int32, (1, LANES), 1)
    rows = pl.ds(pl.multiple_of(chunk_at * chunk, chunk), chunk)
    balance = jnp.zeros((chunk, LANES), jnp.float32)
    through = jnp.zeros((1, LANES), jnp.float32)
    for head in range(heads):
        start, width, offset = head_window(head, head_size)
        inside = lane_mask(width, offset, head_size)
        query = jnp.where(inside, proj_ref[:, start : start + width], 0)
        key = proj_ref[:, features + start : features + start + width]
        key_in = jnp.where(inside, key, 0)
        value = proj_ref[:, 2 * features + start : 2 * features + start + width]
        value_in = jnp.where(inside, value, 0)
        scaled_wide = jnp.broadcast_to(scaled[:, head : head + 1], (chunk, LANES))
        start_col = jnp.exp(scaled_wide)
        end_col = jnp.exp(last_scaled[:, head : head + 1] - scaled_wide)
        start_col = jnp.concatenate([start_col] * (width // LANES), axis=1)
        end_col = jnp.concatenate([end_col] * (width // LANES), axis=1)
        coded = jnp.broadcast_to(ratio_ref[:, head : head + 1], (chunk, LANES))
        ratio = jnp.where(coded < 0.0, -coded, 1.0)
        ratio = jnp.concatenate([ratio] * (width // LANES), axis=1)
        slope = jnp.where(coded < 0.0, 1.0, jnp.where(coded > 1.5, 0.5, 0.0)) / head_size
        slope = jnp.concatenate([slope] * (width // LANES), axis=1)
        normed = jnp.where(inside, normed_ref[rows, start : start + width], 0.0)
        dnorm = jnp.where(inside, dnormed[rows, start : start + width], 0.0)
        along = jnp.sum(dnorm * normed, axis=1, keepdims=True) * slope
        dmixed = (dnorm - normed * along) * ratio
        dmixed_start = (dmixed * start_col).astype(jnp.bfloat16)
        dmixed = dmixed.astype(jnp.bfloat16)
        spread = jnp.concatenate([scaled_wide] * (chunk // LANES), axis=1) - cumul_t[head : head + 1, :]
        weights = jnp.exp(jnp.where(causal, spread, masked_log))
        scores = (dot_nt(query, key) * weights).astype(jnp.bfloat16)
        dscores = (dot_nt(dmixed, value) * weights).astype(jnp.bfloat16)
        held = states_ref[0, head, :width, :width]
        dnext = dstate[head, :width, :width]
        dnext_low = dnext.astype(jnp.bfloat16)
        dquery = dot_nn(dscores, key) + dot_nt(dmixed_start, held)
        dkey_inside = dot_tn(dscores, query)
        dkey_after = end_col * dot_nt(value_in, dnext_low)
        dkey = dkey_inside + dkey_after
        dvalue = dot_tn(scores, dmixed) + end_col * dot_nn(key_in, dnext_low)
        dstate[head, :width, :width] = dnext * whole[:, head : head + 1] + dot_tn(query, dmixed_start)
        kept = jnp.sum(dnext * held, axis=0, keepdims=True) * whole[:, head : head + 1]
        term = jnp.sum(kept + jnp.sum(key_in * dkey_after, axis=0, keepdims=True), axis=1, keepdims=True)
        through = jnp.where(lane_at == head, term, through)
        balance_one = jnp.sum(query * dquery - key_in * dkey, axis=1, keepdims=True)
        balance = jnp.where(lane_at == head, balance_one, balance)
        for place, grad in ((0, dquery), (1, dkey), (2, dvalue)):
            columns = slice(place * features + start, place * features + start + width)
            dproj_ref[:, columns] = jnp.where(inside, grad.astype(dproj_ref.dtype), dproj_ref[:, columns])
    upper = jnp.where(row_at <= col_at, 1.0, 0.0)
    ddecay = dot_nn(upper, balance, highest) + through
    dgate = ddecay / (1.0 + jnp.exp(gate + bias)) / normalizer
    dgate_ref[...] = dgate
    dbias_ref[...] += jnp.sum(dgate, axis=0, keepdims=True)


def attention_backward(flag, proj, gate, bias, taps, normed, ratios, states, grads, heads):
    rows = proj.shape[0]
    features = taps.shape[1]
    head_size = features // heads
    chunks = rows // CHUNK
    whole_rows = lambda at: (0, 0)
    back = lambda at: (chunks - 1 - at, 0)
    return pl.pallas_call(
        functools.partial(attention_backward_kernel, heads, head_size),
        grid=(chunks,),
        in_specs=[
            pl.BlockSpec(memory_space=pltpu.SMEM),
            pl.BlockSpec((CHUNK, 3 * features), back),
            pl.BlockSpec((CHUNK, LANES), back),
            pl.BlockSpec((1, LANES), whole_rows),
            pl.BlockSpec((9, features), whole_rows),
            pl.BlockSpec((rows, features), whole_rows),
            pl.BlockSpec((CHUNK, LANES), back),
            pl.BlockSpec((1, heads, 2 * LANES, 2 * LANES), lambda at: (chunks - 1 - at, 0, 0, 0)),
            pl.BlockSpec((rows, features), whole_rows),
        ],
        out_specs=[
            pl.BlockSpec((CHUNK, 3 * features), back),
            pl.BlockSpec((CHUNK, LANES), back),
            pl.BlockSpec((1, LANES), whole_rows),
            pl.BlockSpec((9, features), whole_rows),
        ],
        out_shape=[
            jax.ShapeDtypeStruct((rows, 3 * features), jnp.bfloat16),
            jax.ShapeDtypeStruct((rows, LANES), jnp.float32),
            jax.ShapeDtypeStruct((1, LANES), jnp.float32),
            jax.ShapeDtypeStruct((9, features), jnp.float32),
        ],
        scratch_shapes=[
            pltpu.VMEM((rows, features), jnp.float32),
            pltpu.VMEM((heads, 2 * LANES, 2 * LANES), jnp.float32),
        ],
        compiler_params=pltpu.CompilerParams(vmem_limit_bytes=VMEM_BYTES),
        cost_estimate=pl.CostEstimate(flops=int(38 * 10**9 * COST), bytes_accessed=int(40 * 10**6 * COST), transcendentals=0),
        name="attention_backward",
    )(flag, proj, gate, bias, taps, normed, ratios, states, grads)


def parts_of(fsdp_size, dp_size):
    return fsdp_size // 2, math.isqrt(dp_size)


def mesh_parts():
    return parts_of(lax.axis_size("fsdp"), lax.axis_size("dp"))


def send(values, move):
    chips, side = mesh_parts()
    pairs = []
    for z in range(chips):
        for core in range(2):
            for u in range(side):
                for v in range(side):
                    to_z, to_core, to_u, to_v = move(z, core, u, v)
                    pairs.append(
                        (
                            ((z * 2 + core) * side + u) * side + v,
                            ((to_z * 2 + to_core) * side + to_u) * side + to_v,
                        )
                    )
    return lax.ppermute(values, ("fsdp", "dp"), pairs)


def along_z(shift):
    chips = mesh_parts()[0]
    return lambda z, core, u, v: ((z + shift) % chips, core, u, v)


def across_core(z, core, u, v):
    return z, 1 - core, u, v


def along_first(shift):
    side = mesh_parts()[1]

    def move(z, core, u, v):
        return (z, core, (u + shift) % side, v) if core == 0 else (z, core, u, (v + shift) % side)

    return move


def along_second(shift):
    side = mesh_parts()[1]

    def move(z, core, u, v):
        return (z, core, u, (v + shift) % side) if core == 0 else (z, core, (u + shift) % side, v)

    return move


def along_dp(shift):
    side = mesh_parts()[1]

    def move(z, core, u, v):
        to = (u * side + v + shift) % (side * side)
        return z, core, to // side, to % side

    return move


def far_pieces(shard):
    chips = mesh_parts()[0]
    return [shard] + [send(shard, along_z(shift)) for shift in range(1, chips)]


def first_pieces(stack):
    side = mesh_parts()[1]
    return [stack] + [send(stack, along_first(shift)) for shift in range(1, side)]


def second_pieces(level):
    side = mesh_parts()[1]
    own = []
    for piece in level:
        own += [piece] + [send(piece, along_second(shift)) for shift in range(1, side)]
    return own


def core_pieces(own):
    return own + [send(piece, across_core) for piece in own]


def gather_shard(shard):
    return core_pieces(second_pieces(first_pieces(jnp.stack(far_pieces(shard)))))


def add_low(*values):
    total = values[0].astype(jnp.float32)
    for value in values[1:]:
        total = total + value.astype(jnp.float32)
    return total


def cross_sum(joint):
    return send(joint, across_core)


def first_send(parts, other):
    side = mesh_parts()[1]
    sent = [add_low(parts[shift], other[shift]).astype(jnp.bfloat16) for shift in range(1, side)]
    return [send(value, along_first(shift + 1)) for shift, value in enumerate(sent)]


def first_add(parts, other, received):
    side = mesh_parts()[1]
    return [
        add_low(parts[0][second], other[0, second], *[value[second] for value in received]).astype(jnp.bfloat16)
        for second in range(side)
    ]


def second_send(level):
    side = mesh_parts()[1]
    return [send(level[shift], along_second(shift)) for shift in range(1, side)]


def second_add(level, received):
    chips = mesh_parts()[0]
    return [
        add_low(level[0][far], *[value[far] for value in received]).astype(jnp.bfloat16)
        for far in range(chips)
    ]


def far_send(level):
    chips = mesh_parts()[0]
    return [send(level[shift], along_z(shift)) for shift in range(1, chips)]


def far_add(level, received):
    return add_low(level[0], *received)


def tied(*values):
    return lax.optimization_barrier(values)


def fold_of(shape, columns):
    return columns if shape[0] % (16 * columns) == 0 else 1


def folded(values, fold):
    height = values.shape[0] // fold
    return jnp.concatenate([values[at * height : (at + 1) * height] for at in range(fold)], axis=1)


def flip_bit(values, bit):
    chips, side = mesh_parts()

    def move(z, core, u, v):
        to = (((z * 2 + core) * side + u) * side + v) ^ bit
        return to // (2 * side * side), to // (side * side) % 2, to // side % side, to % side

    return send(values, move)


def flip_bits(low, high):
    bits = []
    while low < high:
        bits.append(low)
        low *= 2
    return bits


def source_place(where, sibling, first, second, far, chips, side):
    core = 1 - where[CORE_AT] if sibling else where[CORE_AT]
    from_u = lax.rem(where[U_AT] - jnp.where(core == 0, first, second) + side, side)
    from_v = lax.rem(where[V_AT] - jnp.where(core == 0, second, first) + side, side)
    from_z = lax.rem(where[Z_AT] - far + chips, chips)
    return 2 * from_z + core, from_u * side + from_v


def weight_copies(where, pieces, target, sems, chips, side):
    copies = []
    rows = pieces[0].shape[1]
    for at, piece in enumerate(pieces):
        sibling, first, second = at // (side * side), at // side % side, at % side
        for far in range(chips):
            block, column = source_place(where, sibling, first, second, far, chips, side)
            copies.append(
                pltpu.make_async_copy(
                    piece.at[far],
                    target.at[column, pl.ds(pl.multiple_of(block * rows, 8), rows)],
                    sems.at[at * chips + far],
                )
            )
    return copies


def whole_copies(gathered, target, sems):
    rows = gathered.shape[1]
    columns = target.shape[0]
    return [
        pltpu.make_async_copy(
            gathered.at[at], target.at[at % columns, pl.ds(at // columns * rows, rows)], sems.at[at]
        )
        for at in range(gathered.shape[0])
    ]


def normalize(values):
    centred = values - jnp.mean(values, axis=1, keepdims=True)
    scale = lax.rsqrt(jnp.mean(centred * centred, axis=1, keepdims=True) + ln_eps)
    return centred * scale, scale


def normalize_back(grads, unit, scale):
    return scale * (
        grads - jnp.mean(grads, axis=1, keepdims=True) - unit * jnp.mean(grads * unit, axis=1, keepdims=True)
    )


def front_kernel(chips, side, where, tokens_ref, mod_ref, *rest):
    pieces, rest = rest[: 2 * side * side], rest[2 * side * side :]
    proj_ref, gate_ref, normed_t_ref, weight, sems = rest
    columns = side * side
    wide = proj_ref.shape[1] // columns
    narrow = weight.shape[2] - wide
    copies = weight_copies(where, pieces, weight, sems, chips, side)

    @pl.when(pl.program_id(0) == 0)
    def _():
        for copy in copies:
            copy.start()

    unit, ignored = normalize(tokens_ref[...].astype(jnp.float32))
    normed = (unit * (1.0 + mod_ref[0, 1:2, :]) + mod_ref[0, 0:1, :]).astype(jnp.bfloat16)
    normed_t_ref[...] = jnp.transpose(normed)

    @pl.when(pl.program_id(0) == 0)
    def _():
        for copy in copies:
            copy.wait()

    gate_ref[...] = jnp.zeros_like(gate_ref)
    for column in range(columns):
        product = dot_nn(normed, weight[column])
        proj_ref[:, column * wide : (column + 1) * wide] = product[:, :wide].astype(jnp.bfloat16)
        gate_ref[:, column * narrow : (column + 1) * narrow] = product[:, wide:]


def rows_spec(block, width):
    return pl.BlockSpec((block, width), lambda at, where: (at, 0))


def across_spec(height, block):
    return pl.BlockSpec((height, block), lambda at, where: (0, at))


def mod_spec(features, steps=4):
    share = steps // QUARTERS
    return pl.BlockSpec(
        (1, 8, features), lambda at, where: (jnp.where(where[FLAG_AT] == 1, 0, at // share), 0, 0)
    )


def any_specs(count):
    return [pl.BlockSpec(memory_space=pl.ANY)] * count


def shaped(shape, dtype):
    return jax.ShapeDtypeStruct(shape, dtype)


def call(kernel, where, args, grid, in_specs, out_specs, out_shape, scratch, name, flops, moved):
    return pl.pallas_call(
        kernel,
        grid_spec=pltpu.PrefetchScalarGridSpec(
            num_scalar_prefetch=1, grid=grid, in_specs=in_specs, out_specs=out_specs, scratch_shapes=scratch
        ),
        out_shape=out_shape,
        compiler_params=pltpu.CompilerParams(vmem_limit_bytes=VMEM_BYTES),
        cost_estimate=pl.CostEstimate(flops=int(flops * COST), bytes_accessed=int(moved * COST), transcendentals=0),
        name=name,
    )(where, *args)


def front_forward(where, tokens, mod, pieces, wide):
    chips, side = mesh_parts()
    rows, features = tokens.shape
    block = rows // QUARTERS
    columns = side * side
    depth, width = pieces[0].shape[1:]
    return call(
        functools.partial(front_kernel, chips, side),
        where,
        (tokens, mod, *pieces),
        (QUARTERS,),
        [rows_spec(block, features), mod_spec(features)] + any_specs(len(pieces)),
        [rows_spec(block, columns * wide), rows_spec(block, LANES), across_spec(features, block)],
        [
            shaped((rows, columns * wide), jnp.bfloat16),
            shaped((rows, LANES), jnp.float32),
            shaped((features, rows), jnp.bfloat16),
        ],
        [
            pltpu.VMEM((columns, features, width), jnp.bfloat16),
            pltpu.SemaphoreType.DMA((len(pieces) * chips,)),
        ],
        "front_forward",
        2 * rows * features * columns * width,
        20 * 10**6,
    )


def gelu_parts(values):
    square = values * values
    bent = jnp.tanh(values * (gelu_scale + (0.044715 * gelu_scale) * square))
    half = 0.5 + 0.5 * bent
    rise = values * (gelu_scale + (3 * 0.044715 * gelu_scale) * square)
    return values * half, half + half * (1.0 - bent) * rise


def middle_kernel(chips, side, where, conv_ref, tokens_ref, cot_ref, mod_ref, bias_ref, gathered, *rest):
    (
        attended_ref,
        hidden_ref,
        slope_ref,
        normed_t_ref,
        conv_t_ref,
        gradred_ref,
        weight,
        sems,
    ) = rest
    columns = side * side
    wide = hidden_ref.shape[1] // columns
    narrow = weight.shape[2] - wide
    copies = whole_copies(gathered, weight, sems)

    @pl.when(pl.program_id(0) == 0)
    def _():
        for copy in copies:
            copy.start()

    conv = conv_ref[...]
    conv_t_ref[...] = jnp.transpose(conv)
    gradred_ref[...] = (cot_ref[...].astype(jnp.float32) * mod_ref[0, 5:6, :]).astype(jnp.bfloat16)

    @pl.when(pl.program_id(0) == 0)
    def _():
        for copy in copies:
            copy.wait()

    for column in range(columns):
        attended_ref[:, column * narrow : (column + 1) * narrow] = dot_nn(conv, weight[column, :, wide:])
    after = tokens_ref[...].astype(jnp.float32) + mod_ref[0, 2:3, :] * attended_ref[...]
    unit, ignored = normalize(after)
    normed = (unit * (1.0 + mod_ref[0, 4:5, :]) + mod_ref[0, 3:4, :]).astype(jnp.bfloat16)
    normed_t_ref[...] = jnp.transpose(normed)
    for column in range(columns):
        span = slice(column * wide, (column + 1) * wide)
        preact = dot_nn(normed, weight[column, :, :wide]) + bias_ref[:, span]
        hidden, slope = gelu_parts(preact)
        low = hidden.astype(jnp.bfloat16)
        hidden_ref[:, span] = low
        slope_ref[:, span] = slope.astype(jnp.bfloat16)


def middle_forward(where, conv, tokens, cotangent, mod, bias, gathered, wide):
    chips, side = mesh_parts()
    rows, features = tokens.shape
    block = rows // QUARTERS
    columns = side * side
    width = gathered.shape[2]
    hidden = columns * wide
    return call(
        functools.partial(middle_kernel, chips, side),
        where,
        (conv, tokens, cotangent, mod, bias, gathered),
        (QUARTERS,),
        [
            rows_spec(block, features),
            rows_spec(block, features),
            rows_spec(block, features),
            mod_spec(features),
            pl.BlockSpec((1, hidden), lambda at, where: (0, 0)),
        ]
        + any_specs(1),
        [
            rows_spec(block, features),
            rows_spec(block, hidden),
            rows_spec(block, hidden),
            across_spec(features, block),
            across_spec(features, block),
            rows_spec(block, features),
        ],
        [
            shaped((rows, features), jnp.float32),
            shaped((rows, hidden), jnp.bfloat16),
            shaped((rows, hidden), jnp.bfloat16),
            shaped((features, rows), jnp.bfloat16),
            shaped((features, rows), jnp.bfloat16),
            shaped((rows, features), jnp.bfloat16),
        ],
        [
            pltpu.VMEM((columns, features, width), jnp.bfloat16),
            pltpu.SemaphoreType.DMA((gathered.shape[0],)),
        ],
        "middle_forward",
        2 * rows * features * columns * width,
        60 * 10**6,
    )


def middle_back_kernel(
    chips, side, where, hidden_ref, slope_ref, attended_ref, tokens_ref, cot_ref, mod_ref, *rest
):
    gathered, reduce_pieces, rest = rest[0], rest[1], rest[2:]
    (
        out_ref,
        gradpre_ref,
        gradafter_ref,
        gradatt_ref,
        gradconv_ref,
        sums_ref,
        biassum_ref,
        weight,
        reduce_weight,
        stage,
        sems,
        reduce_sems,
    ) = rest
    columns = side * side
    hidden = hidden_ref.shape[1]
    wide = hidden // columns
    narrow = weight.shape[2] - wide
    height = reduce_pieces.shape[1]
    fold = reduce_pieces.shape[2] // narrow
    copies = whole_copies(gathered, weight, sems)

    @pl.when(pl.program_id(0) == 0)
    def _():
        biassum_ref[...] = jnp.zeros_like(biassum_ref)

        def staged(block):
            slot = block % 2
            return [
                pltpu.make_async_copy(
                    reduce_pieces.at[block * columns + column],
                    stage.at[slot, column],
                    reduce_sems.at[slot, column],
                )
                for column in range(columns)
            ]

        turns = [staged(block) for block in range(2 * chips)]
        for copy in turns[0]:
            copy.start()
        for block, found in enumerate(turns):
            if block + 1 < len(turns):
                for copy in turns[block + 1]:
                    copy.start()
            if block == 0:
                for copy in copies:
                    copy.start()
            for copy in found:
                copy.wait()
            for at in range(fold):
                target = slice((block * fold + at) * height, (block * fold + at + 1) * height)
                for column in range(columns):
                    reduce_weight[target, column * narrow : (column + 1) * narrow] = stage[
                        block % 2, column, :, at * narrow : (at + 1) * narrow
                    ]

    cot = cot_ref[...].astype(jnp.float32)
    attended = attended_ref[...]
    after = tokens_ref[...].astype(jnp.float32) + mod_ref[0, 2:3, :] * attended
    reduced = dot_nn(hidden_ref[...], reduce_weight[...])
    sums_ref[...] = jnp.zeros_like(sums_ref)
    sums_ref[0, 3:4, :] = jnp.sum(cot * reduced, axis=0, keepdims=True)
    out_ref[...] = (after + mod_ref[0, 5:6, :] * reduced).astype(out_ref.dtype)
    gradred = (cot * mod_ref[0, 5:6, :]).astype(jnp.bfloat16)

    @pl.when(pl.program_id(0) == 0)
    def _():
        for copy in copies:
            copy.wait()

    gradmid = jnp.zeros(after.shape, jnp.float32)
    for column in range(columns):
        span = slice(column * wide, (column + 1) * wide)
        gradact = dot_nt(gradred, reduce_weight[span, :])
        gradpre = (gradact * slope_ref[:, span].astype(jnp.float32)).astype(jnp.bfloat16)
        gradpre_ref[:, span] = gradpre
        biassum_ref[:, span] += jnp.sum(gradpre.astype(jnp.float32), axis=0, keepdims=True)
        gradmid = gradmid + dot_nt(gradpre, weight[column, :, :wide])
    unit, scale = normalize(after)
    sums_ref[0, 1:2, :] = jnp.sum(gradmid, axis=0, keepdims=True)
    sums_ref[0, 2:3, :] = jnp.sum(gradmid * unit, axis=0, keepdims=True)
    gradafter = cot + normalize_back(gradmid * (1.0 + mod_ref[0, 4:5, :]), unit, scale)
    gradafter_ref[...] = gradafter
    sums_ref[0, 0:1, :] = jnp.sum(gradafter * attended, axis=0, keepdims=True)
    gradatt_ref[...] = (gradafter * mod_ref[0, 2:3, :]).astype(jnp.bfloat16)
    gradconv = jnp.zeros(after.shape, jnp.float32)
    for column in range(columns):
        gradconv = gradconv + dot_nt(
            gradatt_ref[:, column * narrow : (column + 1) * narrow], weight[column, :, wide:]
        )
    gradconv_ref[...] = gradconv


def middle_backward(where, hidden, slope, attended, tokens, cotangent, mod, gathered, reduce_pieces):
    chips, side = mesh_parts()
    rows, features = tokens.shape
    steps = QUARTERS if side * side <= 4 else 2 * QUARTERS
    block = rows // steps
    columns = side * side
    inner = hidden.shape[1]
    width = gathered.shape[2]
    depth, narrow = reduce_pieces.shape[1:]
    return call(
        functools.partial(middle_back_kernel, chips, side),
        where,
        (hidden, slope, attended, tokens, cotangent, mod, gathered, reduce_pieces),
        (steps,),
        [
            rows_spec(block, inner),
            rows_spec(block, inner),
            rows_spec(block, features),
            rows_spec(block, features),
            rows_spec(block, features),
            mod_spec(features, steps),
        ]
        + any_specs(2),
        [
            rows_spec(block, features),
            rows_spec(block, inner),
            rows_spec(block, features),
            rows_spec(block, features),
            rows_spec(block, features),
            pl.BlockSpec((1, 8, features), lambda at, where: (at, 0, 0)),
            pl.BlockSpec((1, inner), lambda at, where: (0, 0)),
        ],
        [
            shaped((rows, features), jnp.bfloat16),
            shaped((rows, inner), jnp.bfloat16),
            shaped((rows, features), jnp.float32),
            shaped((rows, features), jnp.bfloat16),
            shaped((rows, features), jnp.float32),
            shaped((steps, 8, features), jnp.float32),
            shaped((1, inner), jnp.float32),
        ],
        [
            pltpu.VMEM((columns, features, width), jnp.bfloat16),
            pltpu.VMEM((inner, features), jnp.bfloat16),
            pltpu.VMEM((2, columns, depth, narrow), jnp.bfloat16),
            pltpu.SemaphoreType.DMA((gathered.shape[0],)),
            pltpu.SemaphoreType.DMA((2, columns)),
        ],
        "middle_backward",
        6 * rows * features * inner,
        80 * 10**6,
    )


def front_back_kernel(
    chips, side, where, gradproj_ref, gradgate_ref, gradafter_ref, tokens_ref, mod_ref, *rest
):
    pieces, rest = rest[: 2 * side * side], rest[2 * side * side :]
    out_ref, sums_ref, weight, both, sems = rest
    columns = side * side
    wide = gradproj_ref.shape[1] // columns
    narrow = weight.shape[2] - wide
    copies = weight_copies(where, pieces, weight, sems, chips, side)

    @pl.when(pl.program_id(0) == 0)
    def _():
        for copy in copies:
            copy.start()

    unit, scale = normalize(tokens_ref[...].astype(jnp.float32))

    @pl.when(pl.program_id(0) == 0)
    def _():
        for copy in copies:
            copy.wait()

    gradin = jnp.zeros(unit.shape, jnp.float32)
    for column in range(columns):
        both[:, :wide] = gradproj_ref[:, column * wide : (column + 1) * wide]
        both[:, wide:] = gradgate_ref[:, column * narrow : (column + 1) * narrow].astype(jnp.bfloat16)
        gradin = gradin + dot_nt(both[...], weight[column])
    sums_ref[...] = jnp.zeros_like(sums_ref)
    sums_ref[0, 0:1, :] = jnp.sum(gradin, axis=0, keepdims=True)
    sums_ref[0, 1:2, :] = jnp.sum(gradin * unit, axis=0, keepdims=True)
    out_ref[...] = (
        gradafter_ref[...] + normalize_back(gradin * (1.0 + mod_ref[0, 1:2, :]), unit, scale)
    ).astype(out_ref.dtype)


def front_backward(where, gradproj, gradgate, gradafter, tokens, mod, pieces):
    chips, side = mesh_parts()
    rows, features = tokens.shape
    block = rows // QUARTERS
    columns = side * side
    width = pieces[0].shape[2]
    return call(
        functools.partial(front_back_kernel, chips, side),
        where,
        (gradproj, gradgate, gradafter, tokens, mod, *pieces),
        (QUARTERS,),
        [
            rows_spec(block, gradproj.shape[1]),
            rows_spec(block, LANES),
            rows_spec(block, features),
            rows_spec(block, features),
            mod_spec(features),
        ]
        + any_specs(len(pieces)),
        [rows_spec(block, features), pl.BlockSpec((1, 8, features), lambda at, where: (at, 0, 0))],
        [shaped((rows, features), jnp.bfloat16), shaped((QUARTERS, 8, features), jnp.float32)],
        [
            pltpu.VMEM((columns, features, width), jnp.bfloat16),
            pltpu.VMEM((block, width), jnp.bfloat16),
            pltpu.SemaphoreType.DMA((len(pieces) * chips,)),
        ],
        "front_backward",
        2 * rows * features * columns * width,
        25 * 10**6,
    )


def target_block(where, sibling, far, chips):
    core = 1 - where[CORE_AT] if sibling else where[CORE_AT]
    return 2 * lax.rem(where[Z_AT] + far, chips) + core


def target_column(where, first, second, side):
    core = where[CORE_AT]
    to_u = lax.rem(where[U_AT] + jnp.where(core == 0, first, second), side)
    to_v = lax.rem(where[V_AT] + jnp.where(core == 0, second, first), side)
    return to_u * side + to_v


def relative_column(where, column, side):
    core = where[CORE_AT]
    by_u = lax.rem(column // side - where[U_AT] + side, side)
    by_v = lax.rem(column % side - where[V_AT] + side, side)
    return jnp.where(core == 0, by_u, by_v), jnp.where(core == 0, by_v, by_u)


def grads_product(left, right, chips):
    product = dot_nn(left, right)
    return product.reshape(chips, product.shape[0] // chips, product.shape[1]).astype(jnp.bfloat16)


def stack_lefts(lefts, left_all):
    depth = lefts[0].shape[0]
    for at, left in enumerate(lefts):
        left_all[at * depth : (at + 1) * depth, :] = left[...]


def grads_by_column_kernel(side, chips, where, *rest):
    lefts, right_ref, other, rest = rest[: 2 * chips], rest[2 * chips], rest[2 * chips + 1], rest[2 * chips + 2 :]
    outs, left_all = rest[:side], rest[side]
    half = left_all.shape[0] // 2

    @pl.when(pl.program_id(0) == 0)
    def _():
        stack_lefts(lefts, left_all)

    other[0, 0] = grads_product(left_all[half:, :], right_ref[...], chips)
    for first in range(side):

        @pl.when(pl.program_id(0) // side == first)
        def _(first=first):
            outs[first][0] = grads_product(left_all[:half, :], right_ref[...], chips)


def grads_joint_kernel(blocks, aligned, where, left_ref, small_left_ref, right_ref, small_right_ref, out, *scratch):
    small = scratch[0]
    wide = scratch[1].shape[1] if not aligned else right_ref.shape[1]
    narrow = small.shape[1]
    count = small_right_ref.shape[1] // narrow
    for column in range(count):

        @pl.when(pl.program_id(0) == column)
        def _(column=column):
            small[...] = small_right_ref[:, column * narrow : (column + 1) * narrow]
            if not aligned:
                scratch[1][...] = right_ref[:, column * wide : (column + 1) * wide]

    right = right_ref if aligned else scratch[1]
    out[:, 0, :, :wide] = grads_product(left_ref[...], right[...], blocks)
    out[:, 0, :, wide:] = grads_product(small_left_ref[...], small[...], blocks)


def grads_joint(where, left_t, right, small_left_t, small_right):
    chips, side = mesh_parts()
    columns, blocks = side * side, 2 * chips
    height, rows = left_t.shape
    depth = height // blocks
    wide, narrow = right.shape[1] // columns, small_right.shape[1] // columns
    aligned = wide % LANES == 0
    fixed = lambda at, where: (0, 0)
    scratch = [pltpu.VMEM((rows, narrow), jnp.bfloat16)]
    if not aligned:
        scratch.append(pltpu.VMEM((rows, wide), jnp.bfloat16))
    found = call(
        functools.partial(grads_joint_kernel, blocks, aligned),
        where,
        (left_t, small_left_t, right, small_right),
        (columns,),
        [
            pl.BlockSpec(left_t.shape, fixed),
            pl.BlockSpec(small_left_t.shape, fixed),
            pl.BlockSpec((rows, wide), lambda at, where: (0, at)) if aligned else pl.BlockSpec(right.shape, fixed),
            pl.BlockSpec(small_right.shape, fixed),
        ],
        pl.BlockSpec((blocks, 1, depth, wide + narrow), lambda at, where: (0, at, 0, 0)),
        shaped((blocks, columns, depth, wide + narrow), jnp.bfloat16),
        scratch,
        "grads_joint",
        2 * rows * height * columns * (wide + narrow),
        30 * 10**6,
    )
    return found.reshape(blocks * columns, depth, wide + narrow)


def grads_by_row_kernel(side, chips, extra, where, *rest):
    lefts, right_ref, rest = rest[: 2 * chips], rest[2 * chips], rest[2 * chips + 1 :]
    if extra:
        extra_ref, rest = rest[0], rest[1:]
    other, outs, left_all, both = rest[0], rest[1 : 1 + side], rest[1 + side], rest[2 + side]
    columns = side * side
    wide = right_ref.shape[1] // columns
    narrow = both.shape[1] - wide
    half = left_all.shape[0] // 2
    stack_lefts(lefts, left_all)
    for column in range(columns):
        by_first, by_second = relative_column(where, column, side)
        both[:, :wide] = right_ref[:, column * wide : (column + 1) * wide]
        if extra:
            both[:, wide:] = extra_ref[:, column * narrow : (column + 1) * narrow].astype(jnp.bfloat16)
        other[by_second, by_first] = grads_product(left_all[half:, :], both[...], chips)
        for first in range(side):

            @pl.when(by_first == first)
            def _(first=first, by_second=by_second):
                outs[first][by_second] = grads_product(left_all[:half, :], both[...], chips)


def grads_across_kernel(side, chips, where, right_ref, hidden_ref, other, *rest):
    outs, right_t, product = rest[:side], rest[side], rest[side + 1]
    columns = side * side
    wide = right_ref.shape[1] // columns
    depth = hidden_ref.shape[1] // 2

    @pl.when(pl.program_id(0) == 0)
    def _():
        right_t[...] = jnp.transpose(right_ref[...])

    product[...] = dot_nn(right_t[...], hidden_ref[...]).astype(jnp.bfloat16)
    for core in range(2):
        mine = slice(core * depth, (core + 1) * depth)
        theirs = slice((1 - core) * depth, (2 - core) * depth)
        for column in range(columns):
            by_first, by_second = relative_column(where, column, side)
            span = slice(column * wide, (column + 1) * wide)

            @pl.when(where[CORE_AT] == core)
            def _(span=span, theirs=theirs, by_first=by_first, by_second=by_second):
                other[by_second, by_first, 0] = product[span, theirs]

            for first in range(side):

                @pl.when(jnp.logical_and(where[CORE_AT] == core, by_first == first))
                def _(first=first, span=span, mine=mine, by_second=by_second):
                    outs[first][by_second, 0] = product[span, mine]


def piece_shapes(side, chips, piece):
    other = shaped((side, side, chips, *piece), jnp.bfloat16)
    return [other] + [shaped((side, chips, *piece), jnp.bfloat16)] * side


def grads_across(where, hidden, right):
    chips, side = mesh_parts()
    columns = side * side
    rows, inner = hidden.shape
    depth, wide = inner // (2 * chips), right.shape[1] // columns
    piece = (wide, depth)
    found = call(
        functools.partial(grads_across_kernel, side, chips),
        where,
        (right, hidden),
        (chips,),
        [
            pl.BlockSpec(right.shape, lambda at, where: (0, 0)),
            pl.BlockSpec((rows, 2 * depth), lambda at, where: (0, lax.rem(where[Z_AT] + at, chips))),
        ],
        [pl.BlockSpec((side, side, 1, *piece), lambda at, where: (0, 0, at, 0, 0))]
        + [pl.BlockSpec((side, 1, *piece), lambda at, where: (0, at, 0, 0))] * side,
        piece_shapes(side, chips, piece),
        [
            pltpu.VMEM((right.shape[1], rows), jnp.bfloat16),
            pltpu.VMEM((right.shape[1], 2 * depth), jnp.bfloat16),
        ],
        "grads_across",
        2 * rows * inner * right.shape[1],
        24 * 10**6,
    )
    return found[0], found[1:]


def weight_grads(where, left_t, right, extra=None, narrow=0):
    chips, side = mesh_parts()
    columns = side * side
    height, rows = left_t.shape
    depth = height // (2 * chips)
    wide = right.shape[1] // columns
    piece = (depth, wide + narrow)

    def left_spec(sibling, far):
        return pl.BlockSpec((depth, rows), lambda at, where: (target_block(where, sibling, far, chips), 0))

    specs = [left_spec(sibling, far) for sibling in (False, True) for far in range(chips)]
    args = [left_t] * (2 * chips) + [right]
    if wide % LANES == 0 and extra is None:
        steps = columns
        specs.append(
            pl.BlockSpec(
                (rows, wide), lambda at, where: (0, target_column(where, at // side, lax.rem(at, side), side))
            )
        )
        joint = pl.BlockSpec((1, 1, chips, *piece), lambda at, where: (lax.rem(at, side), at // side, 0, 0, 0))

        def out_spec(first):
            return pl.BlockSpec(
                (1, chips, *piece), lambda at, where: (jnp.clip(at - first * side, 0, side - 1), 0, 0, 0)
            )

        kernel = functools.partial(grads_by_column_kernel, side, chips)
        scratch = [pltpu.VMEM((height, rows), jnp.bfloat16)]
    else:
        steps = 1
        specs.append(pl.BlockSpec(right.shape, lambda at, where: (0, 0)))
        if extra is not None:
            specs.append(pl.BlockSpec(extra.shape, lambda at, where: (0, 0)))
            args.append(extra)
        joint = pl.BlockSpec((side, side, chips, *piece), lambda at, where: (0, 0, 0, 0, 0))

        def out_spec(first):
            return pl.BlockSpec((side, chips, *piece), lambda at, where: (0, 0, 0, 0))

        kernel = functools.partial(grads_by_row_kernel, side, chips, extra is not None)
        scratch = [pltpu.VMEM((height, rows), jnp.bfloat16), pltpu.VMEM((rows, wide + narrow), jnp.bfloat16)]
    found = call(
        kernel,
        where,
        args,
        (steps,),
        specs,
        [joint] + [out_spec(first) for first in range(side)],
        piece_shapes(side, chips, piece),
        scratch,
        "weight_grads",
        2 * rows * height * columns * wide,
        2 * (rows * height + rows * columns * wide + height * columns * wide),
    )
    return found[0], found[1:]


def pick(values, at):
    return lax.dynamic_index_in_dim(values, at, 0, keepdims=False)


def on_device(
    tokens,
    conditions,
    resolution,
    modulate_weight,
    modulate_bias,
    attend_weight,
    forget_weight,
    forget_bias,
    conv_taps,
    output_weight,
    expand_weight,
    expand_bias,
    reduce_weight,
    cotangent,
):
    chips, side = mesh_parts()
    columns = side * side
    blocks = 2 * chips
    fsdp_at = lax.axis_index("fsdp")
    dp_at = lax.axis_index("dp")
    z_at, core_at, u_at, v_at = fsdp_at // 2, fsdp_at % 2, dp_at // side, dp_at % side
    where = jnp.stack([z_at, core_at, u_at, v_at, resolution[0]]).astype(jnp.int32)
    slots, features = conditions.shape
    heads = forget_bias.shape[0]
    own_rows, own_columns = modulate_weight.shape
    single = resolution[0] == 1

    attend_pieces = gather_shard(jnp.concatenate([attend_weight, forget_weight], axis=1))

    cond_values = conditions.astype(jnp.float32)
    silu_out, silu_back = jax.vjp(jax.nn.silu, cond_values)
    cond_low = silu_out.astype(jnp.bfloat16)
    small = jnp.concatenate([cond_low.reshape(-1), modulate_bias, expand_bias])
    small_size = small.shape[0]
    small = jnp.stack(gather_shard(small.reshape(1, small_size))).reshape(blocks * columns, small_size)
    order = []
    for block in range(blocks):
        for column in range(columns):
            sibling = jnp.abs(block % 2 - core_at)
            far = (z_at - block // 2) % chips
            by_u, by_v = (u_at - column // side) % side, (v_at - column % side) % side
            first = jnp.where(block % 2 == 0, by_u, by_v)
            second = jnp.where(block % 2 == 0, by_v, by_u)
            order.append(((sibling * side + first) * side + second) * chips + far)
    order = jnp.stack(order)
    chosen = (order[:, None] == jnp.arange(blocks * columns)[None, :]).astype(jnp.bfloat16)
    small = jnp.dot(chosen, small, preferred_element_type=jnp.float32)
    cond_all = small[:, : slots * features].astype(jnp.bfloat16).reshape(-1, features)
    modbias_whole = small[:, slots * features : small_size - expand_bias.shape[0]].reshape(-1)
    expandbias_whole = small[:, small_size - expand_bias.shape[0] :].reshape(1, -1)
    cond_columns = lax.dynamic_slice_in_dim(cond_all, fsdp_at * own_rows, own_rows, axis=1)
    partial = jnp.dot(cond_columns, modulate_weight, preferred_element_type=jnp.float32)
    partial = partial.reshape(chips, 2, columns * slots, own_columns)
    to_sibling = lax.dynamic_index_in_dim(partial, 1 - core_at, 1, keepdims=False)
    partial = lax.dynamic_index_in_dim(partial, core_at, 1, keepdims=False) + send(to_sibling, across_core)
    modulation = pick(partial, z_at)
    for shift in range(1, chips):
        modulation = modulation + send(pick(partial, (z_at + shift) % chips), along_z(shift))
    modulation = modulation.reshape(columns, slots, own_columns)
    pieces = [pick(modulation, dp_at)]
    for shift in range(1, columns):
        pieces.append(send(pick(modulation, (dp_at + shift) % columns), along_dp(shift)))
    pieces = jnp.stack(pieces)
    modulation = jnp.concatenate([pick(pieces, (dp_at - column) % columns) for column in range(columns)], axis=1)
    modulation = (modulation + modbias_whole[None, :]).reshape(slots, 6, features)
    modulation = jnp.pad(modulation, ((0, 0), (0, 2), (0, 0)))

    fold = fold_of(reduce_weight.shape, columns)
    middle_pieces = lax.all_gather(
        jnp.concatenate([expand_weight, output_weight], axis=1), ("fsdp", "dp"), axis=0, tiled=False
    )

    projected, gate_logit, normed_in_t = front_forward(
        where, tokens, modulation, attend_pieces, attend_weight.shape[1]
    )
    projected, reduce_shard = tied(projected, folded(reduce_weight, fold))
    reduce_pieces = lax.all_gather(reduce_shard, ("fsdp", "dp"), axis=0, tiled=False)
    bias_wide = jnp.pad(forget_bias[None, :], ((0, 0), (0, LANES - heads)))
    conv_low, normed_heads, ratios, states = attention_forward(
        resolution, projected, gate_logit, bias_wide, conv_taps, heads
    )
    attended, hidden, slope, normed_mid_t, conv_t, grad_reduced = middle_forward(
        where, conv_low, tokens, cotangent, modulation, expandbias_whole, middle_pieces, expand_weight.shape[1]
    )
    across = (2 * reduce_weight.shape[0]) % LANES == 0
    if across:
        reduce_other, reduce_parts = grads_across(where, hidden, grad_reduced)
    else:
        reduce_other, reduce_parts = weight_grads(where, hidden.T, grad_reduced)
    reduce_other = cross_sum(reduce_other)
    hidden, reduce_parts, reduce_other = tied(hidden, reduce_parts, reduce_other)
    moving = first_send(reduce_parts, reduce_other)
    back = middle_backward(
        where, hidden, slope, attended, tokens, cotangent, modulation, middle_pieces, reduce_pieces
    )
    back, moving = tied(back, moving)
    block_out, grad_preact, grad_after, grad_attended, grad_conv, middle_sums, bias_sums = back
    reduce_level = first_add(reduce_parts, reduce_other, moving)
    moving = second_send(reduce_level)
    joint = grads_joint(where, normed_mid_t, grad_preact, conv_t, grad_attended)
    joint, moving = tied(joint, moving)
    reduce_level = second_add(reduce_level, moving)
    joint = lax.psum_scatter(joint, ("fsdp", "dp"), scatter_dimension=0, tiled=True)
    grad_conv, reduce_level = tied(grad_conv, reduce_level)
    moving = far_send(reduce_level)
    back = attention_backward(
        resolution, projected, gate_logit, bias_wide, conv_taps, normed_heads, ratios, states, grad_conv, heads
    )
    back, moving = tied(back, moving)
    grad_projected, grad_gate, forgetbias_local, taps_local = back
    reduce_grad = far_add(reduce_level, moving)
    reduce_grad = reduce_grad.T if across else reduce_grad
    sums = jnp.concatenate(
        [
            taps_local,
            jnp.pad(forgetbias_local, ((0, 0), (0, features - LANES))),
            bias_sums.reshape(-1, features),
        ],
        axis=0,
    )
    bits = flip_bits(1, columns)
    for bit in bits[:-1]:
        sums = sums + flip_bit(sums, bit)
    attend_other, attend_parts = weight_grads(
        where, normed_in_t, grad_projected, grad_gate, heads // columns
    )
    attend_other, attend_parts, grad_projected, sums = tied(attend_other, attend_parts, grad_projected, sums)
    attend_other = cross_sum(attend_other)
    sums_moving = flip_bit(sums, bits[-1])
    back = front_backward(
        where, grad_projected, grad_gate, grad_after, tokens, modulation, attend_pieces
    )
    back, attend_other, sums_moving = tied(back, attend_other, sums_moving)
    tokens_grad, front_sums = back
    sums = sums + sums_moving
    attend_moving = first_send(attend_parts, attend_other)

    middle_sums = jnp.sum(middle_sums.reshape(QUARTERS, -1, 8, features), axis=1)
    grad_modulation = jnp.concatenate([front_sums[:, :2], middle_sums[:, :4]], axis=1)
    first_slot = (jnp.arange(slots) == 0)[:, None, None]
    grad_modulation = jnp.where(
        single, jnp.where(first_slot, jnp.sum(grad_modulation, axis=0, keepdims=True), 0.0), grad_modulation
    )
    grad_modulation = grad_modulation.reshape(slots, columns, own_columns).astype(jnp.bfloat16)
    grad_modulation = jnp.swapaxes(grad_modulation, 0, 1)
    rows_here = [
        send(pick(grad_modulation, (dp_at + shift) % columns), along_dp(shift)) for shift in range(1, columns)
    ]
    rows_here, attend_moving = tied(rows_here, attend_moving)
    attend_level = first_add(attend_parts, attend_other, attend_moving)
    attend_moving = second_send(attend_level)
    rows_here = jnp.concatenate([pick(grad_modulation, dp_at)] + rows_here, axis=0)
    sums_moving = flip_bit(sums, columns)
    rows_here = jnp.concatenate(
        [rows_here] + [send(rows_here, along_z(shift)) for shift in range(1, chips)], axis=0
    )
    rows_other = send(rows_here, across_core)
    rows_other, attend_moving, sums_moving = tied(rows_other, attend_moving, sums_moving)
    attend_level = second_add(attend_level, attend_moving)
    attend_moving = far_send(attend_level)
    sums = sums + sums_moving
    rows_here = jnp.concatenate([rows_here, rows_other], axis=0)
    order = []
    for sibling in range(2):
        for far in range(chips):
            for shift in range(columns):
                block = 2 * ((z_at - far) % chips) + jnp.abs(core_at - sibling)
                order.append(block * columns + (dp_at - shift) % columns)
    order = (jnp.stack(order)[:, None] * slots + jnp.arange(slots)[None, :]).reshape(-1)
    chosen = (order[:, None] == jnp.arange(order.shape[0])[None, :]).astype(jnp.bfloat16)
    cond_here = jnp.dot(chosen, cond_columns, preferred_element_type=jnp.float32).astype(jnp.bfloat16)
    modulate_grad = lax.dot_general(
        cond_here, rows_here, (((0,), (0,)), ((), ())), preferred_element_type=jnp.float32
    )
    modbias_here = jnp.sum(rows_here.astype(jnp.float32), axis=0, keepdims=True)
    modbias_all = jnp.stack(
        [modbias_here] + [send(modbias_here, along_dp(shift)) for shift in range(1, columns)]
    )
    modbias_all = jnp.concatenate([pick(modbias_all, (dp_at - column) % columns) for column in range(columns)], axis=1)
    own_bias = modulate_bias.shape[0]
    linear_at = fsdp_at * columns + dp_at
    modbias_grad = lax.dynamic_slice_in_dim(modbias_all, linear_at * own_bias, own_bias, axis=1).reshape(-1)
    grad_cond = lax.dot_general(
        rows_here, modulate_weight, (((1,), (1,)), ((), ())), preferred_element_type=jnp.float32
    )
    grad_cond = jnp.moveaxis(grad_cond.reshape(blocks, columns, slots, own_rows), 1, 0)
    bits = flip_bits(2 * columns, blocks * columns)
    sums_moving = flip_bit(sums, bits[0])
    cond_sum = [send(grad_cond[shift], along_dp(-shift)) for shift in range(1, columns)]
    cond_sum, attend_moving, sums_moving = tied(cond_sum, attend_moving, sums_moving)
    attend_both = far_add(attend_level, attend_moving)
    attend_grad, forget_grad = attend_both[:, : attend_weight.shape[1]], attend_both[:, attend_weight.shape[1] :]
    sums = sums + sums_moving
    for bit in bits[1:]:
        sums = sums + flip_bit(sums, bit)
    cond_sum = sum(cond_sum, grad_cond[0]).reshape(2, chips, slots, own_rows)
    cond_sum = jnp.stack([cond_sum[0], send(cond_sum[1], across_core)], axis=1)
    joint = joint[0].astype(jnp.float32)
    expand_grad, output_grad = joint[:, : expand_weight.shape[1]], joint[:, expand_weight.shape[1] :]
    cond_parts = jnp.concatenate(
        [cond_sum[0]] + [send(cond_sum[far], along_z(-far)) for far in range(1, chips)], axis=0
    )
    cond_columns_all = []
    for block in range(blocks):
        sibling = jnp.abs(block % 2 - core_at)
        cond_columns_all.append(pick(cond_parts, (block // 2 - z_at) % chips * 2 + sibling))
    grad_cond_low = jnp.concatenate(cond_columns_all, axis=1)
    conditions_grad = silu_back(grad_cond_low)[0].astype(jnp.bfloat16)

    taps_count = conv_taps.shape[0]
    taps_grad = sums[:taps_count]
    forgetbias_grad = sums[taps_count, :heads]
    own_bias = expand_bias.shape[0]
    expandbias_grad = lax.dynamic_slice_in_dim(
        sums[taps_count + 1 :].reshape(-1), linear_at * own_bias, own_bias, axis=0
    )
    return (
        block_out,
        tokens_grad,
        conditions_grad,
        modulate_grad,
        modbias_grad,
        attend_grad,
        forget_grad,
        forgetbias_grad,
        taps_grad,
        output_grad,
        expand_grad,
        expandbias_grad,
        reduce_grad,
    )


def solution(mesh):
    in_specs = (
        P(("fsdp", "dp"), None),
        P(("fsdp", "dp"), None),
        P(("fsdp", "dp")),
        P("fsdp", "dp"),
        P(("fsdp", "dp")),
        P("fsdp", "dp"),
        P("fsdp", "dp"),
        P(),
        P(),
        P("fsdp", "dp"),
        P("fsdp", "dp"),
        P(("fsdp", "dp")),
        P("fsdp", "dp"),
        P(("fsdp", "dp"), None),
    )
    out_specs = (
        P(("fsdp", "dp"), None),
        P(("fsdp", "dp"), None),
        P(("fsdp", "dp"), None),
        P("fsdp", "dp"),
        P(("fsdp", "dp")),
        P("fsdp", "dp"),
        P("fsdp", "dp"),
        P(),
        P(),
        P("fsdp", "dp"),
        P("fsdp", "dp"),
        P(("fsdp", "dp")),
        P("fsdp", "dp"),
    )
    return jax.shard_map(
        on_device, mesh=mesh, in_specs=in_specs, out_specs=out_specs, check_vma=False
    )
```

```python
import functools
import math

import jax
import jax.numpy as jnp
from jax import lax
from jax.experimental import pallas as pl
from jax.experimental.pallas import tpu as pltpu
from jax.sharding import PartitionSpec as P

GRID = 32
CHUNK = 256
LANES = 128
VMEM_BYTES = 60 * 1024 * 1024
QUARTERS = 4
COST = 0.02
Z_AT, CORE_AT, U_AT, V_AT, FLAG_AT = range(5)
normalizer = 16.0
ln_eps = 1e-06
gelu_scale = math.sqrt(2.0 / math.pi)
rms_floor = 1.0
masked_log = -1e30
highest = lax.Precision.HIGHEST


def dot_nn(former, latter, precision=None):
    return lax.dot_general(
        former, latter, (((1,), (0,)), ((), ())), precision=precision, preferred_element_type=jnp.float32
    )


def dot_nt(former, latter):
    return lax.dot_general(former, latter, (((1,), (1,)), ((), ())), preferred_element_type=jnp.float32)


def dot_tn(former, latter):
    return lax.dot_general(former, latter, (((0,), (0,)), ((), ())), preferred_element_type=jnp.float32)


def head_window(head, head_size):
    first = head * head_size
    start = first // LANES * LANES
    stop = -(-(first + head_size) // LANES) * LANES
    return start, stop - start, first - start


def lane_mask(width, offset, head_size):
    lanes = lax.broadcasted_iota(jnp.int32, (1, width), 1)
    return (lanes >= offset) & (lanes < offset + head_size)


def cell_masks(rows, side):
    position = lax.broadcasted_iota(jnp.int32, (rows, 1), 0)
    grid_col = position & (side - 1)
    grid_row = (position & (side * side - 1)) >> int(math.log2(side))
    return grid_row, grid_col


def conv_forward_tile(values, taps, side):
    rows = values.shape[0]
    grid_row, grid_col = cell_masks(rows, side)
    before = jnp.where(grid_col > 0, pltpu.roll(values, 1, 0), 0.0)
    after = jnp.where(grid_col < side - 1, pltpu.roll(values, rows - 1, 0), 0.0)
    sums = [
        before * taps[3 * step : 3 * step + 1]
        + values * taps[3 * step + 1 : 3 * step + 2]
        + after * taps[3 * step + 2 : 3 * step + 3]
        for step in range(3)
    ]
    upper = jnp.where(grid_row > 0, pltpu.roll(sums[0], side, 0), 0.0)
    lower = jnp.where(grid_row < side - 1, pltpu.roll(sums[2], rows - side, 0), 0.0)
    return sums[1] + upper + lower


def conv_backward_tile(values, grads, taps, side):
    rows = values.shape[0]
    grid_row, grid_col = cell_masks(rows, side)
    before = jnp.where(grid_col > 0, pltpu.roll(values, 1, 0), 0.0)
    after = jnp.where(grid_col < side - 1, pltpu.roll(values, rows - 1, 0), 0.0)
    grad_sums = [
        jnp.where(grid_row < side - 1, pltpu.roll(grads, rows - side, 0), 0.0),
        grads,
        jnp.where(grid_row > 0, pltpu.roll(grads, side, 0), 0.0),
    ]
    tap_rows = []
    for step in range(3):
        for shifted in (before, values, after):
            tap_rows.append(jnp.sum(grad_sums[step] * shifted, axis=0, keepdims=True))
    parts = [
        sum(grad_sums[step] * taps[3 * step + col : 3 * step + col + 1] for step in range(3))
        for col in range(3)
    ]
    result = (
        parts[1]
        + pltpu.roll(jnp.where(grid_col > 0, parts[0], 0.0), rows - 1, 0)
        + pltpu.roll(jnp.where(grid_col < side - 1, parts[2], 0.0), 1, 0)
    )
    return result, tap_rows


def decay_sums(gate, bias, chunk):
    logit = gate + bias
    decay = (jnp.minimum(logit, 0.0) - jnp.log1p(jnp.exp(-jnp.abs(logit)))) / normalizer
    row_at = lax.broadcasted_iota(jnp.int32, (chunk, chunk), 0)
    col_at = lax.broadcasted_iota(jnp.int32, (chunk, chunk), 1)
    lower = jnp.where(row_at >= col_at, 1.0, 0.0)
    return dot_nn(lower, decay, highest)


def attention_forward_kernel(
    heads, head_size, flag_ref, proj_ref, gate_ref, bias_ref, taps_ref, conv_ref, normed_ref, ratio_ref, states_ref, state
):
    chunk_at = pl.program_id(0)
    chunk = proj_ref.shape[0]
    features = heads * head_size
    single = flag_ref[0] == 1

    @pl.when(jnp.logical_or(chunk_at == 0, jnp.logical_not(single)))
    def _():
        state[...] = jnp.zeros_like(state)

    cumul = decay_sums(gate_ref[...], bias_ref[...], chunk)
    cumul_t = jnp.transpose(cumul)
    scaled = cumul + math.log(head_size ** (-0.5))
    last = cumul[chunk - 1 : chunk, :]
    last_scaled = scaled[chunk - 1 : chunk, :]
    whole = jnp.exp(last)
    row_at = lax.broadcasted_iota(jnp.int32, (chunk, chunk), 0)
    col_at = lax.broadcasted_iota(jnp.int32, (chunk, chunk), 1)
    causal = row_at >= col_at
    lane_at = lax.broadcasted_iota(jnp.int32, (1, LANES), 1)
    rows = pl.ds(pl.multiple_of(chunk_at * chunk, chunk), chunk)
    ratios = jnp.zeros((chunk, LANES), jnp.float32)
    for head in range(heads):
        start, width, offset = head_window(head, head_size)
        inside = lane_mask(width, offset, head_size)
        query = jnp.where(inside, proj_ref[:, start : start + width], 0)
        key = proj_ref[:, features + start : features + start + width]
        value = proj_ref[:, 2 * features + start : 2 * features + start + width]
        scaled_wide = jnp.broadcast_to(scaled[:, head : head + 1], (chunk, LANES))
        start_wide = jnp.exp(scaled_wide)
        end_wide = jnp.exp(last_scaled[:, head : head + 1] - scaled_wide)
        start_wide = jnp.concatenate([start_wide] * (width // LANES), axis=1)
        end_wide = jnp.concatenate([end_wide] * (width // LANES), axis=1)
        spread = jnp.concatenate([scaled_wide] * (chunk // LANES), axis=1) - cumul_t[head : head + 1, :]
        weights = jnp.exp(jnp.where(causal, spread, masked_log))
        scores = (dot_nt(query, key) * weights).astype(jnp.bfloat16)
        held = state[head, :width, :width]
        held_low = held.astype(jnp.bfloat16)
        states_ref[0, head, :width, :width] = held_low
        mixed = dot_nn(scores, value) + start_wide * dot_nn(query, held_low)
        mixed = jnp.where(inside, mixed, 0.0)
        mean_square = jnp.sum(mixed * mixed, axis=1, keepdims=True) / head_size
        ratio = lax.rsqrt(jnp.maximum(mean_square, rms_floor))
        coded = jnp.where(mean_square > rms_floor, -ratio, jnp.where(mean_square == rms_floor, 2.0, 1.0))
        ratios = jnp.where(lane_at == head, coded, ratios)
        window = normed_ref[rows, start : start + width]
        normed_ref[rows, start : start + width] = jnp.where(inside, mixed * ratio, window)
        key_end = (jnp.where(inside, key, 0) * end_wide).astype(jnp.bfloat16)
        state[head, :width, :width] = held * whole[:, head : head + 1] + dot_tn(key_end, value)
    ratio_ref[...] = ratios

    def convolve(side):
        def tile(at, carry):
            lanes = pl.ds(pl.multiple_of(at * LANES, LANES), LANES)
            conv_ref[:, lanes] = conv_forward_tile(normed_ref[:, lanes], taps_ref[:, lanes], side).astype(conv_ref.dtype)
            return carry

        lax.fori_loop(0, features // LANES, tile, 0)

    finished = chunk_at == pl.num_programs(0) - 1

    @pl.when(jnp.logical_and(finished, single))
    def _():
        convolve(GRID)

    @pl.when(jnp.logical_and(finished, jnp.logical_not(single)))
    def _():
        convolve(GRID // 2)


def attention_forward(flag, proj, gate, bias, taps, heads):
    rows = proj.shape[0]
    features = taps.shape[1]
    head_size = features // heads
    chunks = rows // CHUNK
    whole_rows = lambda at: (0, 0)
    return pl.pallas_call(
        functools.partial(attention_forward_kernel, heads, head_size),
        grid=(chunks,),
        in_specs=[
            pl.BlockSpec(memory_space=pltpu.SMEM),
            pl.BlockSpec((CHUNK, 3 * features), lambda at: (at, 0)),
            pl.BlockSpec((CHUNK, LANES), lambda at: (at, 0)),
            pl.BlockSpec((1, LANES), whole_rows),
            pl.BlockSpec((9, features), whole_rows),
        ],
        out_specs=[
            pl.BlockSpec((rows, features), whole_rows),
            pl.BlockSpec((rows, features), whole_rows),
            pl.BlockSpec((CHUNK, LANES), lambda at: (at, 0)),
            pl.BlockSpec((1, heads, 2 * LANES, 2 * LANES), lambda at: (at, 0, 0, 0)),
        ],
        out_shape=[
            jax.ShapeDtypeStruct((rows, features), jnp.bfloat16),
            jax.ShapeDtypeStruct((rows, features), jnp.float32),
            jax.ShapeDtypeStruct((rows, LANES), jnp.float32),
            jax.ShapeDtypeStruct((chunks, heads, 2 * LANES, 2 * LANES), jnp.bfloat16),
        ],
        scratch_shapes=[pltpu.VMEM((heads, 2 * LANES, 2 * LANES), jnp.float32)],
        compiler_params=pltpu.CompilerParams(vmem_limit_bytes=VMEM_BYTES),
        cost_estimate=pl.CostEstimate(flops=int(17 * 10**9 * COST), bytes_accessed=int(20 * 10**6 * COST), transcendentals=0),
        name="attention_forward",
    )(flag, proj, gate, bias, taps)


def attention_backward_kernel(
    heads,
    head_size,
    flag_ref,
    proj_ref,
    gate_ref,
    bias_ref,
    taps_ref,
    normed_ref,
    ratio_ref,
    states_ref,
    grads_ref,
    dproj_ref,
    dgate_ref,
    dbias_ref,
    dtaps_ref,
    dnormed,
    dstate,
):
    step = pl.program_id(0)
    chunks = pl.num_programs(0)
    chunk_at = chunks - 1 - step
    chunk = proj_ref.shape[0]
    features = heads * head_size
    single = flag_ref[0] == 1

    def convolve(side):
        def tile(at, carry):
            lanes = pl.ds(pl.multiple_of(at * LANES, LANES), LANES)
            result, tap_rows = conv_backward_tile(
                normed_ref[:, lanes], grads_ref[:, lanes], taps_ref[:, lanes], side
            )
            dnormed[:, lanes] = result
            for row, tap_row in enumerate(tap_rows):
                dtaps_ref[row : row + 1, lanes] = tap_row
            return carry

        lax.fori_loop(0, features // LANES, tile, 0)

    @pl.when(jnp.logical_and(step == 0, single))
    def _():
        convolve(GRID)

    @pl.when(jnp.logical_and(step == 0, jnp.logical_not(single)))
    def _():
        convolve(GRID // 2)

    @pl.when(step == 0)
    def _():
        dbias_ref[...] = jnp.zeros_like(dbias_ref)

    @pl.when(jnp.logical_or(step == 0, jnp.logical_not(single)))
    def _():
        dstate[...] = jnp.zeros_like(dstate)

    gate = gate_ref[...]
    bias = bias_ref[...]
    cumul = decay_sums(gate, bias, chunk)
    cumul_t = jnp.transpose(cumul)
    scaled = cumul + math.log(head_size ** (-0.5))
    last = cumul[chunk - 1 : chunk, :]
    last_scaled = scaled[chunk - 1 : chunk, :]
    whole = jnp.exp(last)
    row_at = lax.broadcasted_iota(jnp.int32, (chunk, chunk), 0)
    col_at = lax.broadcasted_iota(jnp.int32, (chunk, chunk), 1)
    causal = row_at >= col_at
    lane_at = lax.broadcasted_iota(jnp.int32, (1, LANES), 1)
    rows = pl.ds(pl.multiple_of(chunk_at * chunk, chunk), chunk)
    balance = jnp.zeros((chunk, LANES), jnp.float32)
    through = jnp.zeros((1, LANES), jnp.float32)
    for head in range(heads):
        start, width, offset = head_window(head, head_size)
        inside = lane_mask(width, offset, head_size)
        query = jnp.where(inside, proj_ref[:, start : start + width], 0)
        key = proj_ref[:, features + start : features + start + width]
        key_in = jnp.where(inside, key, 0)
        value = proj_ref[:, 2 * features + start : 2 * features + start + width]
        value_in = jnp.where(inside, value, 0)
        scaled_wide = jnp.broadcast_to(scaled[:, head : head + 1], (chunk, LANES))
        start_col = jnp.exp(scaled_wide)
        end_col = jnp.exp(last_scaled[:, head : head + 1] - scaled_wide)
        start_col = jnp.concatenate([start_col] * (width // LANES), axis=1)
        end_col = jnp.concatenate([end_col] * (width // LANES), axis=1)
        coded = jnp.broadcast_to(ratio_ref[:, head : head + 1], (chunk, LANES))
        ratio = jnp.where(coded < 0.0, -coded, 1.0)
        ratio = jnp.concatenate([ratio] * (width // LANES), axis=1)
        slope = jnp.where(coded < 0.0, 1.0, jnp.where(coded > 1.5, 0.5, 0.0)) / head_size
        slope = jnp.concatenate([slope] * (width // LANES), axis=1)
        normed = jnp.where(inside, normed_ref[rows, start : start + width], 0.0)
        dnorm = jnp.where(inside, dnormed[rows, start : start + width], 0.0)
        along = jnp.sum(dnorm * normed, axis=1, keepdims=True) * slope
        dmixed = (dnorm - normed * along) * ratio
        dmixed_start = (dmixed * start_col).astype(jnp.bfloat16)
        dmixed = dmixed.astype(jnp.bfloat16)
        spread = jnp.concatenate([scaled_wide] * (chunk // LANES), axis=1) - cumul_t[head : head + 1, :]
        weights = jnp.exp(jnp.where(causal, spread, masked_log))
        scores = (dot_nt(query, key) * weights).astype(jnp.bfloat16)
        dscores = (dot_nt(dmixed, value) * weights).astype(jnp.bfloat16)
        held = states_ref[0, head, :width, :width]
        dnext = dstate[head, :width, :width]
        dnext_low = dnext.astype(jnp.bfloat16)
        dquery = dot_nn(dscores, key) + dot_nt(dmixed_start, held)
        dkey_inside = dot_tn(dscores, query)
        dkey_after = end_col * dot_nt(value_in, dnext_low)
        dkey = dkey_inside + dkey_after
        dvalue = dot_tn(scores, dmixed) + end_col * dot_nn(key_in, dnext_low)
        dstate[head, :width, :width] = dnext * whole[:, head : head + 1] + dot_tn(query, dmixed_start)
        kept = jnp.sum(dnext * held, axis=0, keepdims=True) * whole[:, head : head + 1]
        term = jnp.sum(kept + jnp.sum(key_in * dkey_after, axis=0, keepdims=True), axis=1, keepdims=True)
        through = jnp.where(lane_at == head, term, through)
        balance_one = jnp.sum(query * dquery - key_in * dkey, axis=1, keepdims=True)
        balance = jnp.where(lane_at == head, balance_one, balance)
        for place, grad in ((0, dquery), (1, dkey), (2, dvalue)):
            columns = slice(place * features + start, place * features + start + width)
            dproj_ref[:, columns] = jnp.where(inside, grad.astype(dproj_ref.dtype), dproj_ref[:, columns])
    upper = jnp.where(row_at <= col_at, 1.0, 0.0)
    ddecay = dot_nn(upper, balance, highest) + through
    dgate = ddecay / (1.0 + jnp.exp(gate + bias)) / normalizer
    dgate_ref[...] = dgate
    dbias_ref[...] += jnp.sum(dgate, axis=0, keepdims=True)


def attention_backward(flag, proj, gate, bias, taps, normed, ratios, states, grads, heads):
    rows = proj.shape[0]
    features = taps.shape[1]
    head_size = features // heads
    chunks = rows // CHUNK
    whole_rows = lambda at: (0, 0)
    back = lambda at: (chunks - 1 - at, 0)
    return pl.pallas_call(
        functools.partial(attention_backward_kernel, heads, head_size),
        grid=(chunks,),
        in_specs=[
            pl.BlockSpec(memory_space=pltpu.SMEM),
            pl.BlockSpec((CHUNK, 3 * features), back),
            pl.BlockSpec((CHUNK, LANES), back),
            pl.BlockSpec((1, LANES), whole_rows),
            pl.BlockSpec((9, features), whole_rows),
            pl.BlockSpec((rows, features), whole_rows),
            pl.BlockSpec((CHUNK, LANES), back),
            pl.BlockSpec((1, heads, 2 * LANES, 2 * LANES), lambda at: (chunks - 1 - at, 0, 0, 0)),
            pl.BlockSpec((rows, features), whole_rows),
        ],
        out_specs=[
            pl.BlockSpec((CHUNK, 3 * features), back),
            pl.BlockSpec((CHUNK, LANES), back),
            pl.BlockSpec((1, LANES), whole_rows),
            pl.BlockSpec((9, features), whole_rows),
        ],
        out_shape=[
            jax.ShapeDtypeStruct((rows, 3 * features), jnp.bfloat16),
            jax.ShapeDtypeStruct((rows, LANES), jnp.float32),
            jax.ShapeDtypeStruct((1, LANES), jnp.float32),
            jax.ShapeDtypeStruct((9, features), jnp.float32),
        ],
        scratch_shapes=[
            pltpu.VMEM((rows, features), jnp.float32),
            pltpu.VMEM((heads, 2 * LANES, 2 * LANES), jnp.float32),
        ],
        compiler_params=pltpu.CompilerParams(vmem_limit_bytes=VMEM_BYTES),
        cost_estimate=pl.CostEstimate(flops=int(38 * 10**9 * COST), bytes_accessed=int(40 * 10**6 * COST), transcendentals=0),
        name="attention_backward",
    )(flag, proj, gate, bias, taps, normed, ratios, states, grads)


def parts_of(fsdp_size, dp_size):
    return fsdp_size // 2, math.isqrt(dp_size)


def mesh_parts():
    return parts_of(lax.axis_size("fsdp"), lax.axis_size("dp"))


def send(values, move):
    chips, side = mesh_parts()
    pairs = []
    for z in range(chips):
        for core in range(2):
            for u in range(side):
                for v in range(side):
                    to_z, to_core, to_u, to_v = move(z, core, u, v)
                    pairs.append(
                        (
                            ((z * 2 + core) * side + u) * side + v,
                            ((to_z * 2 + to_core) * side + to_u) * side + to_v,
                        )
                    )
    return lax.ppermute(values, ("fsdp", "dp"), pairs)


def along_z(shift):
    chips = mesh_parts()[0]
    return lambda z, core, u, v: ((z + shift) % chips, core, u, v)


def across_core(z, core, u, v):
    return z, 1 - core, u, v


def along_first(shift):
    side = mesh_parts()[1]

    def move(z, core, u, v):
        return (z, core, (u + shift) % side, v) if core == 0 else (z, core, u, (v + shift) % side)

    return move


def along_second(shift):
    side = mesh_parts()[1]

    def move(z, core, u, v):
        return (z, core, u, (v + shift) % side) if core == 0 else (z, core, (u + shift) % side, v)

    return move


def along_dp(shift):
    side = mesh_parts()[1]

    def move(z, core, u, v):
        to = (u * side + v + shift) % (side * side)
        return z, core, to // side, to % side

    return move


def far_pieces(shard):
    chips = mesh_parts()[0]
    return [shard] + [send(shard, along_z(shift)) for shift in range(1, chips)]


def first_pieces(stack):
    side = mesh_parts()[1]
    return [stack] + [send(stack, along_first(shift)) for shift in range(1, side)]


def second_pieces(level):
    side = mesh_parts()[1]
    own = []
    for piece in level:
        own += [piece] + [send(piece, along_second(shift)) for shift in range(1, side)]
    return own


def core_pieces(own):
    return own + [send(piece, across_core) for piece in own]


def gather_shard(shard):
    return core_pieces(second_pieces(first_pieces(jnp.stack(far_pieces(shard)))))


def add_low(*values):
    total = values[0].astype(jnp.float32)
    for value in values[1:]:
        total = total + value.astype(jnp.float32)
    return total


def cross_sum(joint):
    return send(joint, across_core)


def first_send(parts, other):
    side = mesh_parts()[1]
    sent = [add_low(parts[shift], other[shift]).astype(jnp.bfloat16) for shift in range(1, side)]
    return [send(value, along_first(shift + 1)) for shift, value in enumerate(sent)]


def first_add(parts, other, received):
    side = mesh_parts()[1]
    return [
        add_low(parts[0][second], other[0, second], *[value[second] for value in received]).astype(jnp.bfloat16)
        for second in range(side)
    ]


def second_send(level):
    side = mesh_parts()[1]
    return [send(level[shift], along_second(shift)) for shift in range(1, side)]


def second_add(level, received):
    chips = mesh_parts()[0]
    return [
        add_low(level[0][far], *[value[far] for value in received]).astype(jnp.bfloat16)
        for far in range(chips)
    ]


def far_send(level):
    chips = mesh_parts()[0]
    return [send(level[shift], along_z(shift)) for shift in range(1, chips)]


def far_add(level, received):
    return add_low(level[0], *received)


def tied(*values):
    return lax.optimization_barrier(values)


def fold_of(shape, columns):
    return columns if shape[0] % (16 * columns) == 0 else 1


def folded(values, fold):
    height = values.shape[0] // fold
    return jnp.concatenate([values[at * height : (at + 1) * height] for at in range(fold)], axis=1)


def flip_bit(values, bit):
    chips, side = mesh_parts()

    def move(z, core, u, v):
        to = (((z * 2 + core) * side + u) * side + v) ^ bit
        return to // (2 * side * side), to // (side * side) % 2, to // side % side, to % side

    return send(values, move)


def flip_bits(low, high):
    bits = []
    while low < high:
        bits.append(low)
        low *= 2
    return bits


def source_place(where, sibling, first, second, far, chips, side):
    core = 1 - where[CORE_AT] if sibling else where[CORE_AT]
    from_u = lax.rem(where[U_AT] - jnp.where(core == 0, first, second) + side, side)
    from_v = lax.rem(where[V_AT] - jnp.where(core == 0, second, first) + side, side)
    from_z = lax.rem(where[Z_AT] - far + chips, chips)
    return 2 * from_z + core, from_u * side + from_v


def weight_copies(where, pieces, target, sems, chips, side):
    copies = []
    rows = pieces[0].shape[1]
    for at, piece in enumerate(pieces):
        sibling, first, second = at // (side * side), at // side % side, at % side
        for far in range(chips):
            block, column = source_place(where, sibling, first, second, far, chips, side)
            copies.append(
                pltpu.make_async_copy(
                    piece.at[far],
                    target.at[column, pl.ds(pl.multiple_of(block * rows, 8), rows)],
                    sems.at[at * chips + far],
                )
            )
    return copies


def whole_copies(gathered, target, sems):
    rows = gathered.shape[1]
    columns = target.shape[0]
    return [
        pltpu.make_async_copy(
            gathered.at[at], target.at[at % columns, pl.ds(at // columns * rows, rows)], sems.at[at]
        )
        for at in range(gathered.shape[0])
    ]


def normalize(values):
    centred = values - jnp.mean(values, axis=1, keepdims=True)
    scale = lax.rsqrt(jnp.mean(centred * centred, axis=1, keepdims=True) + ln_eps)
    return centred * scale, scale


def normalize_back(grads, unit, scale):
    return scale * (
        grads - jnp.mean(grads, axis=1, keepdims=True) - unit * jnp.mean(grads * unit, axis=1, keepdims=True)
    )


def front_kernel(chips, side, where, tokens_ref, mod_ref, *rest):
    pieces, rest = rest[: 2 * side * side], rest[2 * side * side :]
    proj_ref, gate_ref, normed_t_ref, weight, sems = rest
    columns = side * side
    wide = proj_ref.shape[1] // columns
    narrow = weight.shape[2] - wide
    copies = weight_copies(where, pieces, weight, sems, chips, side)

    @pl.when(pl.program_id(0) == 0)
    def _():
        for copy in copies:
            copy.start()

    unit, ignored = normalize(tokens_ref[...].astype(jnp.float32))
    normed = (unit * (1.0 + mod_ref[0, 1:2, :]) + mod_ref[0, 0:1, :]).astype(jnp.bfloat16)
    normed_t_ref[...] = jnp.transpose(normed)

    @pl.when(pl.program_id(0) == 0)
    def _():
        for copy in copies:
            copy.wait()

    gate_ref[...] = jnp.zeros_like(gate_ref)
    for column in range(columns):
        product = dot_nn(normed, weight[column])
        proj_ref[:, column * wide : (column + 1) * wide] = product[:, :wide].astype(jnp.bfloat16)
        gate_ref[:, column * narrow : (column + 1) * narrow] = product[:, wide:]


def rows_spec(block, width):
    return pl.BlockSpec((block, width), lambda at, where: (at, 0))


def across_spec(height, block):
    return pl.BlockSpec((height, block), lambda at, where: (0, at))


def mod_spec(features, steps=4):
    share = steps // QUARTERS
    return pl.BlockSpec(
        (1, 8, features), lambda at, where: (jnp.where(where[FLAG_AT] == 1, 0, at // share), 0, 0)
    )


def any_specs(count):
    return [pl.BlockSpec(memory_space=pl.ANY)] * count


def shaped(shape, dtype):
    return jax.ShapeDtypeStruct(shape, dtype)


def call(kernel, where, args, grid, in_specs, out_specs, out_shape, scratch, name, flops, moved):
    return pl.pallas_call(
        kernel,
        grid_spec=pltpu.PrefetchScalarGridSpec(
            num_scalar_prefetch=1, grid=grid, in_specs=in_specs, out_specs=out_specs, scratch_shapes=scratch
        ),
        out_shape=out_shape,
        compiler_params=pltpu.CompilerParams(vmem_limit_bytes=VMEM_BYTES),
        cost_estimate=pl.CostEstimate(flops=int(flops * COST), bytes_accessed=int(moved * COST), transcendentals=0),
        name=name,
    )(where, *args)


def front_forward(where, tokens, mod, pieces, wide):
    chips, side = mesh_parts()
    rows, features = tokens.shape
    block = rows // QUARTERS
    columns = side * side
    depth, width = pieces[0].shape[1:]
    return call(
        functools.partial(front_kernel, chips, side),
        where,
        (tokens, mod, *pieces),
        (QUARTERS,),
        [rows_spec(block, features), mod_spec(features)] + any_specs(len(pieces)),
        [rows_spec(block, columns * wide), rows_spec(block, LANES), across_spec(features, block)],
        [
            shaped((rows, columns * wide), jnp.bfloat16),
            shaped((rows, LANES), jnp.float32),
            shaped((features, rows), jnp.bfloat16),
        ],
        [
            pltpu.VMEM((columns, features, width), jnp.bfloat16),
            pltpu.SemaphoreType.DMA((len(pieces) * chips,)),
        ],
        "front_forward",
        2 * rows * features * columns * width,
        20 * 10**6,
    )


def gelu_parts(values):
    square = values * values
    bent = jnp.tanh(values * (gelu_scale + (0.044715 * gelu_scale) * square))
    half = 0.5 + 0.5 * bent
    rise = values * (gelu_scale + (3 * 0.044715 * gelu_scale) * square)
    return values * half, half + half * (1.0 - bent) * rise


def middle_kernel(chips, side, where, conv_ref, tokens_ref, cot_ref, mod_ref, bias_ref, gathered, *rest):
    (
        attended_ref,
        hidden_ref,
        slope_ref,
        normed_t_ref,
        conv_t_ref,
        gradred_ref,
        weight,
        sems,
    ) = rest
    columns = side * side
    wide = hidden_ref.shape[1] // columns
    narrow = weight.shape[2] - wide
    copies = whole_copies(gathered, weight, sems)

    @pl.when(pl.program_id(0) == 0)
    def _():
        for copy in copies:
            copy.start()

    conv = conv_ref[...]
    conv_t_ref[...] = jnp.transpose(conv)
    gradred_ref[...] = (cot_ref[...].astype(jnp.float32) * mod_ref[0, 5:6, :]).astype(jnp.bfloat16)

    @pl.when(pl.program_id(0) == 0)
    def _():
        for copy in copies:
            copy.wait()

    for column in range(columns):
        attended_ref[:, column * narrow : (column + 1) * narrow] = dot_nn(conv, weight[column, :, wide:])
    after = tokens_ref[...].astype(jnp.float32) + mod_ref[0, 2:3, :] * attended_ref[...]
    unit, ignored = normalize(after)
    normed = (unit * (1.0 + mod_ref[0, 4:5, :]) + mod_ref[0, 3:4, :]).astype(jnp.bfloat16)
    normed_t_ref[...] = jnp.transpose(normed)
    ahead = dot_nn(normed, weight[0, :, :wide])
    for column in range(columns):
        span = slice(column * wide, (column + 1) * wide)
        preact = ahead + bias_ref[:, span]
        if column + 1 < columns:
            ahead = dot_nn(normed, weight[column + 1, :, :wide])
        hidden, slope = gelu_parts(preact)
        hidden_ref[:, span] = hidden.astype(jnp.bfloat16)
        slope_ref[:, span] = slope.astype(jnp.bfloat16)


def middle_forward(where, conv, tokens, cotangent, mod, bias, gathered, wide):
    chips, side = mesh_parts()
    rows, features = tokens.shape
    block = rows // QUARTERS
    columns = side * side
    width = gathered.shape[2]
    hidden = columns * wide
    return call(
        functools.partial(middle_kernel, chips, side),
        where,
        (conv, tokens, cotangent, mod, bias, gathered),
        (QUARTERS,),
        [
            rows_spec(block, features),
            rows_spec(block, features),
            rows_spec(block, features),
            mod_spec(features),
            pl.BlockSpec((1, hidden), lambda at, where: (0, 0)),
        ]
        + any_specs(1),
        [
            rows_spec(block, features),
            rows_spec(block, hidden),
            rows_spec(block, hidden),
            across_spec(features, block),
            across_spec(features, block),
            rows_spec(block, features),
        ],
        [
            shaped((rows, features), jnp.float32),
            shaped((rows, hidden), jnp.bfloat16),
            shaped((rows, hidden), jnp.bfloat16),
            shaped((features, rows), jnp.bfloat16),
            shaped((features, rows), jnp.bfloat16),
            shaped((rows, features), jnp.bfloat16),
        ],
        [
            pltpu.VMEM((columns, features, width), jnp.bfloat16),
            pltpu.SemaphoreType.DMA((gathered.shape[0],)),
        ],
        "middle_forward",
        2 * rows * features * columns * width,
        60 * 10**6,
    )


def middle_back_kernel(
    chips, side, where, hidden_ref, slope_ref, attended_ref, tokens_ref, cot_ref, mod_ref, *rest
):
    gathered, reduce_pieces, rest = rest[0], rest[1], rest[2:]
    (
        out_ref,
        gradpre_ref,
        gradafter_ref,
        gradatt_ref,
        gradconv_ref,
        sums_ref,
        biassum_ref,
        weight,
        reduce_weight,
        stage,
        sems,
        reduce_sems,
    ) = rest
    columns = side * side
    hidden = hidden_ref.shape[1]
    wide = hidden // columns
    narrow = weight.shape[2] - wide
    height = reduce_pieces.shape[1]
    fold = reduce_pieces.shape[2] // narrow
    copies = whole_copies(gathered, weight, sems)

    @pl.when(pl.program_id(0) == 0)
    def _():
        biassum_ref[...] = jnp.zeros_like(biassum_ref)

        def staged(block):
            slot = block % 2
            return [
                pltpu.make_async_copy(
                    reduce_pieces.at[block * columns + column],
                    stage.at[slot, column],
                    reduce_sems.at[slot, column],
                )
                for column in range(columns)
            ]

        turns = [staged(block) for block in range(2 * chips)]
        for copy in turns[0]:
            copy.start()
        for block, found in enumerate(turns):
            if block + 1 < len(turns):
                for copy in turns[block + 1]:
                    copy.start()
            if block == 0:
                for copy in copies:
                    copy.start()
            for copy in found:
                copy.wait()
            for at in range(fold):
                target = slice((block * fold + at) * height, (block * fold + at + 1) * height)
                for column in range(columns):
                    reduce_weight[target, column * narrow : (column + 1) * narrow] = stage[
                        block % 2, column, :, at * narrow : (at + 1) * narrow
                    ]

    cot = cot_ref[...].astype(jnp.float32)
    attended = attended_ref[...]
    after = tokens_ref[...].astype(jnp.float32) + mod_ref[0, 2:3, :] * attended
    reduced = dot_nn(hidden_ref[...], reduce_weight[...])
    sums_ref[...] = jnp.zeros_like(sums_ref)
    sums_ref[0, 3:4, :] = jnp.sum(cot * reduced, axis=0, keepdims=True)
    out_ref[...] = (after + mod_ref[0, 5:6, :] * reduced).astype(out_ref.dtype)
    gradred = (cot * mod_ref[0, 5:6, :]).astype(jnp.bfloat16)

    @pl.when(pl.program_id(0) == 0)
    def _():
        for copy in copies:
            copy.wait()

    gradmid = jnp.zeros(after.shape, jnp.float32)
    ahead = dot_nt(gradred, reduce_weight[:wide, :])
    for column in range(columns):
        span = slice(column * wide, (column + 1) * wide)
        gradact = ahead
        if column + 1 < columns:
            ahead = dot_nt(gradred, reduce_weight[(column + 1) * wide : (column + 2) * wide, :])
        gradpre = (gradact * slope_ref[:, span].astype(jnp.float32)).astype(jnp.bfloat16)
        gradpre_ref[:, span] = gradpre
        biassum_ref[:, span] += jnp.sum(gradpre.astype(jnp.float32), axis=0, keepdims=True)
        gradmid = gradmid + dot_nt(gradpre, weight[column, :, :wide])
    unit, scale = normalize(after)
    sums_ref[0, 1:2, :] = jnp.sum(gradmid, axis=0, keepdims=True)
    sums_ref[0, 2:3, :] = jnp.sum(gradmid * unit, axis=0, keepdims=True)
    gradafter = cot + normalize_back(gradmid * (1.0 + mod_ref[0, 4:5, :]), unit, scale)
    gradafter_ref[...] = gradafter
    sums_ref[0, 0:1, :] = jnp.sum(gradafter * attended, axis=0, keepdims=True)
    gradatt_ref[...] = (gradafter * mod_ref[0, 2:3, :]).astype(jnp.bfloat16)
    gradconv = jnp.zeros(after.shape, jnp.float32)
    for column in range(columns):
        gradconv = gradconv + dot_nt(
            gradatt_ref[:, column * narrow : (column + 1) * narrow], weight[column, :, wide:]
        )
    gradconv_ref[...] = gradconv


def middle_backward(where, hidden, slope, attended, tokens, cotangent, mod, gathered, reduce_pieces):
    chips, side = mesh_parts()
    rows, features = tokens.shape
    steps = QUARTERS if side * side <= 4 else 2 * QUARTERS
    block = rows // steps
    columns = side * side
    inner = hidden.shape[1]
    width = gathered.shape[2]
    depth, narrow = reduce_pieces.shape[1:]
    return call(
        functools.partial(middle_back_kernel, chips, side),
        where,
        (hidden, slope, attended, tokens, cotangent, mod, gathered, reduce_pieces),
        (steps,),
        [
            rows_spec(block, inner),
            rows_spec(block, inner),
            rows_spec(block, features),
            rows_spec(block, features),
            rows_spec(block, features),
            mod_spec(features, steps),
        ]
        + any_specs(2),
        [
            rows_spec(block, features),
            rows_spec(block, inner),
            rows_spec(block, features),
            rows_spec(block, features),
            rows_spec(block, features),
            pl.BlockSpec((1, 8, features), lambda at, where: (at, 0, 0)),
            pl.BlockSpec((1, inner), lambda at, where: (0, 0)),
        ],
        [
            shaped((rows, features), jnp.bfloat16),
            shaped((rows, inner), jnp.bfloat16),
            shaped((rows, features), jnp.float32),
            shaped((rows, features), jnp.bfloat16),
            shaped((rows, features), jnp.float32),
            shaped((steps, 8, features), jnp.float32),
            shaped((1, inner), jnp.float32),
        ],
        [
            pltpu.VMEM((columns, features, width), jnp.bfloat16),
            pltpu.VMEM((inner, features), jnp.bfloat16),
            pltpu.VMEM((2, columns, depth, narrow), jnp.bfloat16),
            pltpu.SemaphoreType.DMA((gathered.shape[0],)),
            pltpu.SemaphoreType.DMA((2, columns)),
        ],
        "middle_backward",
        6 * rows * features * inner,
        80 * 10**6,
    )


def front_back_kernel(
    chips, side, where, gradproj_ref, gradgate_ref, gradafter_ref, tokens_ref, mod_ref, *rest
):
    pieces, rest = rest[: 2 * side * side], rest[2 * side * side :]
    out_ref, sums_ref, weight, both, sems = rest
    columns = side * side
    wide = gradproj_ref.shape[1] // columns
    narrow = weight.shape[2] - wide
    copies = weight_copies(where, pieces, weight, sems, chips, side)

    @pl.when(pl.program_id(0) == 0)
    def _():
        for copy in copies:
            copy.start()

    unit, scale = normalize(tokens_ref[...].astype(jnp.float32))

    @pl.when(pl.program_id(0) == 0)
    def _():
        for copy in copies:
            copy.wait()

    gradin = jnp.zeros(unit.shape, jnp.float32)
    for column in range(columns):
        both[:, :wide] = gradproj_ref[:, column * wide : (column + 1) * wide]
        both[:, wide:] = gradgate_ref[:, column * narrow : (column + 1) * narrow].astype(jnp.bfloat16)
        gradin = gradin + dot_nt(both[...], weight[column])
    sums_ref[...] = jnp.zeros_like(sums_ref)
    sums_ref[0, 0:1, :] = jnp.sum(gradin, axis=0, keepdims=True)
    sums_ref[0, 1:2, :] = jnp.sum(gradin * unit, axis=0, keepdims=True)
    out_ref[...] = (
        gradafter_ref[...] + normalize_back(gradin * (1.0 + mod_ref[0, 1:2, :]), unit, scale)
    ).astype(out_ref.dtype)


def front_backward(where, gradproj, gradgate, gradafter, tokens, mod, pieces):
    chips, side = mesh_parts()
    rows, features = tokens.shape
    block = rows // QUARTERS
    columns = side * side
    width = pieces[0].shape[2]
    return call(
        functools.partial(front_back_kernel, chips, side),
        where,
        (gradproj, gradgate, gradafter, tokens, mod, *pieces),
        (QUARTERS,),
        [
            rows_spec(block, gradproj.shape[1]),
            rows_spec(block, LANES),
            rows_spec(block, features),
            rows_spec(block, features),
            mod_spec(features),
        ]
        + any_specs(len(pieces)),
        [rows_spec(block, features), pl.BlockSpec((1, 8, features), lambda at, where: (at, 0, 0))],
        [shaped((rows, features), jnp.bfloat16), shaped((QUARTERS, 8, features), jnp.float32)],
        [
            pltpu.VMEM((columns, features, width), jnp.bfloat16),
            pltpu.VMEM((block, width), jnp.bfloat16),
            pltpu.SemaphoreType.DMA((len(pieces) * chips,)),
        ],
        "front_backward",
        2 * rows * features * columns * width,
        25 * 10**6,
    )


def target_block(where, sibling, far, chips):
    core = 1 - where[CORE_AT] if sibling else where[CORE_AT]
    return 2 * lax.rem(where[Z_AT] + far, chips) + core


def target_column(where, first, second, side):
    core = where[CORE_AT]
    to_u = lax.rem(where[U_AT] + jnp.where(core == 0, first, second), side)
    to_v = lax.rem(where[V_AT] + jnp.where(core == 0, second, first), side)
    return to_u * side + to_v


def relative_column(where, column, side):
    core = where[CORE_AT]
    by_u = lax.rem(column // side - where[U_AT] + side, side)
    by_v = lax.rem(column % side - where[V_AT] + side, side)
    return jnp.where(core == 0, by_u, by_v), jnp.where(core == 0, by_v, by_u)


def grads_product(left, right, chips):
    product = dot_nn(left, right)
    return product.reshape(chips, product.shape[0] // chips, product.shape[1]).astype(jnp.bfloat16)


def stack_lefts(lefts, left_all):
    depth = lefts[0].shape[0]
    for at, left in enumerate(lefts):
        left_all[at * depth : (at + 1) * depth, :] = left[...]


def grads_by_column_kernel(side, chips, where, *rest):
    lefts, right_ref, other, rest = rest[: 2 * chips], rest[2 * chips], rest[2 * chips + 1], rest[2 * chips + 2 :]
    outs, left_all = rest[:side], rest[side]
    half = left_all.shape[0] // 2

    @pl.when(pl.program_id(0) == 0)
    def _():
        stack_lefts(lefts, left_all)

    other[0, 0] = grads_product(left_all[half:, :], right_ref[...], chips)
    for first in range(side):

        @pl.when(pl.program_id(0) // side == first)
        def _(first=first):
            outs[first][0] = grads_product(left_all[:half, :], right_ref[...], chips)


def grads_joint_kernel(blocks, aligned, where, left_ref, small_left_ref, right_ref, small_right_ref, out, *scratch):
    small = scratch[0]
    wide = scratch[1].shape[1] if not aligned else right_ref.shape[1]
    narrow = small.shape[1]
    count = small_right_ref.shape[1] // narrow
    for column in range(count):

        @pl.when(pl.program_id(0) == column)
        def _(column=column):
            small[...] = small_right_ref[:, column * narrow : (column + 1) * narrow]
            if not aligned:
                scratch[1][...] = right_ref[:, column * wide : (column + 1) * wide]

    right = right_ref if aligned else scratch[1]
    out[:, 0, :, :wide] = grads_product(left_ref[...], right[...], blocks)
    out[:, 0, :, wide:] = grads_product(small_left_ref[...], small[...], blocks)


def grads_joint(where, left_t, right, small_left_t, small_right):
    chips, side = mesh_parts()
    columns, blocks = side * side, 2 * chips
    height, rows = left_t.shape
    depth = height // blocks
    wide, narrow = right.shape[1] // columns, small_right.shape[1] // columns
    aligned = wide % LANES == 0
    fixed = lambda at, where: (0, 0)
    scratch = [pltpu.VMEM((rows, narrow), jnp.bfloat16)]
    if not aligned:
        scratch.append(pltpu.VMEM((rows, wide), jnp.bfloat16))
    found = call(
        functools.partial(grads_joint_kernel, blocks, aligned),
        where,
        (left_t, small_left_t, right, small_right),
        (columns,),
        [
            pl.BlockSpec(left_t.shape, fixed),
            pl.BlockSpec(small_left_t.shape, fixed),
            pl.BlockSpec((rows, wide), lambda at, where: (0, at)) if aligned else pl.BlockSpec(right.shape, fixed),
            pl.BlockSpec(small_right.shape, fixed),
        ],
        pl.BlockSpec((blocks, 1, depth, wide + narrow), lambda at, where: (0, at, 0, 0)),
        shaped((blocks, columns, depth, wide + narrow), jnp.bfloat16),
        scratch,
        "grads_joint",
        2 * rows * height * columns * (wide + narrow),
        30 * 10**6,
    )
    return found.reshape(blocks * columns, depth, wide + narrow)


def grads_by_row_kernel(side, chips, extra, where, *rest):
    lefts, right_ref, rest = rest[: 2 * chips], rest[2 * chips], rest[2 * chips + 1 :]
    if extra:
        extra_ref, rest = rest[0], rest[1:]
    other, outs, left_all, both = rest[0], rest[1 : 1 + side], rest[1 + side], rest[2 + side]
    columns = side * side
    wide = right_ref.shape[1] // columns
    narrow = both.shape[1] - wide
    half = left_all.shape[0] // 2
    stack_lefts(lefts, left_all)
    for column in range(columns):
        by_first, by_second = relative_column(where, column, side)
        both[:, :wide] = right_ref[:, column * wide : (column + 1) * wide]
        if extra:
            both[:, wide:] = extra_ref[:, column * narrow : (column + 1) * narrow].astype(jnp.bfloat16)
        other[by_second, by_first] = grads_product(left_all[half:, :], both[...], chips)
        for first in range(side):

            @pl.when(by_first == first)
            def _(first=first, by_second=by_second):
                outs[first][by_second] = grads_product(left_all[:half, :], both[...], chips)


def grads_across_kernel(side, chips, where, right_ref, hidden_ref, other, *rest):
    outs, right_t, product = rest[:side], rest[side], rest[side + 1]
    columns = side * side
    wide = right_ref.shape[1] // columns
    depth = hidden_ref.shape[1] // 2

    @pl.when(pl.program_id(0) == 0)
    def _():
        right_t[...] = jnp.transpose(right_ref[...])

    product[...] = dot_nn(right_t[...], hidden_ref[...]).astype(jnp.bfloat16)
    for core in range(2):
        mine = slice(core * depth, (core + 1) * depth)
        theirs = slice((1 - core) * depth, (2 - core) * depth)
        for column in range(columns):
            by_first, by_second = relative_column(where, column, side)
            span = slice(column * wide, (column + 1) * wide)

            @pl.when(where[CORE_AT] == core)
            def _(span=span, theirs=theirs, by_first=by_first, by_second=by_second):
                other[by_second, by_first, 0] = product[span, theirs]

            for first in range(side):

                @pl.when(jnp.logical_and(where[CORE_AT] == core, by_first == first))
                def _(first=first, span=span, mine=mine, by_second=by_second):
                    outs[first][by_second, 0] = product[span, mine]


def piece_shapes(side, chips, piece):
    other = shaped((side, side, chips, *piece), jnp.bfloat16)
    return [other] + [shaped((side, chips, *piece), jnp.bfloat16)] * side


def grads_across(where, hidden, right):
    chips, side = mesh_parts()
    columns = side * side
    rows, inner = hidden.shape
    depth, wide = inner // (2 * chips), right.shape[1] // columns
    piece = (wide, depth)
    found = call(
        functools.partial(grads_across_kernel, side, chips),
        where,
        (right, hidden),
        (chips,),
        [
            pl.BlockSpec(right.shape, lambda at, where: (0, 0)),
            pl.BlockSpec((rows, 2 * depth), lambda at, where: (0, lax.rem(where[Z_AT] + at, chips))),
        ],
        [pl.BlockSpec((side, side, 1, *piece), lambda at, where: (0, 0, at, 0, 0))]
        + [pl.BlockSpec((side, 1, *piece), lambda at, where: (0, at, 0, 0))] * side,
        piece_shapes(side, chips, piece),
        [
            pltpu.VMEM((right.shape[1], rows), jnp.bfloat16),
            pltpu.VMEM((right.shape[1], 2 * depth), jnp.bfloat16),
        ],
        "grads_across",
        2 * rows * inner * right.shape[1],
        24 * 10**6,
    )
    return found[0], found[1:]


def weight_grads(where, left_t, right, extra=None, narrow=0):
    chips, side = mesh_parts()
    columns = side * side
    height, rows = left_t.shape
    depth = height // (2 * chips)
    wide = right.shape[1] // columns
    piece = (depth, wide + narrow)

    def left_spec(sibling, far):
        return pl.BlockSpec((depth, rows), lambda at, where: (target_block(where, sibling, far, chips), 0))

    specs = [left_spec(sibling, far) for sibling in (False, True) for far in range(chips)]
    args = [left_t] * (2 * chips) + [right]
    if wide % LANES == 0 and extra is None:
        steps = columns
        specs.append(
            pl.BlockSpec(
                (rows, wide), lambda at, where: (0, target_column(where, at // side, lax.rem(at, side), side))
            )
        )
        joint = pl.BlockSpec((1, 1, chips, *piece), lambda at, where: (lax.rem(at, side), at // side, 0, 0, 0))

        def out_spec(first):
            return pl.BlockSpec(
                (1, chips, *piece), lambda at, where: (jnp.clip(at - first * side, 0, side - 1), 0, 0, 0)
            )

        kernel = functools.partial(grads_by_column_kernel, side, chips)
        scratch = [pltpu.VMEM((height, rows), jnp.bfloat16)]
    else:
        steps = 1
        specs.append(pl.BlockSpec(right.shape, lambda at, where: (0, 0)))
        if extra is not None:
            specs.append(pl.BlockSpec(extra.shape, lambda at, where: (0, 0)))
            args.append(extra)
        joint = pl.BlockSpec((side, side, chips, *piece), lambda at, where: (0, 0, 0, 0, 0))

        def out_spec(first):
            return pl.BlockSpec((side, chips, *piece), lambda at, where: (0, 0, 0, 0))

        kernel = functools.partial(grads_by_row_kernel, side, chips, extra is not None)
        scratch = [pltpu.VMEM((height, rows), jnp.bfloat16), pltpu.VMEM((rows, wide + narrow), jnp.bfloat16)]
    found = call(
        kernel,
        where,
        args,
        (steps,),
        specs,
        [joint] + [out_spec(first) for first in range(side)],
        piece_shapes(side, chips, piece),
        scratch,
        "weight_grads",
        2 * rows * height * columns * wide,
        2 * (rows * height + rows * columns * wide + height * columns * wide),
    )
    return found[0], found[1:]


def pick(values, at):
    return lax.dynamic_index_in_dim(values, at, 0, keepdims=False)


def on_device(
    tokens,
    conditions,
    resolution,
    modulate_weight,
    modulate_bias,
    attend_weight,
    forget_weight,
    forget_bias,
    conv_taps,
    output_weight,
    expand_weight,
    expand_bias,
    reduce_weight,
    cotangent,
):
    chips, side = mesh_parts()
    columns = side * side
    blocks = 2 * chips
    fsdp_at = lax.axis_index("fsdp")
    dp_at = lax.axis_index("dp")
    z_at, core_at, u_at, v_at = fsdp_at // 2, fsdp_at % 2, dp_at // side, dp_at % side
    where = jnp.stack([z_at, core_at, u_at, v_at, resolution[0]]).astype(jnp.int32)
    slots, features = conditions.shape
    heads = forget_bias.shape[0]
    own_rows, own_columns = modulate_weight.shape
    single = resolution[0] == 1

    attend_pieces = gather_shard(jnp.concatenate([attend_weight, forget_weight], axis=1))

    cond_values = conditions.astype(jnp.float32)
    silu_out, silu_back = jax.vjp(jax.nn.silu, cond_values)
    cond_low = silu_out.astype(jnp.bfloat16)
    small = jnp.concatenate([cond_low.reshape(-1), modulate_bias, expand_bias])
    small_size = small.shape[0]
    small = jnp.stack(gather_shard(small.reshape(1, small_size))).reshape(blocks * columns, small_size)
    order = []
    for block in range(blocks):
        for column in range(columns):
            sibling = jnp.abs(block % 2 - core_at)
            far = (z_at - block // 2) % chips
            by_u, by_v = (u_at - column // side) % side, (v_at - column % side) % side
            first = jnp.where(block % 2 == 0, by_u, by_v)
            second = jnp.where(block % 2 == 0, by_v, by_u)
            order.append(((sibling * side + first) * side + second) * chips + far)
    order = jnp.stack(order)
    chosen = (order[:, None] == jnp.arange(blocks * columns)[None, :]).astype(jnp.bfloat16)
    small = jnp.dot(chosen, small, preferred_element_type=jnp.float32)
    cond_all = small[:, : slots * features].astype(jnp.bfloat16).reshape(-1, features)
    modbias_whole = small[:, slots * features : small_size - expand_bias.shape[0]].reshape(-1)
    expandbias_whole = small[:, small_size - expand_bias.shape[0] :].reshape(1, -1)
    cond_columns = lax.dynamic_slice_in_dim(cond_all, fsdp_at * own_rows, own_rows, axis=1)
    partial = jnp.dot(cond_columns, modulate_weight, preferred_element_type=jnp.float32)
    partial = partial.reshape(chips, 2, columns * slots, own_columns)
    to_sibling = lax.dynamic_index_in_dim(partial, 1 - core_at, 1, keepdims=False)
    partial = lax.dynamic_index_in_dim(partial, core_at, 1, keepdims=False) + send(to_sibling, across_core)
    modulation = pick(partial, z_at)
    for shift in range(1, chips):
        modulation = modulation + send(pick(partial, (z_at + shift) % chips), along_z(shift))
    modulation = modulation.reshape(columns, slots, own_columns)
    pieces = [pick(modulation, dp_at)]
    for shift in range(1, columns):
        pieces.append(send(pick(modulation, (dp_at + shift) % columns), along_dp(shift)))
    pieces = jnp.stack(pieces)
    modulation = jnp.concatenate([pick(pieces, (dp_at - column) % columns) for column in range(columns)], axis=1)
    modulation = (modulation + modbias_whole[None, :]).reshape(slots, 6, features)
    modulation = jnp.pad(modulation, ((0, 0), (0, 2), (0, 0)))

    fold = fold_of(reduce_weight.shape, columns)
    middle_pieces = lax.all_gather(
        jnp.concatenate([expand_weight, output_weight], axis=1), ("fsdp", "dp"), axis=0, tiled=False
    )

    projected, gate_logit, normed_in_t = front_forward(
        where, tokens, modulation, attend_pieces, attend_weight.shape[1]
    )
    projected, reduce_shard = tied(projected, folded(reduce_weight, fold))
    reduce_pieces = lax.all_gather(reduce_shard, ("fsdp", "dp"), axis=0, tiled=False)
    bias_wide = jnp.pad(forget_bias[None, :], ((0, 0), (0, LANES - heads)))
    conv_low, normed_heads, ratios, states = attention_forward(
        resolution, projected, gate_logit, bias_wide, conv_taps, heads
    )
    attended, hidden, slope, normed_mid_t, conv_t, grad_reduced = middle_forward(
        where, conv_low, tokens, cotangent, modulation, expandbias_whole, middle_pieces, expand_weight.shape[1]
    )
    across = (2 * reduce_weight.shape[0]) % LANES == 0
    if across:
        reduce_other, reduce_parts = grads_across(where, hidden, grad_reduced)
    else:
        reduce_other, reduce_parts = weight_grads(where, hidden.T, grad_reduced)
    reduce_other = cross_sum(reduce_other)
    hidden, reduce_parts, reduce_other = tied(hidden, reduce_parts, reduce_other)
    moving = first_send(reduce_parts, reduce_other)
    back = middle_backward(
        where, hidden, slope, attended, tokens, cotangent, modulation, middle_pieces, reduce_pieces
    )
    back, moving = tied(back, moving)
    block_out, grad_preact, grad_after, grad_attended, grad_conv, middle_sums, bias_sums = back
    reduce_level = first_add(reduce_parts, reduce_other, moving)
    moving = second_send(reduce_level)
    joint = grads_joint(where, normed_mid_t, grad_preact, conv_t, grad_attended)
    joint, moving = tied(joint, moving)
    reduce_level = second_add(reduce_level, moving)
    joint = lax.psum_scatter(joint, ("fsdp", "dp"), scatter_dimension=0, tiled=True)
    grad_conv, reduce_level = tied(grad_conv, reduce_level)
    moving = far_send(reduce_level)
    back = attention_backward(
        resolution, projected, gate_logit, bias_wide, conv_taps, normed_heads, ratios, states, grad_conv, heads
    )
    back, moving = tied(back, moving)
    grad_projected, grad_gate, forgetbias_local, taps_local = back
    reduce_grad = far_add(reduce_level, moving)
    reduce_grad = reduce_grad.T if across else reduce_grad
    sums = jnp.concatenate(
        [
            taps_local,
            jnp.pad(forgetbias_local, ((0, 0), (0, features - LANES))),
            bias_sums.reshape(-1, features),
        ],
        axis=0,
    )
    bits = flip_bits(1, columns)
    for bit in bits[:-1]:
        sums = sums + flip_bit(sums, bit)
    attend_other, attend_parts = weight_grads(
        where, normed_in_t, grad_projected, grad_gate, heads // columns
    )
    attend_other, attend_parts, grad_projected, sums = tied(attend_other, attend_parts, grad_projected, sums)
    attend_other = cross_sum(attend_other)
    sums_moving = flip_bit(sums, bits[-1])
    grad_projected, attend_other, sums_moving = tied(grad_projected, attend_other, sums_moving)
    sums = sums + sums_moving
    attend_moving = first_send(attend_parts, attend_other)
    back = front_backward(
        where, grad_projected, grad_gate, grad_after, tokens, modulation, attend_pieces
    )
    back, attend_moving = tied(back, attend_moving)
    tokens_grad, front_sums = back
    attend_level = first_add(attend_parts, attend_other, attend_moving)

    middle_sums = jnp.sum(middle_sums.reshape(QUARTERS, -1, 8, features), axis=1)
    grad_modulation = jnp.concatenate([front_sums[:, :2], middle_sums[:, :4]], axis=1)
    first_slot = (jnp.arange(slots) == 0)[:, None, None]
    grad_modulation = jnp.where(
        single, jnp.where(first_slot, jnp.sum(grad_modulation, axis=0, keepdims=True), 0.0), grad_modulation
    )
    grad_modulation = grad_modulation.reshape(slots, columns, own_columns).astype(jnp.bfloat16)
    grad_modulation = jnp.swapaxes(grad_modulation, 0, 1)
    rows_here = [
        send(pick(grad_modulation, (dp_at + shift) % columns), along_dp(shift)) for shift in range(1, columns)
    ]
    rows_here, attend_level = tied(rows_here, attend_level)
    attend_moving = second_send(attend_level)
    rows_here = jnp.stack([pick(grad_modulation, dp_at)] + rows_here).reshape(columns * slots, own_columns)
    sums_moving = flip_bit(sums, columns)
    rows_here = jnp.stack([rows_here] + [send(rows_here, along_z(shift)) for shift in range(1, chips)])
    rows_other = send(rows_here, across_core)
    rows_other, attend_moving, sums_moving = tied(rows_other, attend_moving, sums_moving)
    attend_level = second_add(attend_level, attend_moving)
    attend_moving = far_send(attend_level)
    sums = sums + sums_moving
    bits = flip_bits(2 * columns, blocks * columns)
    sums_moving = flip_bit(sums, bits[0])
    rows_here = jnp.stack([rows_here, rows_other]).reshape(-1, own_columns)
    order = []
    for sibling in range(2):
        for far in range(chips):
            for shift in range(columns):
                block = 2 * ((z_at - far) % chips) + jnp.abs(core_at - sibling)
                order.append(block * columns + (dp_at - shift) % columns)
    order = (jnp.stack(order)[:, None] * slots + jnp.arange(slots)[None, :]).reshape(-1)
    chosen = (order[:, None] == jnp.arange(order.shape[0])[None, :]).astype(jnp.bfloat16)
    cond_here = jnp.dot(chosen, cond_columns, preferred_element_type=jnp.float32).astype(jnp.bfloat16)
    modulate_grad = lax.dot_general(
        cond_here, rows_here, (((0,), (0,)), ((), ())), preferred_element_type=jnp.float32
    )
    modbias_here = jnp.sum(rows_here.astype(jnp.float32), axis=0, keepdims=True)
    grad_cond = lax.dot_general(
        rows_here, modulate_weight, (((1,), (1,)), ((), ())), preferred_element_type=jnp.float32
    )
    grad_cond = jnp.moveaxis(grad_cond.reshape(blocks, columns, slots, own_rows), 1, 0)
    modulate_grad, grad_cond, modbias_here, attend_moving, sums_moving = tied(
        modulate_grad, grad_cond, modbias_here, attend_moving, sums_moving
    )
    modbias_all = jnp.stack(
        [modbias_here] + [send(modbias_here, along_dp(shift)) for shift in range(1, columns)]
    )
    modbias_all = jnp.concatenate([pick(modbias_all, (dp_at - column) % columns) for column in range(columns)], axis=1)
    own_bias = modulate_bias.shape[0]
    linear_at = fsdp_at * columns + dp_at
    modbias_grad = lax.dynamic_slice_in_dim(modbias_all, linear_at * own_bias, own_bias, axis=1).reshape(-1)
    cond_sum = [send(grad_cond[shift], along_dp(-shift)) for shift in range(1, columns)]
    attend_both = far_add(attend_level, attend_moving)
    attend_grad, forget_grad = attend_both[:, : attend_weight.shape[1]], attend_both[:, attend_weight.shape[1] :]
    sums = sums + sums_moving
    for bit in bits[1:]:
        sums = sums + flip_bit(sums, bit)
    cond_sum = sum(cond_sum, grad_cond[0]).reshape(2, chips, slots, own_rows)
    cond_sum = jnp.stack([cond_sum[0], send(cond_sum[1], across_core)], axis=1)
    joint = joint[0].astype(jnp.float32)
    expand_grad, output_grad = joint[:, : expand_weight.shape[1]], joint[:, expand_weight.shape[1] :]
    cond_parts = jnp.stack(
        [cond_sum[0]] + [send(cond_sum[far], along_z(-far)) for far in range(1, chips)]
    ).reshape(blocks, slots, own_rows)
    cond_columns_all = []
    for block in range(blocks):
        sibling = jnp.abs(block % 2 - core_at)
        cond_columns_all.append(pick(cond_parts, (block // 2 - z_at) % chips * 2 + sibling))
    grad_cond_low = jnp.concatenate(cond_columns_all, axis=1)
    conditions_grad = silu_back(grad_cond_low)[0].astype(jnp.bfloat16)

    taps_count = conv_taps.shape[0]
    taps_grad = sums[:taps_count]
    forgetbias_grad = sums[taps_count, :heads]
    own_bias = expand_bias.shape[0]
    expandbias_grad = lax.dynamic_slice_in_dim(
        sums[taps_count + 1 :].reshape(-1), linear_at * own_bias, own_bias, axis=0
    )
    return (
        block_out,
        tokens_grad,
        conditions_grad,
        modulate_grad,
        modbias_grad,
        attend_grad,
        forget_grad,
        forgetbias_grad,
        taps_grad,
        output_grad,
        expand_grad,
        expandbias_grad,
        reduce_grad,
    )


def solution(mesh):
    in_specs = (
        P(("fsdp", "dp"), None),
        P(("fsdp", "dp"), None),
        P(("fsdp", "dp")),
        P("fsdp", "dp"),
        P(("fsdp", "dp")),
        P("fsdp", "dp"),
        P("fsdp", "dp"),
        P(),
        P(),
        P("fsdp", "dp"),
        P("fsdp", "dp"),
        P(("fsdp", "dp")),
        P("fsdp", "dp"),
        P(("fsdp", "dp"), None),
    )
    out_specs = (
        P(("fsdp", "dp"), None),
        P(("fsdp", "dp"), None),
        P(("fsdp", "dp"), None),
        P("fsdp", "dp"),
        P(("fsdp", "dp")),
        P("fsdp", "dp"),
        P("fsdp", "dp"),
        P(),
        P(),
        P("fsdp", "dp"),
        P("fsdp", "dp"),
        P(("fsdp", "dp")),
        P("fsdp", "dp"),
    )
    return jax.shard_map(
        on_device, mesh=mesh, in_specs=in_specs, out_specs=out_specs, check_vma=False
    )
```

```python
import functools
import math

import jax
import jax.numpy as jnp
from jax import lax
from jax.experimental import pallas as pl
from jax.experimental.pallas import tpu as pltpu
from jax.sharding import PartitionSpec as P

GRID = 32
CHUNK = 256
LANES = 128
VMEM_BYTES = 60 * 1024 * 1024
QUARTERS = 4
COST = 0.02
Z_AT, CORE_AT, U_AT, V_AT, FLAG_AT = range(5)
normalizer = 16.0
ln_eps = 1e-06
gelu_scale = math.sqrt(2.0 / math.pi)
rms_floor = 1.0
masked_log = -1e30
highest = lax.Precision.HIGHEST


def dot_nn(former, latter, precision=None):
    return lax.dot_general(
        former, latter, (((1,), (0,)), ((), ())), precision=precision, preferred_element_type=jnp.float32
    )


def dot_nt(former, latter):
    return lax.dot_general(former, latter, (((1,), (1,)), ((), ())), preferred_element_type=jnp.float32)


def dot_tn(former, latter):
    return lax.dot_general(former, latter, (((0,), (0,)), ((), ())), preferred_element_type=jnp.float32)


def head_window(head, head_size):
    first = head * head_size
    start = first // LANES * LANES
    stop = -(-(first + head_size) // LANES) * LANES
    return start, stop - start, first - start


def lane_mask(width, offset, head_size):
    lanes = lax.broadcasted_iota(jnp.int32, (1, width), 1)
    return (lanes >= offset) & (lanes < offset + head_size)


def cell_masks(rows, side):
    position = lax.broadcasted_iota(jnp.int32, (rows, 1), 0)
    grid_col = position & (side - 1)
    grid_row = (position & (side * side - 1)) >> int(math.log2(side))
    return grid_row, grid_col


def conv_forward_tile(values, taps, side):
    rows = values.shape[0]
    grid_row, grid_col = cell_masks(rows, side)
    before = jnp.where(grid_col > 0, pltpu.roll(values, 1, 0), 0.0)
    after = jnp.where(grid_col < side - 1, pltpu.roll(values, rows - 1, 0), 0.0)
    sums = [
        before * taps[3 * step : 3 * step + 1]
        + values * taps[3 * step + 1 : 3 * step + 2]
        + after * taps[3 * step + 2 : 3 * step + 3]
        for step in range(3)
    ]
    upper = jnp.where(grid_row > 0, pltpu.roll(sums[0], side, 0), 0.0)
    lower = jnp.where(grid_row < side - 1, pltpu.roll(sums[2], rows - side, 0), 0.0)
    return sums[1] + upper + lower


def conv_backward_tile(values, grads, taps, side):
    rows = values.shape[0]
    grid_row, grid_col = cell_masks(rows, side)
    before = jnp.where(grid_col > 0, pltpu.roll(values, 1, 0), 0.0)
    after = jnp.where(grid_col < side - 1, pltpu.roll(values, rows - 1, 0), 0.0)
    grad_sums = [
        jnp.where(grid_row < side - 1, pltpu.roll(grads, rows - side, 0), 0.0),
        grads,
        jnp.where(grid_row > 0, pltpu.roll(grads, side, 0), 0.0),
    ]
    tap_rows = []
    for step in range(3):
        for shifted in (before, values, after):
            tap_rows.append(jnp.sum(grad_sums[step] * shifted, axis=0, keepdims=True))
    parts = [
        sum(grad_sums[step] * taps[3 * step + col : 3 * step + col + 1] for step in range(3))
        for col in range(3)
    ]
    result = (
        parts[1]
        + pltpu.roll(jnp.where(grid_col > 0, parts[0], 0.0), rows - 1, 0)
        + pltpu.roll(jnp.where(grid_col < side - 1, parts[2], 0.0), 1, 0)
    )
    return result, tap_rows


def decay_sums(gate, bias, chunk):
    logit = gate + bias
    decay = (jnp.minimum(logit, 0.0) - jnp.log1p(jnp.exp(-jnp.abs(logit)))) / normalizer
    row_at = lax.broadcasted_iota(jnp.int32, (chunk, chunk), 0)
    col_at = lax.broadcasted_iota(jnp.int32, (chunk, chunk), 1)
    lower = jnp.where(row_at >= col_at, 1.0, 0.0)
    return dot_nn(lower, decay, highest)


def attention_forward_kernel(
    heads, head_size, flag_ref, proj_ref, gate_ref, bias_ref, taps_ref, conv_ref, normed_ref, ratio_ref, states_ref, state
):
    chunk_at = pl.program_id(0)
    chunk = proj_ref.shape[0]
    features = heads * head_size
    single = flag_ref[0] == 1

    @pl.when(jnp.logical_or(chunk_at == 0, jnp.logical_not(single)))
    def _():
        state[...] = jnp.zeros_like(state)

    cumul = decay_sums(gate_ref[...], bias_ref[...], chunk)
    cumul_t = jnp.transpose(cumul)
    scaled = cumul + math.log(head_size ** (-0.5))
    last = cumul[chunk - 1 : chunk, :]
    last_scaled = scaled[chunk - 1 : chunk, :]
    whole = jnp.exp(last)
    row_at = lax.broadcasted_iota(jnp.int32, (chunk, chunk), 0)
    col_at = lax.broadcasted_iota(jnp.int32, (chunk, chunk), 1)
    causal = row_at >= col_at
    lane_at = lax.broadcasted_iota(jnp.int32, (1, LANES), 1)
    rows = pl.ds(pl.multiple_of(chunk_at * chunk, chunk), chunk)
    ratios = jnp.zeros((chunk, LANES), jnp.float32)
    for head in range(heads):
        start, width, offset = head_window(head, head_size)
        inside = lane_mask(width, offset, head_size)
        query = jnp.where(inside, proj_ref[:, start : start + width], 0)
        key = proj_ref[:, features + start : features + start + width]
        value = proj_ref[:, 2 * features + start : 2 * features + start + width]
        scaled_wide = jnp.broadcast_to(scaled[:, head : head + 1], (chunk, LANES))
        start_wide = jnp.exp(scaled_wide)
        end_wide = jnp.exp(last_scaled[:, head : head + 1] - scaled_wide)
        start_wide = jnp.concatenate([start_wide] * (width // LANES), axis=1)
        end_wide = jnp.concatenate([end_wide] * (width // LANES), axis=1)
        spread = jnp.concatenate([scaled_wide] * (chunk // LANES), axis=1) - cumul_t[head : head + 1, :]
        weights = jnp.exp(jnp.where(causal, spread, masked_log))
        scores = (dot_nt(query, key) * weights).astype(jnp.bfloat16)
        held = state[head, :width, :width]
        held_low = held.astype(jnp.bfloat16)
        states_ref[0, head, :width, :width] = held_low
        mixed = dot_nn(scores, value) + start_wide * dot_nn(query, held_low)
        mixed = jnp.where(inside, mixed, 0.0)
        mean_square = jnp.sum(mixed * mixed, axis=1, keepdims=True) / head_size
        ratio = lax.rsqrt(jnp.maximum(mean_square, rms_floor))
        coded = jnp.where(mean_square > rms_floor, -ratio, jnp.where(mean_square == rms_floor, 2.0, 1.0))
        ratios = jnp.where(lane_at == head, coded, ratios)
        window = normed_ref[rows, start : start + width]
        normed_ref[rows, start : start + width] = jnp.where(inside, mixed * ratio, window)
        key_end = (jnp.where(inside, key, 0) * end_wide).astype(jnp.bfloat16)
        state[head, :width, :width] = held * whole[:, head : head + 1] + dot_tn(key_end, value)
    ratio_ref[...] = ratios

    def convolve(side):
        def tile(at, carry):
            lanes = pl.ds(pl.multiple_of(at * LANES, LANES), LANES)
            conv_ref[:, lanes] = conv_forward_tile(normed_ref[:, lanes], taps_ref[:, lanes], side).astype(conv_ref.dtype)
            return carry

        lax.fori_loop(0, features // LANES, tile, 0)

    finished = chunk_at == pl.num_programs(0) - 1

    @pl.when(jnp.logical_and(finished, single))
    def _():
        convolve(GRID)

    @pl.when(jnp.logical_and(finished, jnp.logical_not(single)))
    def _():
        convolve(GRID // 2)


def attention_forward(flag, proj, gate, bias, taps, heads):
    rows = proj.shape[0]
    features = taps.shape[1]
    head_size = features // heads
    chunks = rows // CHUNK
    whole_rows = lambda at: (0, 0)
    return pl.pallas_call(
        functools.partial(attention_forward_kernel, heads, head_size),
        grid=(chunks,),
        in_specs=[
            pl.BlockSpec(memory_space=pltpu.SMEM),
            pl.BlockSpec((CHUNK, 3 * features), lambda at: (at, 0)),
            pl.BlockSpec((CHUNK, LANES), lambda at: (at, 0)),
            pl.BlockSpec((1, LANES), whole_rows),
            pl.BlockSpec((9, features), whole_rows),
        ],
        out_specs=[
            pl.BlockSpec((rows, features), whole_rows),
            pl.BlockSpec((rows, features), whole_rows),
            pl.BlockSpec((CHUNK, LANES), lambda at: (at, 0)),
            pl.BlockSpec((1, heads, 2 * LANES, 2 * LANES), lambda at: (at, 0, 0, 0)),
        ],
        out_shape=[
            jax.ShapeDtypeStruct((rows, features), jnp.bfloat16),
            jax.ShapeDtypeStruct((rows, features), jnp.float32),
            jax.ShapeDtypeStruct((rows, LANES), jnp.float32),
            jax.ShapeDtypeStruct((chunks, heads, 2 * LANES, 2 * LANES), jnp.bfloat16),
        ],
        scratch_shapes=[pltpu.VMEM((heads, 2 * LANES, 2 * LANES), jnp.float32)],
        compiler_params=pltpu.CompilerParams(vmem_limit_bytes=VMEM_BYTES),
        cost_estimate=pl.CostEstimate(flops=int(17 * 10**9 * COST), bytes_accessed=int(20 * 10**6 * COST), transcendentals=0),
        name="attention_forward",
    )(flag, proj, gate, bias, taps)


def attention_backward_kernel(
    heads,
    head_size,
    flag_ref,
    proj_ref,
    gate_ref,
    bias_ref,
    taps_ref,
    normed_ref,
    ratio_ref,
    states_ref,
    grads_ref,
    dproj_ref,
    dgate_ref,
    dbias_ref,
    dtaps_ref,
    dnormed,
    dstate,
):
    step = pl.program_id(0)
    chunks = pl.num_programs(0)
    chunk_at = chunks - 1 - step
    chunk = proj_ref.shape[0]
    features = heads * head_size
    single = flag_ref[0] == 1

    def convolve(side):
        def tile(at, carry):
            lanes = pl.ds(pl.multiple_of(at * LANES, LANES), LANES)
            result, tap_rows = conv_backward_tile(
                normed_ref[:, lanes], grads_ref[:, lanes], taps_ref[:, lanes], side
            )
            dnormed[:, lanes] = result
            for row, tap_row in enumerate(tap_rows):
                dtaps_ref[row : row + 1, lanes] = tap_row
            return carry

        lax.fori_loop(0, features // LANES, tile, 0)

    @pl.when(jnp.logical_and(step == 0, single))
    def _():
        convolve(GRID)

    @pl.when(jnp.logical_and(step == 0, jnp.logical_not(single)))
    def _():
        convolve(GRID // 2)

    @pl.when(step == 0)
    def _():
        dbias_ref[...] = jnp.zeros_like(dbias_ref)

    @pl.when(jnp.logical_or(step == 0, jnp.logical_not(single)))
    def _():
        dstate[...] = jnp.zeros_like(dstate)

    gate = gate_ref[...]
    bias = bias_ref[...]
    cumul = decay_sums(gate, bias, chunk)
    cumul_t = jnp.transpose(cumul)
    scaled = cumul + math.log(head_size ** (-0.5))
    last = cumul[chunk - 1 : chunk, :]
    last_scaled = scaled[chunk - 1 : chunk, :]
    whole = jnp.exp(last)
    row_at = lax.broadcasted_iota(jnp.int32, (chunk, chunk), 0)
    col_at = lax.broadcasted_iota(jnp.int32, (chunk, chunk), 1)
    causal = row_at >= col_at
    lane_at = lax.broadcasted_iota(jnp.int32, (1, LANES), 1)
    rows = pl.ds(pl.multiple_of(chunk_at * chunk, chunk), chunk)
    balance = jnp.zeros((chunk, LANES), jnp.float32)
    through = jnp.zeros((1, LANES), jnp.float32)
    for head in range(heads):
        start, width, offset = head_window(head, head_size)
        inside = lane_mask(width, offset, head_size)
        query = jnp.where(inside, proj_ref[:, start : start + width], 0)
        key = proj_ref[:, features + start : features + start + width]
        key_in = jnp.where(inside, key, 0)
        value = proj_ref[:, 2 * features + start : 2 * features + start + width]
        value_in = jnp.where(inside, value, 0)
        scaled_wide = jnp.broadcast_to(scaled[:, head : head + 1], (chunk, LANES))
        start_col = jnp.exp(scaled_wide)
        end_col = jnp.exp(last_scaled[:, head : head + 1] - scaled_wide)
        start_col = jnp.concatenate([start_col] * (width // LANES), axis=1)
        end_col = jnp.concatenate([end_col] * (width // LANES), axis=1)
        coded = jnp.broadcast_to(ratio_ref[:, head : head + 1], (chunk, LANES))
        ratio = jnp.where(coded < 0.0, -coded, 1.0)
        ratio = jnp.concatenate([ratio] * (width // LANES), axis=1)
        slope = jnp.where(coded < 0.0, 1.0, jnp.where(coded > 1.5, 0.5, 0.0)) / head_size
        slope = jnp.concatenate([slope] * (width // LANES), axis=1)
        normed = jnp.where(inside, normed_ref[rows, start : start + width], 0.0)
        dnorm = jnp.where(inside, dnormed[rows, start : start + width], 0.0)
        along = jnp.sum(dnorm * normed, axis=1, keepdims=True) * slope
        dmixed = (dnorm - normed * along) * ratio
        dmixed_start = (dmixed * start_col).astype(jnp.bfloat16)
        dmixed = dmixed.astype(jnp.bfloat16)
        spread = jnp.concatenate([scaled_wide] * (chunk // LANES), axis=1) - cumul_t[head : head + 1, :]
        weights = jnp.exp(jnp.where(causal, spread, masked_log))
        scores = (dot_nt(query, key) * weights).astype(jnp.bfloat16)
        dscores = (dot_nt(dmixed, value) * weights).astype(jnp.bfloat16)
        held = states_ref[0, head, :width, :width]
        dnext = dstate[head, :width, :width]
        dnext_low = dnext.astype(jnp.bfloat16)
        dquery = dot_nn(dscores, key) + dot_nt(dmixed_start, held)
        dkey_inside = dot_tn(dscores, query)
        dkey_after = end_col * dot_nt(value_in, dnext_low)
        dkey = dkey_inside + dkey_after
        dvalue = dot_tn(scores, dmixed) + end_col * dot_nn(key_in, dnext_low)
        dstate[head, :width, :width] = dnext * whole[:, head : head + 1] + dot_tn(query, dmixed_start)
        kept = jnp.sum(dnext * held, axis=0, keepdims=True) * whole[:, head : head + 1]
        term = jnp.sum(kept + jnp.sum(key_in * dkey_after, axis=0, keepdims=True), axis=1, keepdims=True)
        through = jnp.where(lane_at == head, term, through)
        balance_one = jnp.sum(query * dquery - key_in * dkey, axis=1, keepdims=True)
        balance = jnp.where(lane_at == head, balance_one, balance)
        for place, grad in ((0, dquery), (1, dkey), (2, dvalue)):
            columns = slice(place * features + start, place * features + start + width)
            dproj_ref[:, columns] = jnp.where(inside, grad.astype(dproj_ref.dtype), dproj_ref[:, columns])
    upper = jnp.where(row_at <= col_at, 1.0, 0.0)
    ddecay = dot_nn(upper, balance, highest) + through
    dgate = ddecay / (1.0 + jnp.exp(gate + bias)) / normalizer
    dgate_ref[...] = dgate
    dbias_ref[...] += jnp.sum(dgate, axis=0, keepdims=True)


def attention_backward(flag, proj, gate, bias, taps, normed, ratios, states, grads, heads):
    rows = proj.shape[0]
    features = taps.shape[1]
    head_size = features // heads
    chunks = rows // CHUNK
    whole_rows = lambda at: (0, 0)
    back = lambda at: (chunks - 1 - at, 0)
    return pl.pallas_call(
        functools.partial(attention_backward_kernel, heads, head_size),
        grid=(chunks,),
        in_specs=[
            pl.BlockSpec(memory_space=pltpu.SMEM),
            pl.BlockSpec((CHUNK, 3 * features), back),
            pl.BlockSpec((CHUNK, LANES), back),
            pl.BlockSpec((1, LANES), whole_rows),
            pl.BlockSpec((9, features), whole_rows),
            pl.BlockSpec((rows, features), whole_rows),
            pl.BlockSpec((CHUNK, LANES), back),
            pl.BlockSpec((1, heads, 2 * LANES, 2 * LANES), lambda at: (chunks - 1 - at, 0, 0, 0)),
            pl.BlockSpec((rows, features), whole_rows),
        ],
        out_specs=[
            pl.BlockSpec((CHUNK, 3 * features), back),
            pl.BlockSpec((CHUNK, LANES), back),
            pl.BlockSpec((1, LANES), whole_rows),
            pl.BlockSpec((9, features), whole_rows),
        ],
        out_shape=[
            jax.ShapeDtypeStruct((rows, 3 * features), jnp.bfloat16),
            jax.ShapeDtypeStruct((rows, LANES), jnp.float32),
            jax.ShapeDtypeStruct((1, LANES), jnp.float32),
            jax.ShapeDtypeStruct((9, features), jnp.float32),
        ],
        scratch_shapes=[
            pltpu.VMEM((rows, features), jnp.float32),
            pltpu.VMEM((heads, 2 * LANES, 2 * LANES), jnp.float32),
        ],
        compiler_params=pltpu.CompilerParams(vmem_limit_bytes=VMEM_BYTES),
        cost_estimate=pl.CostEstimate(flops=int(38 * 10**9 * COST), bytes_accessed=int(40 * 10**6 * COST), transcendentals=0),
        name="attention_backward",
    )(flag, proj, gate, bias, taps, normed, ratios, states, grads)


def parts_of(fsdp_size, dp_size):
    return fsdp_size // 2, math.isqrt(dp_size)


def mesh_parts():
    return parts_of(lax.axis_size("fsdp"), lax.axis_size("dp"))


def send(values, move):
    chips, side = mesh_parts()
    pairs = []
    for z in range(chips):
        for core in range(2):
            for u in range(side):
                for v in range(side):
                    to_z, to_core, to_u, to_v = move(z, core, u, v)
                    pairs.append(
                        (
                            ((z * 2 + core) * side + u) * side + v,
                            ((to_z * 2 + to_core) * side + to_u) * side + to_v,
                        )
                    )
    return lax.ppermute(values, ("fsdp", "dp"), pairs)


def along_z(shift):
    chips = mesh_parts()[0]
    return lambda z, core, u, v: ((z + shift) % chips, core, u, v)


def across_core(z, core, u, v):
    return z, 1 - core, u, v


def along_first(shift):
    side = mesh_parts()[1]

    def move(z, core, u, v):
        return (z, core, (u + shift) % side, v) if core == 0 else (z, core, u, (v + shift) % side)

    return move


def along_second(shift):
    side = mesh_parts()[1]

    def move(z, core, u, v):
        return (z, core, u, (v + shift) % side) if core == 0 else (z, core, (u + shift) % side, v)

    return move


def along_dp(shift):
    side = mesh_parts()[1]

    def move(z, core, u, v):
        to = (u * side + v + shift) % (side * side)
        return z, core, to // side, to % side

    return move


def far_pieces(shard):
    chips = mesh_parts()[0]
    return [shard] + [send(shard, along_z(shift)) for shift in range(1, chips)]


def first_pieces(stack):
    side = mesh_parts()[1]
    return [stack] + [send(stack, along_first(shift)) for shift in range(1, side)]


def second_pieces(level):
    side = mesh_parts()[1]
    own = []
    for piece in level:
        own += [piece] + [send(piece, along_second(shift)) for shift in range(1, side)]
    return own


def core_pieces(own):
    return own + [send(piece, across_core) for piece in own]


def gather_shard(shard):
    return core_pieces(second_pieces(first_pieces(jnp.stack(far_pieces(shard)))))


def add_low(*values):
    total = values[0].astype(jnp.float32)
    for value in values[1:]:
        total = total + value.astype(jnp.float32)
    return total


def cross_sum(joint):
    return send(joint, across_core)


def first_send(parts, other):
    side = mesh_parts()[1]
    sent = [add_low(parts[shift], other[shift]).astype(jnp.bfloat16) for shift in range(1, side)]
    return [send(value, along_first(shift + 1)) for shift, value in enumerate(sent)]


def first_add(parts, other, received):
    side = mesh_parts()[1]
    return [
        add_low(parts[0, second], other[0, second], *[value[second] for value in received]).astype(jnp.bfloat16)
        for second in range(side)
    ]


def second_send(level):
    side = mesh_parts()[1]
    return [send(level[shift], along_second(shift)) for shift in range(1, side)]


def second_add(level, received):
    chips = mesh_parts()[0]
    return [
        add_low(level[0][far], *[value[far] for value in received]).astype(jnp.bfloat16)
        for far in range(chips)
    ]


def far_send(level):
    chips = mesh_parts()[0]
    return [send(level[shift], along_z(shift)) for shift in range(1, chips)]


def far_add(level, received):
    return add_low(level[0], *received)


def tied(*values):
    return lax.optimization_barrier(values)


def fold_of(shape, columns):
    return columns if shape[0] % (16 * columns) == 0 else 1


def folded(values, fold):
    height = values.shape[0] // fold
    return jnp.concatenate([values[at * height : (at + 1) * height] for at in range(fold)], axis=1)


def flip_bit(values, bit):
    chips, side = mesh_parts()

    def move(z, core, u, v):
        to = (((z * 2 + core) * side + u) * side + v) ^ bit
        return to // (2 * side * side), to // (side * side) % 2, to // side % side, to % side

    return send(values, move)


def flip_bits(low, high):
    bits = []
    while low < high:
        bits.append(low)
        low *= 2
    return bits


def source_place(where, sibling, first, second, far, chips, side):
    core = 1 - where[CORE_AT] if sibling else where[CORE_AT]
    from_u = lax.rem(where[U_AT] - jnp.where(core == 0, first, second) + side, side)
    from_v = lax.rem(where[V_AT] - jnp.where(core == 0, second, first) + side, side)
    from_z = lax.rem(where[Z_AT] - far + chips, chips)
    return 2 * from_z + core, from_u * side + from_v


def weight_copies(where, pieces, target, sems, chips, side):
    copies = []
    rows = pieces[0].shape[1]
    for at, piece in enumerate(pieces):
        sibling, first, second = at // (side * side), at // side % side, at % side
        for far in range(chips):
            block, column = source_place(where, sibling, first, second, far, chips, side)
            copies.append(
                pltpu.make_async_copy(
                    piece.at[far],
                    target.at[column, pl.ds(pl.multiple_of(block * rows, 8), rows)],
                    sems.at[at * chips + far],
                )
            )
    return copies


def whole_copies(gathered, target, sems):
    rows = gathered.shape[1]
    columns = target.shape[0]
    return [
        pltpu.make_async_copy(
            gathered.at[at], target.at[at % columns, pl.ds(at // columns * rows, rows)], sems.at[at]
        )
        for at in range(gathered.shape[0])
    ]


def normalize(values):
    centred = values - jnp.mean(values, axis=1, keepdims=True)
    scale = lax.rsqrt(jnp.mean(centred * centred, axis=1, keepdims=True) + ln_eps)
    return centred * scale, scale


def normalize_back(grads, unit, scale):
    return scale * (
        grads - jnp.mean(grads, axis=1, keepdims=True) - unit * jnp.mean(grads * unit, axis=1, keepdims=True)
    )


def front_kernel(chips, side, where, tokens_ref, mod_ref, *rest):
    pieces, rest = rest[: 2 * side * side], rest[2 * side * side :]
    proj_ref, gate_ref, normed_t_ref, weight, sems = rest
    columns = side * side
    wide = proj_ref.shape[1] // columns
    narrow = weight.shape[2] - wide
    copies = weight_copies(where, pieces, weight, sems, chips, side)

    @pl.when(pl.program_id(0) == 0)
    def _():
        for copy in copies:
            copy.start()

    unit, ignored = normalize(tokens_ref[...].astype(jnp.float32))
    normed = (unit * (1.0 + mod_ref[0, 1:2, :]) + mod_ref[0, 0:1, :]).astype(jnp.bfloat16)
    normed_t_ref[...] = jnp.transpose(normed)

    @pl.when(pl.program_id(0) == 0)
    def _():
        for copy in copies:
            copy.wait()

    gate_ref[...] = jnp.zeros_like(gate_ref)
    for column in range(columns):
        product = dot_nn(normed, weight[column])
        proj_ref[:, column * wide : (column + 1) * wide] = product[:, :wide].astype(jnp.bfloat16)
        gate_ref[:, column * narrow : (column + 1) * narrow] = product[:, wide:]


def rows_spec(block, width):
    return pl.BlockSpec((block, width), lambda at, where: (at, 0))


def across_spec(height, block):
    return pl.BlockSpec((height, block), lambda at, where: (0, at))


def mod_spec(features, steps=4):
    share = steps // QUARTERS
    return pl.BlockSpec(
        (1, 8, features), lambda at, where: (jnp.where(where[FLAG_AT] == 1, 0, at // share), 0, 0)
    )


def any_specs(count):
    return [pl.BlockSpec(memory_space=pl.ANY)] * count


def shaped(shape, dtype):
    return jax.ShapeDtypeStruct(shape, dtype)


def call(kernel, where, args, grid, in_specs, out_specs, out_shape, scratch, name, flops, moved):
    return pl.pallas_call(
        kernel,
        grid_spec=pltpu.PrefetchScalarGridSpec(
            num_scalar_prefetch=1, grid=grid, in_specs=in_specs, out_specs=out_specs, scratch_shapes=scratch
        ),
        out_shape=out_shape,
        compiler_params=pltpu.CompilerParams(vmem_limit_bytes=VMEM_BYTES),
        cost_estimate=pl.CostEstimate(flops=int(flops * COST), bytes_accessed=int(moved * COST), transcendentals=0),
        name=name,
    )(where, *args)


def front_forward(where, tokens, mod, pieces, wide):
    chips, side = mesh_parts()
    rows, features = tokens.shape
    block = rows // QUARTERS
    columns = side * side
    depth, width = pieces[0].shape[1:]
    return call(
        functools.partial(front_kernel, chips, side),
        where,
        (tokens, mod, *pieces),
        (QUARTERS,),
        [rows_spec(block, features), mod_spec(features)] + any_specs(len(pieces)),
        [rows_spec(block, columns * wide), rows_spec(block, LANES), across_spec(features, block)],
        [
            shaped((rows, columns * wide), jnp.bfloat16),
            shaped((rows, LANES), jnp.float32),
            shaped((features, rows), jnp.bfloat16),
        ],
        [
            pltpu.VMEM((columns, features, width), jnp.bfloat16),
            pltpu.SemaphoreType.DMA((len(pieces) * chips,)),
        ],
        "front_forward",
        2 * rows * features * columns * width,
        20 * 10**6,
    )


def gelu_parts(values):
    square = values * values
    bent = jnp.tanh(values * (gelu_scale + (0.044715 * gelu_scale) * square))
    half = 0.5 + 0.5 * bent
    rise = values * (gelu_scale + (3 * 0.044715 * gelu_scale) * square)
    return values * half, half + half * (1.0 - bent) * rise


def middle_kernel(chips, side, where, conv_ref, tokens_ref, cot_ref, mod_ref, bias_ref, gathered, *rest):
    (
        attended_ref,
        hidden_ref,
        slope_ref,
        normed_t_ref,
        conv_t_ref,
        gradred_ref,
        weight,
        sems,
    ) = rest
    columns = side * side
    wide = hidden_ref.shape[1] // columns
    narrow = weight.shape[2] - wide
    copies = whole_copies(gathered, weight, sems)

    @pl.when(pl.program_id(0) == 0)
    def _():
        for copy in copies:
            copy.start()

    conv = conv_ref[...]
    conv_t_ref[...] = jnp.transpose(conv)
    gradred_ref[...] = (cot_ref[...].astype(jnp.float32) * mod_ref[0, 5:6, :]).astype(jnp.bfloat16)

    @pl.when(pl.program_id(0) == 0)
    def _():
        for copy in copies:
            copy.wait()

    for column in range(columns):
        attended_ref[:, column * narrow : (column + 1) * narrow] = dot_nn(conv, weight[column, :, wide:])
    after = tokens_ref[...].astype(jnp.float32) + mod_ref[0, 2:3, :] * attended_ref[...]
    unit, ignored = normalize(after)
    normed = (unit * (1.0 + mod_ref[0, 4:5, :]) + mod_ref[0, 3:4, :]).astype(jnp.bfloat16)
    normed_t_ref[...] = jnp.transpose(normed)
    ahead = dot_nn(normed, weight[0, :, :wide])
    for column in range(columns):
        span = slice(column * wide, (column + 1) * wide)
        preact = ahead + bias_ref[:, span]
        if column + 1 < columns:
            ahead = dot_nn(normed, weight[column + 1, :, :wide])
        hidden, slope = gelu_parts(preact)
        hidden_ref[:, span] = hidden.astype(jnp.bfloat16)
        slope_ref[:, span] = slope.astype(jnp.bfloat16)


def middle_forward(where, conv, tokens, cotangent, mod, bias, gathered, wide):
    chips, side = mesh_parts()
    rows, features = tokens.shape
    block = rows // QUARTERS
    columns = side * side
    width = gathered.shape[2]
    hidden = columns * wide
    return call(
        functools.partial(middle_kernel, chips, side),
        where,
        (conv, tokens, cotangent, mod, bias, gathered),
        (QUARTERS,),
        [
            rows_spec(block, features),
            rows_spec(block, features),
            rows_spec(block, features),
            mod_spec(features),
            pl.BlockSpec((1, hidden), lambda at, where: (0, 0)),
        ]
        + any_specs(1),
        [
            rows_spec(block, features),
            rows_spec(block, hidden),
            rows_spec(block, hidden),
            across_spec(features, block),
            across_spec(features, block),
            rows_spec(block, features),
        ],
        [
            shaped((rows, features), jnp.float32),
            shaped((rows, hidden), jnp.bfloat16),
            shaped((rows, hidden), jnp.bfloat16),
            shaped((features, rows), jnp.bfloat16),
            shaped((features, rows), jnp.bfloat16),
            shaped((rows, features), jnp.bfloat16),
        ],
        [
            pltpu.VMEM((columns, features, width), jnp.bfloat16),
            pltpu.SemaphoreType.DMA((gathered.shape[0],)),
        ],
        "middle_forward",
        2 * rows * features * columns * width,
        60 * 10**6,
    )


def middle_back_kernel(
    chips, side, where, hidden_ref, slope_ref, attended_ref, tokens_ref, cot_ref, mod_ref, *rest
):
    gathered, reduce_pieces, rest = rest[0], rest[1], rest[2:]
    (
        out_ref,
        gradpre_ref,
        gradafter_ref,
        gradatt_ref,
        gradconv_ref,
        sums_ref,
        biassum_ref,
        weight,
        reduce_weight,
        stage,
        sems,
        reduce_sems,
    ) = rest
    columns = side * side
    hidden = hidden_ref.shape[1]
    wide = hidden // columns
    narrow = weight.shape[2] - wide
    height = reduce_pieces.shape[1]
    fold = reduce_pieces.shape[2] // narrow
    copies = whole_copies(gathered, weight, sems)

    @pl.when(pl.program_id(0) == 0)
    def _():
        biassum_ref[...] = jnp.zeros_like(biassum_ref)

        def staged(block):
            slot = block % 2
            return [
                pltpu.make_async_copy(
                    reduce_pieces.at[block * columns + column],
                    stage.at[slot, column],
                    reduce_sems.at[slot, column],
                )
                for column in range(columns)
            ]

        turns = [staged(block) for block in range(2 * chips)]
        for copy in turns[0]:
            copy.start()
        for block, found in enumerate(turns):
            if block + 1 < len(turns):
                for copy in turns[block + 1]:
                    copy.start()
            if block == 0:
                for copy in copies:
                    copy.start()
            for copy in found:
                copy.wait()
            for at in range(fold):
                target = slice((block * fold + at) * height, (block * fold + at + 1) * height)
                for column in range(columns):
                    reduce_weight[target, column * narrow : (column + 1) * narrow] = stage[
                        block % 2, column, :, at * narrow : (at + 1) * narrow
                    ]

    cot = cot_ref[...].astype(jnp.float32)
    attended = attended_ref[...]
    after = tokens_ref[...].astype(jnp.float32) + mod_ref[0, 2:3, :] * attended
    reduced = dot_nn(hidden_ref[...], reduce_weight[...])
    sums_ref[...] = jnp.zeros_like(sums_ref)
    sums_ref[0, 3:4, :] = jnp.sum(cot * reduced, axis=0, keepdims=True)
    out_ref[...] = (after + mod_ref[0, 5:6, :] * reduced).astype(out_ref.dtype)
    gradred = (cot * mod_ref[0, 5:6, :]).astype(jnp.bfloat16)

    @pl.when(pl.program_id(0) == 0)
    def _():
        for copy in copies:
            copy.wait()

    gradmid = jnp.zeros(after.shape, jnp.float32)
    ahead = dot_nt(gradred, reduce_weight[:wide, :])
    for column in range(columns):
        span = slice(column * wide, (column + 1) * wide)
        gradact = ahead
        if column + 1 < columns:
            ahead = dot_nt(gradred, reduce_weight[(column + 1) * wide : (column + 2) * wide, :])
        gradpre = (gradact * slope_ref[:, span].astype(jnp.float32)).astype(jnp.bfloat16)
        gradpre_ref[:, span] = gradpre
        biassum_ref[:, span] += jnp.sum(gradpre.astype(jnp.float32), axis=0, keepdims=True)
        gradmid = gradmid + dot_nt(gradpre, weight[column, :, :wide])
    unit, scale = normalize(after)
    sums_ref[0, 1:2, :] = jnp.sum(gradmid, axis=0, keepdims=True)
    sums_ref[0, 2:3, :] = jnp.sum(gradmid * unit, axis=0, keepdims=True)
    gradafter = cot + normalize_back(gradmid * (1.0 + mod_ref[0, 4:5, :]), unit, scale)
    gradafter_ref[...] = gradafter
    sums_ref[0, 0:1, :] = jnp.sum(gradafter * attended, axis=0, keepdims=True)
    gradatt_ref[...] = (gradafter * mod_ref[0, 2:3, :]).astype(jnp.bfloat16)
    gradconv = jnp.zeros(after.shape, jnp.float32)
    for column in range(columns):
        gradconv = gradconv + dot_nt(
            gradatt_ref[:, column * narrow : (column + 1) * narrow], weight[column, :, wide:]
        )
    gradconv_ref[...] = gradconv


def middle_backward(where, hidden, slope, attended, tokens, cotangent, mod, gathered, reduce_pieces):
    chips, side = mesh_parts()
    rows, features = tokens.shape
    steps = QUARTERS if side * side <= 4 else 2 * QUARTERS
    block = rows // steps
    columns = side * side
    inner = hidden.shape[1]
    width = gathered.shape[2]
    depth, narrow = reduce_pieces.shape[1:]
    return call(
        functools.partial(middle_back_kernel, chips, side),
        where,
        (hidden, slope, attended, tokens, cotangent, mod, gathered, reduce_pieces),
        (steps,),
        [
            rows_spec(block, inner),
            rows_spec(block, inner),
            rows_spec(block, features),
            rows_spec(block, features),
            rows_spec(block, features),
            mod_spec(features, steps),
        ]
        + any_specs(2),
        [
            rows_spec(block, features),
            rows_spec(block, inner),
            rows_spec(block, features),
            rows_spec(block, features),
            rows_spec(block, features),
            pl.BlockSpec((1, 8, features), lambda at, where: (at, 0, 0)),
            pl.BlockSpec((1, inner), lambda at, where: (0, 0)),
        ],
        [
            shaped((rows, features), jnp.bfloat16),
            shaped((rows, inner), jnp.bfloat16),
            shaped((rows, features), jnp.float32),
            shaped((rows, features), jnp.bfloat16),
            shaped((rows, features), jnp.float32),
            shaped((steps, 8, features), jnp.float32),
            shaped((1, inner), jnp.float32),
        ],
        [
            pltpu.VMEM((columns, features, width), jnp.bfloat16),
            pltpu.VMEM((inner, features), jnp.bfloat16),
            pltpu.VMEM((2, columns, depth, narrow), jnp.bfloat16),
            pltpu.SemaphoreType.DMA((gathered.shape[0],)),
            pltpu.SemaphoreType.DMA((2, columns)),
        ],
        "middle_backward",
        6 * rows * features * inner,
        80 * 10**6,
    )


def front_back_kernel(
    chips, side, where, gradproj_ref, gradgate_ref, gradafter_ref, tokens_ref, mod_ref, *rest
):
    pieces, rest = rest[: 2 * side * side], rest[2 * side * side :]
    out_ref, sums_ref, weight, both, sems = rest
    columns = side * side
    wide = gradproj_ref.shape[1] // columns
    narrow = weight.shape[2] - wide
    copies = weight_copies(where, pieces, weight, sems, chips, side)

    @pl.when(pl.program_id(0) == 0)
    def _():
        for copy in copies:
            copy.start()

    unit, scale = normalize(tokens_ref[...].astype(jnp.float32))

    @pl.when(pl.program_id(0) == 0)
    def _():
        for copy in copies:
            copy.wait()

    gradin = jnp.zeros(unit.shape, jnp.float32)
    for column in range(columns):
        both[:, :wide] = gradproj_ref[:, column * wide : (column + 1) * wide]
        both[:, wide:] = gradgate_ref[:, column * narrow : (column + 1) * narrow].astype(jnp.bfloat16)
        gradin = gradin + dot_nt(both[...], weight[column])
    sums_ref[...] = jnp.zeros_like(sums_ref)
    sums_ref[0, 0:1, :] = jnp.sum(gradin, axis=0, keepdims=True)
    sums_ref[0, 1:2, :] = jnp.sum(gradin * unit, axis=0, keepdims=True)
    out_ref[...] = (
        gradafter_ref[...] + normalize_back(gradin * (1.0 + mod_ref[0, 1:2, :]), unit, scale)
    ).astype(out_ref.dtype)


def front_backward(where, gradproj, gradgate, gradafter, tokens, mod, pieces):
    chips, side = mesh_parts()
    rows, features = tokens.shape
    block = rows // QUARTERS
    columns = side * side
    width = pieces[0].shape[2]
    return call(
        functools.partial(front_back_kernel, chips, side),
        where,
        (gradproj, gradgate, gradafter, tokens, mod, *pieces),
        (QUARTERS,),
        [
            rows_spec(block, gradproj.shape[1]),
            rows_spec(block, LANES),
            rows_spec(block, features),
            rows_spec(block, features),
            mod_spec(features),
        ]
        + any_specs(len(pieces)),
        [rows_spec(block, features), pl.BlockSpec((1, 8, features), lambda at, where: (at, 0, 0))],
        [shaped((rows, features), jnp.bfloat16), shaped((QUARTERS, 8, features), jnp.float32)],
        [
            pltpu.VMEM((columns, features, width), jnp.bfloat16),
            pltpu.VMEM((block, width), jnp.bfloat16),
            pltpu.SemaphoreType.DMA((len(pieces) * chips,)),
        ],
        "front_backward",
        2 * rows * features * columns * width,
        25 * 10**6,
    )


def target_block(where, sibling, far, chips):
    core = 1 - where[CORE_AT] if sibling else where[CORE_AT]
    return 2 * lax.rem(where[Z_AT] + far, chips) + core


def target_column(where, first, second, side):
    core = where[CORE_AT]
    to_u = lax.rem(where[U_AT] + jnp.where(core == 0, first, second), side)
    to_v = lax.rem(where[V_AT] + jnp.where(core == 0, second, first), side)
    return to_u * side + to_v


def relative_column(where, column, side):
    core = where[CORE_AT]
    by_u = lax.rem(column // side - where[U_AT] + side, side)
    by_v = lax.rem(column % side - where[V_AT] + side, side)
    return jnp.where(core == 0, by_u, by_v), jnp.where(core == 0, by_v, by_u)


def grads_product(left, right, chips):
    product = dot_nn(left, right)
    return product.reshape(chips, product.shape[0] // chips, product.shape[1]).astype(jnp.bfloat16)


def stack_lefts(lefts, left_all):
    depth = lefts[0].shape[0]
    for at, left in enumerate(lefts):
        left_all[at * depth : (at + 1) * depth, :] = left[...]


def grads_joint_kernel(blocks, aligned, where, left_ref, small_left_ref, right_ref, small_right_ref, out, *scratch):
    small = scratch[0]
    wide = scratch[1].shape[1] if not aligned else right_ref.shape[1]
    narrow = small.shape[1]
    count = small_right_ref.shape[1] // narrow
    for column in range(count):

        @pl.when(pl.program_id(0) == column)
        def _(column=column):
            small[...] = small_right_ref[:, column * narrow : (column + 1) * narrow]
            if not aligned:
                scratch[1][...] = right_ref[:, column * wide : (column + 1) * wide]

    right = right_ref if aligned else scratch[1]
    out[:, 0, :, :wide] = grads_product(left_ref[...], right[...], blocks)
    out[:, 0, :, wide:] = grads_product(small_left_ref[...], small[...], blocks)


def grads_joint(where, left_t, right, small_left_t, small_right):
    chips, side = mesh_parts()
    columns, blocks = side * side, 2 * chips
    height, rows = left_t.shape
    depth = height // blocks
    wide, narrow = right.shape[1] // columns, small_right.shape[1] // columns
    aligned = wide % LANES == 0
    fixed = lambda at, where: (0, 0)
    scratch = [pltpu.VMEM((rows, narrow), jnp.bfloat16)]
    if not aligned:
        scratch.append(pltpu.VMEM((rows, wide), jnp.bfloat16))
    found = call(
        functools.partial(grads_joint_kernel, blocks, aligned),
        where,
        (left_t, small_left_t, right, small_right),
        (columns,),
        [
            pl.BlockSpec(left_t.shape, fixed),
            pl.BlockSpec(small_left_t.shape, fixed),
            pl.BlockSpec((rows, wide), lambda at, where: (0, at)) if aligned else pl.BlockSpec(right.shape, fixed),
            pl.BlockSpec(small_right.shape, fixed),
        ],
        pl.BlockSpec((blocks, 1, depth, wide + narrow), lambda at, where: (0, at, 0, 0)),
        shaped((blocks, columns, depth, wide + narrow), jnp.bfloat16),
        scratch,
        "grads_joint",
        2 * rows * height * columns * (wide + narrow),
        30 * 10**6,
    )
    return found.reshape(blocks * columns, depth, wide + narrow)


def grads_by_row_kernel(side, chips, extra, where, *rest):
    lefts, right_ref, rest = rest[: 2 * chips], rest[2 * chips], rest[2 * chips + 1 :]
    if extra:
        extra_ref, rest = rest[0], rest[1:]
    other, mine, left_all, both = rest
    columns = side * side
    wide = right_ref.shape[1] // columns
    narrow = both.shape[2] - wide
    half = left_all.shape[0] // 2
    stack_lefts(lefts, left_all)
    for column in range(columns):
        by_first, by_second = relative_column(where, column, side)
        right = both.at[column % 2]
        right[:, :wide] = right_ref[:, column * wide : (column + 1) * wide]
        if extra:
            right[:, wide:] = extra_ref[:, column * narrow : (column + 1) * narrow].astype(jnp.bfloat16)
        other[by_second, by_first] = grads_product(left_all[half:, :], right[...], chips)
        mine[by_first, by_second] = grads_product(left_all[:half, :], right[...], chips)


def grads_across_kernel(side, chips, where, right_ref, hidden_ref, other, mine, right_t):
    columns = side * side
    wide = right_ref.shape[1] // columns
    depth = hidden_ref.shape[1] // 2

    @pl.when(pl.program_id(0) == 0)
    def _():
        right_t[...] = jnp.transpose(right_ref[...])

    low_core = where[CORE_AT] == 0
    for column in range(columns):
        by_first, by_second = relative_column(where, column, side)
        product = dot_nn(right_t[column * wide : (column + 1) * wide, :], hidden_ref[...]).astype(jnp.bfloat16)
        former, latter = product[:, :depth], product[:, depth:]
        other[by_second, by_first, 0] = jnp.where(low_core, latter, former)
        mine[by_first, by_second, 0] = jnp.where(low_core, former, latter)


def piece_shapes(side, chips, piece):
    return [shaped((side, side, chips, *piece), jnp.bfloat16)] * 2


def grads_across(where, hidden, right):
    chips, side = mesh_parts()
    columns = side * side
    rows, inner = hidden.shape
    depth, wide = inner // (2 * chips), right.shape[1] // columns
    piece = (wide, depth)
    found = call(
        functools.partial(grads_across_kernel, side, chips),
        where,
        (right, hidden),
        (chips,),
        [
            pl.BlockSpec(right.shape, lambda at, where: (0, 0)),
            pl.BlockSpec((rows, 2 * depth), lambda at, where: (0, lax.rem(where[Z_AT] + at, chips))),
        ],
        [pl.BlockSpec((side, side, 1, *piece), lambda at, where: (0, 0, at, 0, 0))] * 2,
        piece_shapes(side, chips, piece),
        [
            pltpu.VMEM((right.shape[1], rows), jnp.bfloat16),
        ],
        "grads_across",
        2 * rows * inner * right.shape[1],
        24 * 10**6,
    )
    return found[0], found[1]


def weight_grads(where, left_t, right, extra=None, narrow=0):
    chips, side = mesh_parts()
    columns = side * side
    height, rows = left_t.shape
    depth = height // (2 * chips)
    wide = right.shape[1] // columns
    piece = (depth, wide + narrow)

    def left_spec(sibling, far):
        return pl.BlockSpec((depth, rows), lambda at, where: (target_block(where, sibling, far, chips), 0))

    specs = [left_spec(sibling, far) for sibling in (False, True) for far in range(chips)]
    args = [left_t] * (2 * chips) + [right]
    fixed = lambda at, where: (0, 0)
    specs.append(pl.BlockSpec(right.shape, fixed))
    if extra is not None:
        specs.append(pl.BlockSpec(extra.shape, fixed))
        args.append(extra)
    joint = pl.BlockSpec((side, side, chips, *piece), lambda at, where: (0, 0, 0, 0, 0))
    kernel = functools.partial(grads_by_row_kernel, side, chips, extra is not None)
    scratch = [pltpu.VMEM((height, rows), jnp.bfloat16), pltpu.VMEM((2, rows, wide + narrow), jnp.bfloat16)]
    found = call(
        kernel,
        where,
        args,
        (1,),
        specs,
        [joint] * 2,
        piece_shapes(side, chips, piece),
        scratch,
        "weight_grads",
        2 * rows * height * columns * wide,
        2 * (rows * height + rows * columns * wide + height * columns * wide),
    )
    return found[0], found[1]


def pick(values, at):
    return lax.dynamic_index_in_dim(values, at, 0, keepdims=False)


def on_device(
    tokens,
    conditions,
    resolution,
    modulate_weight,
    modulate_bias,
    attend_weight,
    forget_weight,
    forget_bias,
    conv_taps,
    output_weight,
    expand_weight,
    expand_bias,
    reduce_weight,
    cotangent,
):
    chips, side = mesh_parts()
    columns = side * side
    blocks = 2 * chips
    fsdp_at = lax.axis_index("fsdp")
    dp_at = lax.axis_index("dp")
    z_at, core_at, u_at, v_at = fsdp_at // 2, fsdp_at % 2, dp_at // side, dp_at % side
    where = jnp.stack([z_at, core_at, u_at, v_at, resolution[0]]).astype(jnp.int32)
    slots, features = conditions.shape
    heads = forget_bias.shape[0]
    own_rows, own_columns = modulate_weight.shape
    single = resolution[0] == 1

    attend_pieces = gather_shard(jnp.concatenate([attend_weight, forget_weight], axis=1))

    cond_values = conditions.astype(jnp.float32)
    silu_out, silu_back = jax.vjp(jax.nn.silu, cond_values)
    cond_low = silu_out.astype(jnp.bfloat16)
    small = jnp.concatenate([cond_low.reshape(-1), modulate_bias, expand_bias])
    small_size = small.shape[0]
    small = jnp.stack(gather_shard(small.reshape(1, small_size))).reshape(blocks * columns, small_size)
    order = []
    for block in range(blocks):
        for column in range(columns):
            sibling = jnp.abs(block % 2 - core_at)
            far = (z_at - block // 2) % chips
            by_u, by_v = (u_at - column // side) % side, (v_at - column % side) % side
            first = jnp.where(block % 2 == 0, by_u, by_v)
            second = jnp.where(block % 2 == 0, by_v, by_u)
            order.append(((sibling * side + first) * side + second) * chips + far)
    order = jnp.stack(order)
    chosen = (order[:, None] == jnp.arange(blocks * columns)[None, :]).astype(jnp.bfloat16)
    small = jnp.dot(chosen, small, preferred_element_type=jnp.float32)
    cond_all = small[:, : slots * features].astype(jnp.bfloat16).reshape(-1, features)
    modbias_whole = small[:, slots * features : small_size - expand_bias.shape[0]].reshape(-1)
    expandbias_whole = small[:, small_size - expand_bias.shape[0] :].reshape(1, -1)
    cond_columns = lax.dynamic_slice_in_dim(cond_all, fsdp_at * own_rows, own_rows, axis=1)
    partial = jnp.dot(cond_columns, modulate_weight, preferred_element_type=jnp.float32)
    partial = partial.reshape(chips, 2, columns * slots, own_columns)
    to_sibling = lax.dynamic_index_in_dim(partial, 1 - core_at, 1, keepdims=False)
    partial = lax.dynamic_index_in_dim(partial, core_at, 1, keepdims=False) + send(to_sibling, across_core)
    modulation = pick(partial, z_at)
    for shift in range(1, chips):
        modulation = modulation + send(pick(partial, (z_at + shift) % chips), along_z(shift))
    modulation = modulation.reshape(columns, slots, own_columns)
    pieces = [pick(modulation, dp_at)]
    for shift in range(1, columns):
        pieces.append(send(pick(modulation, (dp_at + shift) % columns), along_dp(shift)))
    pieces = jnp.stack(pieces)
    modulation = jnp.concatenate([pick(pieces, (dp_at - column) % columns) for column in range(columns)], axis=1)
    modulation = (modulation + modbias_whole[None, :]).reshape(slots, 6, features)
    modulation = jnp.pad(modulation, ((0, 0), (0, 2), (0, 0)))

    fold = fold_of(reduce_weight.shape, columns)
    middle_pieces = lax.all_gather(
        jnp.concatenate([expand_weight, output_weight], axis=1), ("fsdp", "dp"), axis=0, tiled=False
    )

    projected, gate_logit, normed_in_t = front_forward(
        where, tokens, modulation, attend_pieces, attend_weight.shape[1]
    )
    projected, reduce_shard = tied(projected, folded(reduce_weight, fold))
    reduce_pieces = lax.all_gather(reduce_shard, ("fsdp", "dp"), axis=0, tiled=False)
    bias_wide = jnp.pad(forget_bias[None, :], ((0, 0), (0, LANES - heads)))
    conv_low, normed_heads, ratios, states = attention_forward(
        resolution, projected, gate_logit, bias_wide, conv_taps, heads
    )
    attended, hidden, slope, normed_mid_t, conv_t, grad_reduced = middle_forward(
        where, conv_low, tokens, cotangent, modulation, expandbias_whole, middle_pieces, expand_weight.shape[1]
    )
    across = (2 * reduce_weight.shape[0]) % LANES == 0
    if across:
        reduce_other, reduce_parts = grads_across(where, hidden, grad_reduced)
    else:
        reduce_other, reduce_parts = weight_grads(where, hidden.T, grad_reduced)
    reduce_other = cross_sum(reduce_other)
    hidden, reduce_parts, reduce_other = tied(hidden, reduce_parts, reduce_other)
    moving = first_send(reduce_parts, reduce_other)
    back = middle_backward(
        where, hidden, slope, attended, tokens, cotangent, modulation, middle_pieces, reduce_pieces
    )
    back, moving = tied(back, moving)
    block_out, grad_preact, grad_after, grad_attended, grad_conv, middle_sums, bias_sums = back
    reduce_level = first_add(reduce_parts, reduce_other, moving)
    moving = second_send(reduce_level)
    joint = grads_joint(where, normed_mid_t, grad_preact, conv_t, grad_attended)
    joint, moving = tied(joint, moving)
    reduce_level = second_add(reduce_level, moving)
    joint = lax.psum_scatter(joint, ("fsdp", "dp"), scatter_dimension=0, tiled=True)
    grad_conv, reduce_level = tied(grad_conv, reduce_level)
    moving = far_send(reduce_level)
    back = attention_backward(
        resolution, projected, gate_logit, bias_wide, conv_taps, normed_heads, ratios, states, grad_conv, heads
    )
    back, moving = tied(back, moving)
    grad_projected, grad_gate, forgetbias_local, taps_local = back
    reduce_grad = far_add(reduce_level, moving)
    reduce_grad = reduce_grad.T if across else reduce_grad
    sums = jnp.concatenate(
        [
            taps_local,
            jnp.pad(forgetbias_local, ((0, 0), (0, features - LANES))),
            bias_sums.reshape(-1, features),
        ],
        axis=0,
    )
    bits = flip_bits(1, columns)
    for bit in bits[:-1]:
        sums = sums + flip_bit(sums, bit)
    attend_other, attend_parts = weight_grads(
        where, normed_in_t, grad_projected, grad_gate, heads // columns
    )
    attend_other, attend_parts, grad_projected, sums = tied(attend_other, attend_parts, grad_projected, sums)
    attend_other = cross_sum(attend_other)
    sums_moving = flip_bit(sums, bits[-1])
    grad_projected, attend_other, sums_moving = tied(grad_projected, attend_other, sums_moving)
    sums = sums + sums_moving
    attend_moving = first_send(attend_parts, attend_other)
    back = front_backward(
        where, grad_projected, grad_gate, grad_after, tokens, modulation, attend_pieces
    )
    back, attend_moving = tied(back, attend_moving)
    tokens_grad, front_sums = back
    attend_level = first_add(attend_parts, attend_other, attend_moving)

    middle_sums = jnp.sum(middle_sums.reshape(QUARTERS, -1, 8, features), axis=1)
    grad_modulation = jnp.concatenate([front_sums[:, :2], middle_sums[:, :4]], axis=1)
    first_slot = (jnp.arange(slots) == 0)[:, None, None]
    grad_modulation = jnp.where(
        single, jnp.where(first_slot, jnp.sum(grad_modulation, axis=0, keepdims=True), 0.0), grad_modulation
    )
    grad_modulation = grad_modulation.reshape(slots, columns, own_columns).astype(jnp.bfloat16)
    grad_modulation = jnp.swapaxes(grad_modulation, 0, 1)
    rows_here = [
        send(pick(grad_modulation, (dp_at + shift) % columns), along_dp(shift)) for shift in range(1, columns)
    ]
    rows_here, attend_level = tied(rows_here, attend_level)
    attend_moving = second_send(attend_level)
    rows_here = jnp.stack([pick(grad_modulation, dp_at)] + rows_here).reshape(columns * slots, own_columns)
    sums_moving = flip_bit(sums, columns)
    rows_here = jnp.stack([rows_here] + [send(rows_here, along_z(shift)) for shift in range(1, chips)])
    rows_other = send(rows_here, across_core)
    rows_other, attend_moving, sums_moving = tied(rows_other, attend_moving, sums_moving)
    attend_level = second_add(attend_level, attend_moving)
    attend_moving = far_send(attend_level)
    sums = sums + sums_moving
    bits = flip_bits(2 * columns, blocks * columns)
    sums_moving = flip_bit(sums, bits[0])
    rows_here = jnp.stack([rows_here, rows_other]).reshape(-1, own_columns)
    order = []
    for sibling in range(2):
        for far in range(chips):
            for shift in range(columns):
                block = 2 * ((z_at - far) % chips) + jnp.abs(core_at - sibling)
                order.append(block * columns + (dp_at - shift) % columns)
    order = (jnp.stack(order)[:, None] * slots + jnp.arange(slots)[None, :]).reshape(-1)
    chosen = (order[:, None] == jnp.arange(order.shape[0])[None, :]).astype(jnp.bfloat16)
    cond_here = jnp.dot(chosen, cond_columns, preferred_element_type=jnp.float32).astype(jnp.bfloat16)
    modulate_grad = lax.dot_general(
        cond_here, rows_here, (((0,), (0,)), ((), ())), preferred_element_type=jnp.float32
    )
    modbias_here = jnp.sum(rows_here.astype(jnp.float32), axis=0, keepdims=True)
    grad_cond = lax.dot_general(
        rows_here, modulate_weight, (((1,), (1,)), ((), ())), preferred_element_type=jnp.float32
    )
    grad_cond = jnp.moveaxis(grad_cond.reshape(blocks, columns, slots, own_rows), 1, 0)
    modulate_grad, grad_cond, modbias_here, attend_moving, sums_moving = tied(
        modulate_grad, grad_cond, modbias_here, attend_moving, sums_moving
    )
    modbias_all = jnp.stack(
        [modbias_here] + [send(modbias_here, along_dp(shift)) for shift in range(1, columns)]
    )
    modbias_all = jnp.concatenate([pick(modbias_all, (dp_at - column) % columns) for column in range(columns)], axis=1)
    own_bias = modulate_bias.shape[0]
    linear_at = fsdp_at * columns + dp_at
    modbias_grad = lax.dynamic_slice_in_dim(modbias_all, linear_at * own_bias, own_bias, axis=1).reshape(-1)
    cond_sum = [send(grad_cond[shift], along_dp(-shift)) for shift in range(1, columns)]
    attend_both = far_add(attend_level, attend_moving)
    attend_grad, forget_grad = attend_both[:, : attend_weight.shape[1]], attend_both[:, attend_weight.shape[1] :]
    sums = sums + sums_moving
    for bit in bits[1:]:
        sums = sums + flip_bit(sums, bit)
    cond_sum = sum(cond_sum, grad_cond[0]).reshape(2, chips, slots, own_rows)
    cond_sum = jnp.stack([cond_sum[0], send(cond_sum[1], across_core)], axis=1)
    joint = joint[0].astype(jnp.float32)
    expand_grad, output_grad = joint[:, : expand_weight.shape[1]], joint[:, expand_weight.shape[1] :]
    cond_parts = jnp.stack(
        [cond_sum[0]] + [send(cond_sum[far], along_z(-far)) for far in range(1, chips)]
    ).reshape(blocks, slots, own_rows)
    cond_columns_all = []
    for block in range(blocks):
        sibling = jnp.abs(block % 2 - core_at)
        cond_columns_all.append(pick(cond_parts, (block // 2 - z_at) % chips * 2 + sibling))
    grad_cond_low = jnp.concatenate(cond_columns_all, axis=1)
    conditions_grad = silu_back(grad_cond_low)[0].astype(jnp.bfloat16)

    taps_count = conv_taps.shape[0]
    taps_grad = sums[:taps_count]
    forgetbias_grad = sums[taps_count, :heads]
    own_bias = expand_bias.shape[0]
    expandbias_grad = lax.dynamic_slice_in_dim(
        sums[taps_count + 1 :].reshape(-1), linear_at * own_bias, own_bias, axis=0
    )
    return (
        block_out,
        tokens_grad,
        conditions_grad,
        modulate_grad,
        modbias_grad,
        attend_grad,
        forget_grad,
        forgetbias_grad,
        taps_grad,
        output_grad,
        expand_grad,
        expandbias_grad,
        reduce_grad,
    )


def solution(mesh):
    in_specs = (
        P(("fsdp", "dp"), None),
        P(("fsdp", "dp"), None),
        P(("fsdp", "dp")),
        P("fsdp", "dp"),
        P(("fsdp", "dp")),
        P("fsdp", "dp"),
        P("fsdp", "dp"),
        P(),
        P(),
        P("fsdp", "dp"),
        P("fsdp", "dp"),
        P(("fsdp", "dp")),
        P("fsdp", "dp"),
        P(("fsdp", "dp"), None),
    )
    out_specs = (
        P(("fsdp", "dp"), None),
        P(("fsdp", "dp"), None),
        P(("fsdp", "dp"), None),
        P("fsdp", "dp"),
        P(("fsdp", "dp")),
        P("fsdp", "dp"),
        P("fsdp", "dp"),
        P(),
        P(),
        P("fsdp", "dp"),
        P("fsdp", "dp"),
        P(("fsdp", "dp")),
        P("fsdp", "dp"),
    )
    return jax.shard_map(
        on_device, mesh=mesh, in_specs=in_specs, out_specs=out_specs, check_vma=False
    )
```
